32 devices in a mesh: dp: 8 (over y, x, core), tensor: 4 (over z).
Axes of the slice: x: 2, y: 2, z: 4, core: 2. Of those that a mesh axis runs over, the one named last changes fastest.
Arguments:
- layer_input: bfloat16 [16, 768, 768], P('dp', 'tensor'), may hold values from -6 to 6
- word_segments: int32 [16, 256], P('dp'), may hold values from 0 to 13, never falling along the last dimension, each value on 1 to 36 neighbouring positions
- image_order: int32 [16, 14], P('dp'), may hold values from 0 to 13, each once within a row
- cross_qkv: bfloat16 [3, 768, 768], P(None, None, 'tensor'), may hold values from -0.21875 to 0.21875
- cross_out: bfloat16 [768, 768], P('tensor'), may hold values from -0.875 to 0.875
- self_qkv: bfloat16 [2, 3, 768, 768], P(None, None, None, 'tensor'), may hold values from -0.21875 to 0.21875
- self_out: bfloat16 [2, 768, 768], P(None, 'tensor'), may hold values from -0.875 to 0.875
- ffn_up: bfloat16 [2, 768, 3072], P(None, None, 'tensor'), may hold values from -0.21875 to 0.21875
- ffn_down: bfloat16 [2, 3072, 768], P(None, 'tensor'), may hold values from -0.109375 to 0.109375
- norm_gains: float32 [5, 768], replicated, may hold values from 0.5 to 1.5
- norm_biases: float32 [5, 768], replicated, may hold values from -3 to 3
- out_grad: bfloat16 [16, 768, 768], P('dp', 'tensor'), may hold values from -6 to 6
Outputs:
- layer_output: bfloat16 [16, 768, 768], P('dp', 'tensor')
- input_grad: float32 [16, 768, 768], P('dp', 'tensor')
- cross_qkv_grad: float32 [3, 768, 768], P(None, None, 'tensor')
- cross_out_grad: float32 [768, 768], P('tensor')
- self_qkv_grad: float32 [2, 3, 768, 768], P(None, None, None, 'tensor')
- self_out_grad: float32 [2, 768, 768], P(None, 'tensor')
- ffn_up_grad: float32 [2, 768, 3072], P(None, None, 'tensor')
- ffn_down_grad: float32 [2, 3072, 768], P(None, 'tensor')
- norm_gains_grad: float32 [5, 768], replicated
- norm_biases_grad: float32 [5, 768], replicated
The draws below stay inside these ranges and needn't reach their ends.
Inputs may be any that keep to these rules, and one draw needn't show every extreme that they name: `word_segments`: in each row the ids never fall along the word slots, and each of the 14 captions has 1 to 36 slots. `image_order`: each row names every image once.
All inputs are finite; a program needn't handle non-finite values.
Results may differ from the reference program's by a relative error of at most 0.035.
Values may be sent and summed in bfloat16 or wider, within the bound.
A program may use at most 192 MiB of HBM per device.

```python
import math
import jax
import jax.numpy as jnp
import numpy as np
from jax import lax

HEADS = 12
HEAD_DIM = 64
D = 768
FF = 3072
WORDS = 256
CAPTIONS = 14
CAP_MOST = 36
BOXES = 36
REGIONS = 504
PADS = 8
SLOTS = 768
ROWS = 16


def shard_levels(stream_key, dims, cuts, low, largest):
    level = 1.0
    for dim, parts in cuts:
        heights = jax.random.uniform(jax.random.fold_in(jax.random.fold_in(stream_key, 6), dim), (parts,), jnp.float32, low / len(cuts), largest / len(cuts))
        level = level * jnp.repeat(jnp.exp(heights), dims[dim] // parts).reshape((-1,) + (1,) * (len(dims) - 1 - dim))
    return level


def split_up(amount, total, bound, lean):
    portions = [(1 << 20) // math.isqrt(rank ** lean) + 1 for rank in range(2, amount + 1)]
    rest, given = total - bound - (amount - 1), [1] * (amount - 1)
    while rest > 0:
        movable = [i for i in range(amount - 1) if given[i] < bound]
        whole, budget = sum([portions[i] for i in movable]), rest
        for i in movable:
            more = min(bound - given[i], max(1, budget * portions[i] // whole), rest)
            given[i] = given[i] + more
            rest = rest - more
    return np.array([bound] + given)


def uneven(rng, number_of, total, reach, slope):
    if number_of == 2:
        one = jax.random.randint(rng, (), max(1, total - reach), min(reach, total - 1) + 1)
        return jnp.stack([one, total - one])
    tallies = jnp.asarray(split_up(number_of, total, reach, slope), jnp.int32)
    twos = (number_of - 1) // 2
    donor, sink = tallies[1:1 + 2 * twos:2], tallies[2:2 + 2 * twos:2]
    margin = jnp.minimum(donor - 1, reach - sink)
    shifted = jax.random.randint(jax.random.fold_in(rng, 1), (twos,), 0, 1 << 20) % (margin + 1)
    tallies = tallies.at[1:1 + 2 * twos:2].set(donor - shifted).at[2:2 + 2 * twos:2].set(sink + shifted)
    return tallies[jax.random.permutation(jax.random.fold_in(rng, 2), number_of)]


def noise(key, extent, scale, limit, shards=(), dtype=jnp.bfloat16):
    entries = scale * jax.random.normal(key, extent, jnp.float32)
    if shards:
        entries = entries * shard_levels(key, extent, shards, -0.22, 0.18)
    return jnp.clip(entries, -limit, limit).astype(dtype)


def setup_inputs(seed: int = 0) -> dict:
    seeds = jax.random.split(jax.random.key(seed), 13)
    return {
        "layer_input": noise(seeds[0], (ROWS, SLOTS, D), 1.0, 6.0, ((0, 8), (1, 4))),
        "word_segments": jax.vmap(lambda own: jnp.searchsorted(jnp.cumsum(uneven(own, CAPTIONS, WORDS, CAP_MOST, 2)), jnp.arange(WORDS), side="right"))(jax.random.split(seeds[1], ROWS)).reshape((ROWS, WORDS)).astype(jnp.int32),
        "image_order": jax.vmap(lambda own: jax.random.permutation(own, CAPTIONS))(jax.random.split(seeds[2], ROWS)).reshape((ROWS, CAPTIONS)).astype(jnp.int32),
        "cross_qkv": noise(seeds[3], (3, D, D), D ** -0.5, 0.21875, ((2, 4),)),
        "cross_out": noise(seeds[4], (D, D), (D // 16) ** -0.5, 0.875, ((0, 4),)),
        "self_qkv": noise(seeds[5], (2, 3, D, D), D ** -0.5, 0.21875, ((3, 4),)),
        "self_out": noise(seeds[6], (2, D, D), (D // 16) ** -0.5, 0.875, ((1, 4),)),
        "ffn_up": noise(seeds[7], (2, D, FF), D ** -0.5, 0.21875, ((2, 4),)),
        "ffn_down": noise(seeds[8], (2, FF, D), FF ** -0.5, 0.109375, ((1, 4),)),
        "norm_gains": jnp.clip(1.0 + 0.1 * jax.random.normal(seeds[9], (5, D), jnp.float32), 0.5, 1.5),
        "norm_biases": noise(seeds[10], (5, D), 0.5, 3.0, (), jnp.float32),
        "out_grad": noise(seeds[11], (ROWS, SLOTS, D), 1.0, 6.0, ((0, 8), (1, 4))),
    }


NORM_EPSILON = 1e-12

@jax.custom_vjp
def low(v):
    return lax.optimization_barrier(v.astype(jnp.bfloat16)).astype(jnp.float32)

@jax.custom_vjp
def low_back(v):
    return v

def low_keep(v):
    return (low(v), None)

def low_pass(kept, grad):
    return (grad,)

def back_keep(v):
    return (v, None)

def back_low(kept, grad):
    return (low(grad),)
low.defvjp(low_keep, low_pass)
low_back.defvjp(back_keep, back_low)

def product(left_side, right_side):
    return jnp.dot(left_side, right_side, precision=lax.Precision.HIGHEST, preferred_element_type=jnp.float32)

def project(hidden, w_words, w_regions):
    return jnp.concatenate([product(hidden[:WORDS], w_words), product(hidden[WORDS:], w_regions)], axis=0)

def layer_norm(summed, gain_rows, shift_rows):
    center = summed - lax.optimization_barrier(jnp.mean(summed, axis=-1, keepdims=True))
    scaled = center * lax.rsqrt(lax.optimization_barrier(jnp.mean(center * center, axis=-1, keepdims=True)) + NORM_EPSILON)
    return scaled * gain_rows + shift_rows

def attend(hidden, qkv_words, qkv_regions, out_words, out_regions, allowed):
    scaling = HEAD_DIM ** (-0.5)
    query_heads = low_back(low(project(hidden, qkv_words[0], qkv_regions[0]))).reshape(SLOTS, HEADS, HEAD_DIM)
    key_heads = low_back(low(project(hidden, qkv_words[1], qkv_regions[1]))).reshape(SLOTS, HEADS, HEAD_DIM)
    value_heads = low_back(low(project(hidden, qkv_words[2], qkv_regions[2]))).reshape(SLOTS, HEADS, HEAD_DIM)
    raw_scores = jnp.einsum('qhd,khd->hqk', query_heads, key_heads, precision=lax.Precision.HIGHEST) * scaling
    scores = low_back(raw_scores)
    masked = jnp.where(allowed[None], scores, -1e+30)
    attention_probs = jax.nn.softmax(masked, axis=-1)
    context = jnp.einsum('hqk,khd->qhd', low(attention_probs), value_heads, precision=lax.Precision.HIGHEST).reshape(SLOTS, D)
    context = low_back(low(context))
    return low_back(project(context, out_words, out_regions))

def row_forward(inputs, word_ids, ordering, weight_set):
    cross_qkv, cross_out, self_qkv, self_out, ffn_up, ffn_down, gains, shifts = weight_set
    groups = jnp.concatenate([word_ids.astype(jnp.int32), jnp.repeat(ordering.astype(jnp.int32), BOXES), jnp.full((PADS,), CAPTIONS, jnp.int32)])
    slot_kind = jnp.concatenate([jnp.zeros((WORDS,), jnp.int32), jnp.ones((REGIONS,), jnp.int32), jnp.full((PADS,), 2, jnp.int32)])
    same_group = groups[:, None] == groups[None, :]
    cross_ok = same_group & ((slot_kind[:, None] != slot_kind[None, :]) | (slot_kind[:, None] == 2))
    self_ok = same_group & (slot_kind[:, None] == slot_kind[None, :])
    is_word = (jnp.arange(SLOTS) < WORDS)[:, None]
    cross_branch = attend(inputs, cross_qkv, cross_qkv, cross_out, cross_out, cross_ok)
    section_one = layer_norm(inputs + cross_branch, gains[0], shifts[0])
    self_branch = attend(low(section_one), self_qkv[0], self_qkv[1], self_out[0], self_out[1], self_ok)
    section_two = layer_norm(section_one + self_branch, jnp.where(is_word, gains[1], gains[2]), jnp.where(is_word, shifts[1], shifts[2]))
    upward = low_back(project(low(section_two), ffn_up[0], ffn_up[1]))
    active = low(jax.nn.gelu(upward, approximate=False))
    ffn_branch = low_back(project(active, ffn_down[0], ffn_down[1]))
    return layer_norm(section_two + ffn_branch, jnp.where(is_word, gains[3], gains[4]), jnp.where(is_word, shifts[3], shifts[4]))

def reference(layer_input, word_segments, image_order, cross_qkv, cross_out, self_qkv, self_out, ffn_up, ffn_down, norm_gains, norm_biases, out_grad):
    as_float = [item.astype(jnp.float32) for item in (layer_input, cross_qkv, cross_out, self_qkv, self_out, ffn_up, ffn_down, norm_gains, norm_biases)]

    def forward(inputs, *weight_set):

        def row_step(carried, row_data):
            return (carried, row_forward(row_data[0], row_data[1], row_data[2], weight_set))
        carried, outputs = lax.scan(jax.checkpoint(row_step), None, (inputs, word_segments, image_order))
        return outputs
    result, pull_back = jax.vjp(forward, *as_float)
    gradients = pull_back(out_grad.astype(jnp.float32))
    return (result.astype(jnp.bfloat16), gradients[0], gradients[1], gradients[2], gradients[3], gradients[4], gradients[5], gradients[6], gradients[7], gradients[8])
```

```python
import jax
import jax.numpy as jnp
from jax import lax
from jax.sharding import PartitionSpec as P

HEAD_DIM = 64
WORDS = 256
CAPTIONS = 14
BOXES = 36
REGIONS = 504
PADS = 8


NORM_EPSILON = 1e-12


def contract_in(hidden, w_words, w_regions):
    if w_regions is None:
        return jnp.einsum("rsd,dc->rsc", hidden, w_words, preferred_element_type=jnp.float32)
    return jnp.concatenate(
        [
            jnp.einsum(
                "rsd,dc->rsc", hidden[:, :WORDS], w_words, preferred_element_type=jnp.float32
            ),
            jnp.einsum(
                "rsd,dc->rsc", hidden[:, WORDS:], w_regions, preferred_element_type=jnp.float32
            ),
        ],
        axis=1,
    )


def contract_back(grad_b, w_words, w_regions):
    if w_regions is None:
        return jnp.einsum("rsc,dc->rsd", grad_b, w_words, preferred_element_type=jnp.float32)
    return jnp.concatenate(
        [
            jnp.einsum(
                "rsc,dc->rsd", grad_b[:, :WORDS], w_words, preferred_element_type=jnp.float32
            ),
            jnp.einsum(
                "rsc,dc->rsd", grad_b[:, WORDS:], w_regions, preferred_element_type=jnp.float32
            ),
        ],
        axis=1,
    )


def weight_grad(hidden, grad_b, by_modality):
    if not by_modality:
        return jnp.einsum("rsd,rsc->dc", hidden, grad_b, preferred_element_type=jnp.float32)
    return jnp.stack(
        [
            jnp.einsum(
                "rsd,rsc->dc",
                hidden[:, :WORDS],
                grad_b[:, :WORDS],
                preferred_element_type=jnp.float32,
            ),
            jnp.einsum(
                "rsd,rsc->dc",
                hidden[:, WORDS:],
                grad_b[:, WORDS:],
                preferred_element_type=jnp.float32,
            ),
        ],
        axis=0,
    )


def head_split(tensor_b):
    return tensor_b.reshape(
        tensor_b.shape[0], tensor_b.shape[1], tensor_b.shape[2] // HEAD_DIM, HEAD_DIM
    )


def masked_scores(query_heads, key_heads, allowed):
    raw_scores = jnp.einsum(
        "rqhd,rkhd->rhqk", query_heads, key_heads, preferred_element_type=jnp.float32
    ) * HEAD_DIM ** (-0.5)
    return jnp.where(allowed[:, None], raw_scores, -1e30)


def region_matrix(table, member):
    if table is None:
        return None
    return table[member]


def attend(hidden, qkv_words, qkv_regions, out_words, out_regions, allowed):
    projected = [
        contract_in(hidden, qkv_words[member], region_matrix(qkv_regions, member)).astype(
            jnp.bfloat16
        )
        for member in range(3)
    ]
    query_b, key_b, value_b = projected
    scores = masked_scores(head_split(query_b), head_split(key_b), allowed)
    top_score = jnp.max(scores, axis=-1, keepdims=True)
    exponent = jnp.exp(scores - top_score)
    denominator = jnp.sum(exponent, axis=-1, keepdims=True)
    attention_probs = exponent / denominator
    log_total = top_score + jnp.log(denominator)
    context_b = (
        jnp.einsum(
            "rhqk,rkhd->rqhd",
            attention_probs.astype(jnp.bfloat16),
            head_split(value_b),
            preferred_element_type=jnp.float32,
        )
        .reshape(query_b.shape)
        .astype(jnp.bfloat16)
    )
    partial_out = contract_in(context_b, out_words, out_regions)
    return (partial_out, (query_b, key_b, value_b, log_total, context_b))


def attend_back(
    hidden, grad_b, kept_values, qkv_words, qkv_regions, out_words, out_regions, allowed
):
    query_b, key_b, value_b, log_total, context_b = kept_values
    by_modality = qkv_regions is not None
    out_weight_grad = weight_grad(context_b, grad_b, by_modality)
    context_grad = head_split(contract_back(grad_b, out_words, out_regions).astype(jnp.bfloat16))
    query_heads = head_split(query_b)
    key_heads = head_split(key_b)
    attention_probs = jnp.exp(masked_scores(query_heads, key_heads, allowed) - log_total)
    probs_grad = jnp.einsum(
        "rqhd,rkhd->rhqk", context_grad, head_split(value_b), preferred_element_type=jnp.float32
    )
    score_grad = (
        attention_probs
        * (probs_grad - jnp.sum(attention_probs * probs_grad, axis=-1, keepdims=True))
    ).astype(jnp.bfloat16)
    scaling = HEAD_DIM ** (-0.5)
    query_grad = (
        (
            jnp.einsum("rhqk,rkhd->rqhd", score_grad, key_heads, preferred_element_type=jnp.float32)
            * scaling
        )
        .reshape(query_b.shape)
        .astype(jnp.bfloat16)
    )
    key_grad = (
        (
            jnp.einsum(
                "rhqk,rqhd->rkhd", score_grad, query_heads, preferred_element_type=jnp.float32
            )
            * scaling
        )
        .reshape(key_b.shape)
        .astype(jnp.bfloat16)
    )
    value_grad = (
        jnp.einsum(
            "rhqk,rqhd->rkhd",
            attention_probs.astype(jnp.bfloat16),
            context_grad,
            preferred_element_type=jnp.float32,
        )
        .reshape(value_b.shape)
        .astype(jnp.bfloat16)
    )
    member_grads = [query_grad, key_grad, value_grad]
    qkv_grad = jnp.stack(
        [weight_grad(hidden, member_grads[member], by_modality) for member in range(3)],
        axis=1 if by_modality else 0,
    )
    hidden_grad = contract_back(query_grad, qkv_words[0], region_matrix(qkv_regions, 0))
    hidden_grad = hidden_grad + contract_back(key_grad, qkv_words[1], region_matrix(qkv_regions, 1))
    hidden_grad = hidden_grad + contract_back(
        value_grad, qkv_words[2], region_matrix(qkv_regions, 2)
    )
    return (hidden_grad, qkv_grad, out_weight_grad)


def norm_forward(summed, gain_rows, shift_rows):
    center = summed - jnp.mean(summed, axis=-1, keepdims=True)
    inverse = lax.rsqrt(jnp.mean(center * center, axis=-1, keepdims=True) + NORM_EPSILON)
    normed = center * inverse
    return (normed * gain_rows + shift_rows, normed, inverse)


def norm_backward(upstream, normed, inverse, gain_rows):
    scaled = upstream * gain_rows
    return inverse * (
        scaled
        - jnp.mean(scaled, axis=-1, keepdims=True)
        - normed * jnp.mean(scaled * normed, axis=-1, keepdims=True)
    )


def exact_gelu(values):
    return jax.nn.gelu(values, approximate=False)


def spread(piece_b):
    return lax.all_gather(piece_b, "tensor", axis=1, tiled=True)


def collect(partial_grad):
    return lax.psum_scatter(
        partial_grad.astype(jnp.bfloat16), "tensor", scatter_dimension=1, tiled=True
    ).astype(jnp.float32)


def widen(piece_b):
    return spread(piece_b)


def finish(partial_out):
    return lax.psum_scatter(
        partial_out.astype(jnp.bfloat16), "tensor", scatter_dimension=1, tiled=True
    ).astype(jnp.float32)


def back_sum(partial_grad):
    return collect(partial_grad)


def body(
    layer_input,
    word_segments,
    image_order,
    cross_qkv,
    cross_out,
    self_qkv,
    self_out,
    ffn_up,
    ffn_down,
    norm_gains,
    norm_biases,
    out_grad,
):
    row_count = layer_input.shape[0]
    share_len = layer_input.shape[1]
    slot_count = share_len * lax.axis_size("tensor")
    tensor_place = lax.axis_index("tensor")
    groups = jnp.concatenate(
        [
            word_segments,
            jnp.repeat(image_order, BOXES, axis=1),
            jnp.full((row_count, PADS), CAPTIONS, jnp.int32),
        ],
        axis=1,
    )
    slot_ids = jnp.arange(slot_count)
    slot_kind = jnp.where(slot_ids < WORDS, 0, jnp.where(slot_ids < WORDS + REGIONS, 1, 2))
    same_group = groups[:, :, None] == groups[:, None, :]
    differ = slot_kind[:, None] != slot_kind[None, :]
    cross_ok = same_group & (differ | (slot_kind[:, None] == 2))[None]
    self_ok = same_group & jnp.logical_not(differ)[None]
    stream_ids = tensor_place * share_len + jnp.arange(share_len)
    stream_word = (stream_ids < WORDS)[:, None]
    own_rows = (stream_ids // share_len == tensor_place).astype(jnp.float32)[:, None]
    word_weight = stream_word.astype(jnp.float32) * own_rows
    other_weight = own_rows - word_weight

    def pick(table, first_norm, second_norm):
        return jnp.where(stream_word, table[first_norm], table[second_norm])

    def norm_terms(upstream, normed, first_norm, second_norm, gain_grad, bias_grad):
        gain_terms = upstream * normed
        gain_grad = gain_grad.at[first_norm].add(jnp.sum(gain_terms * word_weight, axis=(0, 1)))
        gain_grad = gain_grad.at[second_norm].add(jnp.sum(gain_terms * other_weight, axis=(0, 1)))
        bias_grad = bias_grad.at[first_norm].add(jnp.sum(upstream * word_weight, axis=(0, 1)))
        bias_grad = bias_grad.at[second_norm].add(jnp.sum(upstream * other_weight, axis=(0, 1)))
        return (gain_grad, bias_grad)

    input_full = spread(layer_input)
    stream = layer_input.astype(jnp.float32)
    cross_part, cross_kept = attend(input_full, cross_qkv, None, cross_out, None, cross_ok)
    section_one, normed_one, inverse_one = norm_forward(
        stream + finish(cross_part), norm_gains[0], norm_biases[0]
    )
    one_full = widen(section_one.astype(jnp.bfloat16))
    self_part, self_kept = attend(
        one_full, self_qkv[0], self_qkv[1], self_out[0], self_out[1], self_ok
    )
    gains_two = pick(norm_gains, 1, 2)
    section_two, normed_two, inverse_two = norm_forward(
        section_one + finish(self_part), gains_two, pick(norm_biases, 1, 2)
    )
    two_full = widen(section_two.astype(jnp.bfloat16))
    upward = contract_in(two_full, ffn_up[0], ffn_up[1])
    active, gelu_pull = jax.vjp(exact_gelu, upward)
    active_b = active.astype(jnp.bfloat16)
    ffn_part = contract_in(active_b, ffn_down[0], ffn_down[1])
    gains_three = pick(norm_gains, 3, 4)
    result, normed_three, inverse_three = norm_forward(
        section_two + finish(ffn_part), gains_three, pick(norm_biases, 3, 4)
    )
    layer_output = result.astype(jnp.bfloat16)
    upstream = out_grad.astype(jnp.float32)
    gain_grad, bias_grad = norm_terms(
        upstream, normed_three, 3, 4, jnp.zeros_like(norm_gains), jnp.zeros_like(norm_biases)
    )
    grad_three = norm_backward(upstream, normed_three, inverse_three, gains_three)
    three_full = widen(grad_three.astype(jnp.bfloat16))
    down_grad = weight_grad(active_b, three_full, True)
    active_grad = contract_back(three_full, ffn_down[0], ffn_down[1])
    upward_grad = gelu_pull(active_grad)[0].astype(jnp.bfloat16)
    up_grad = weight_grad(two_full, upward_grad, True)
    section_two_grad = grad_three + back_sum(contract_back(upward_grad, ffn_up[0], ffn_up[1]))
    gain_grad, bias_grad = norm_terms(section_two_grad, normed_two, 1, 2, gain_grad, bias_grad)
    grad_two = norm_backward(section_two_grad, normed_two, inverse_two, gains_two)
    two_back = widen(grad_two.astype(jnp.bfloat16))
    hidden_two, self_qkv_grad, self_out_grad = attend_back(
        one_full, two_back, self_kept, self_qkv[0], self_qkv[1], self_out[0], self_out[1], self_ok
    )
    section_one_grad = grad_two + back_sum(hidden_two)
    gain_grad, bias_grad = norm_terms(section_one_grad, normed_one, 0, 0, gain_grad, bias_grad)
    grad_one = norm_backward(section_one_grad, normed_one, inverse_one, norm_gains[0])
    one_back = widen(grad_one.astype(jnp.bfloat16))
    hidden_one, cross_qkv_grad, cross_out_grad = attend_back(
        input_full, one_back, cross_kept, cross_qkv, None, cross_out, None, cross_ok
    )
    input_grad = grad_one + collect(hidden_one)
    summed_grads = [
        total.astype(jnp.float32)
        for total in lax.psum(
            [
                grad.astype(jnp.bfloat16)
                for grad in (
                    cross_qkv_grad,
                    cross_out_grad,
                    self_qkv_grad,
                    self_out_grad,
                    up_grad,
                    down_grad,
                )
            ],
            "dp",
        )
    ]
    norm_grads = lax.psum((gain_grad, bias_grad), ("dp", "tensor"))
    return (
        layer_output,
        input_grad,
        summed_grads[0],
        summed_grads[1],
        summed_grads[2],
        summed_grads[3],
        summed_grads[4],
        summed_grads[5],
        norm_grads[0],
        norm_grads[1],
    )


def solution(mesh):
    in_specs = (
        P("dp", "tensor", None),
        P("dp", None),
        P("dp", None),
        P(None, None, "tensor"),
        P("tensor", None),
        P(None, None, None, "tensor"),
        P(None, "tensor", None),
        P(None, None, "tensor"),
        P(None, "tensor", None),
        P(),
        P(),
        P("dp", "tensor", None),
    )
    out_specs = (
        P("dp", "tensor", None),
        P("dp", "tensor", None),
        P(None, None, "tensor"),
        P("tensor", None),
        P(None, None, None, "tensor"),
        P(None, "tensor", None),
        P(None, None, "tensor"),
        P(None, "tensor", None),
        P(),
        P(),
    )
    return jax.shard_map(body, mesh=mesh, in_specs=in_specs, out_specs=out_specs, check_vma=False)
```

```python
import functools

import jax
import jax.numpy as jnp
from jax import lax
from jax.experimental import pallas as pl
from jax.experimental.pallas import tpu as pltpu
from jax.sharding import PartitionSpec as P

HEAD_DIM = 64
WORDS = 256
CAPTIONS = 14
BOXES = 36
REGIONS = 504
PADS = 8
NORM_EPSILON = 1e-12
BLOCK = 256
BF16 = jnp.bfloat16
F32 = jnp.float32
MESH = pl.DeviceIdType.MESH
CROSS, SELF, UP, DOWN = 0, 1, 2, 3


def dot_nn(left, right):
    return jnp.dot(left, right, preferred_element_type=F32)


def dot_nt(left, right):
    return lax.dot_general(left, right, (((1,), (1,)), ((), ())), preferred_element_type=F32)


def aligned(value, step):
    return pl.multiple_of(value, step)


def layer_kernel(
    x_in,
    og_in,
    codes_in,
    cross_in,
    self_in,
    up_in,
    down_in,
    gains,
    biases,
    y_out,
    dx_out,
    cross_out,
    self_out,
    up_out,
    down_out,
    norm_out,
    wa,
    wf,
    xrow,
    ogrow,
    codes,
    kcode,
    qkv1,
    qkv2,
    ctx_t,
    lse,
    xh,
    rstd,
    sb,
    res,
    acc,
    act,
    gp,
    dzb,
    tt,
    yb,
    dhk_recv,
    kv_acc,
    nrm,
    nrm_recv,
    r1f,
    r2f,
    r3f,
    r2s,
    r3s,
    r2c,
    r3c,
    send_sems,
    recv_sems,
    local_sems,
    credit,
):
    d = lax.axis_index("dp")
    t = lax.axis_index("tensor")
    c = d % 2
    px = (d // 2) % 2
    py = (d // 4) % 2
    q = px + 2 * py
    d_core = d + 1 - 2 * c
    d_x = d + 2 - 4 * px
    d_y = d + 4 - 8 * py
    holder = t // 2
    d_holder = d - c + holder
    turn = t % 2
    nb = 1 + c
    near = {"x": d_x, "y": d_y, "core": d_core}

    def at(dp_index, tensor_index):
        return {"dp": dp_index, "tensor": tensor_index}

    counter = [0]
    local_counter = [0]
    pending = []

    def new_id(count=1):
        counter[0] += count
        return counter[0] - count

    def remote(src, dst, device, ident, arrival=None):
        return pltpu.make_async_remote_copy(
            src_ref=src,
            dst_ref=dst,
            send_sem=send_sems.at[ident],
            recv_sem=recv_sems.at[ident if arrival is None else arrival],
            device_id=device,
            device_id_type=MESH,
        )

    def send(src, dst, device, ident):
        copy = remote(src, dst, device, ident)
        copy.start()
        pending.append(copy.wait_send)

    def arrive(dst, ident):
        remote(dst, dst, at(d_core, t), ident).wait_recv()

    def local(src, dst):
        copy = pltpu.make_async_copy(src, dst, local_sems.at[local_counter[0]])
        local_counter[0] += 1
        return copy

    def blocks(body):
        def step(i, carry):
            body(i, aligned(i * BLOCK, BLOCK))
            return carry

        lax.fori_loop(0, nb, step, 0)

    def times(count, body):
        def step(i, carry):
            body(i)
            return carry

        lax.fori_loop(0, count, step, 0)

    barrier = pltpu.get_barrier_semaphore()
    partners = [at(d_core, t), at(d_x, t), at(d_y, t)]
    for m in range(1, 4):
        partners.append(at(d, (t + m) % 4))
        partners.append(at(d_core, (t + m) % 4))
    for partner in partners:
        pl.semaphore_signal(barrier, inc=1, device_id=partner, device_id_type=MESH)

    half_rows = aligned(t * 192, 16)
    own_copies = [
        local(cross_in, wa.at[CROSS, :, pl.ds(half_rows, 192), :]),
        local(self_in.at[c], wa.at[SELF, :, pl.ds(half_rows, 192), :]),
        local(up_in.at[c], wf.at[0, t]),
        local(down_in.at[c], wf.at[1, t]),
    ]
    for copy in own_copies:
        copy.start()

    zero_half = jnp.zeros((BLOCK, 768), BF16)

    @pl.when(c == 0)
    def _():
        for ref in (qkv2.at[1], qkv2.at[2], sb.at[0], sb.at[1], dzb):
            ref[BLOCK:, :] = zero_half
        for k in range(4):
            act[k, BLOCK:, :] = zero_half
            gp[k, BLOCK:, :] = zero_half
        for k in range(2):
            ctx_t[k, :, BLOCK:] = jnp.zeros((768, BLOCK), BF16)
        tt[0, :, BLOCK:] = jnp.zeros((768, BLOCK), BF16)

    nrm[...] = jnp.zeros_like(nrm)
    pl.semaphore_wait(barrier, len(partners))

    def spread_row(source, row):
        base = new_id(4)
        core_base = new_id(4)
        own = local(source.at[turn], row.at[pl.ds(half_rows, 192), :])

        def each_target(action):
            for r in range(2):
                target = 2 * c + r

                @pl.when(target != t)
                def _():
                    action(
                        remote(
                            source.at[r],
                            row.at[pl.ds(half_rows, 192), :],
                            at(d, target),
                            base + r,
                            base + t,
                        )
                    )

        def each_relay(action):
            @pl.when(holder == c)
            def _():
                for s in range(4):
                    part = row.at[pl.ds(192 * s, 192), :]
                    action(s, part, remote(part, part, at(d_core, t), core_base + s))

        def begin():
            each_target(lambda copy: copy.start())

            @pl.when(holder == c)
            def _():
                own.start()

        def relay():
            def action(s, part, copy):
                @pl.when(t == s)
                def _():
                    own.wait()

                @pl.when(t != s)
                def _():
                    arrive(part, base + s)

                copy.start()

            each_relay(action)

        def finish():
            @pl.when(holder != c)
            def _():
                for s in range(4):
                    arrive(row.at[pl.ds(192 * s, 192), :], core_base + s)

        def close():
            each_target(lambda copy: copy.wait_send())
            each_relay(lambda s, part, copy: copy.wait_send())

        return begin, relay, finish, close

    x_begin, x_relay, x_finish, x_close = spread_row(x_in, xrow)
    og_begin, og_relay, og_finish, og_close = spread_row(og_in, ogrow)
    pending.append(x_close)
    x_begin()

    code_ident = new_id()
    code_own = local(codes_in.at[turn], codes)

    @pl.when(holder == c)
    def _():
        code_own.start()
        remote(codes_in.at[turn], codes, at(d_core, t), code_ident).start()

    def share(g, shard, quarter, low, high):
        if g >= UP:
            rows = aligned(quarter * 192 + low * 96, 16)
            return wf.at[g - UP, shard, pl.ds(rows, (high - low) * 96), :]
        rows = aligned(shard * 192 + quarter * 48, 16)
        if g == SELF:
            return wa.at[SELF, pl.ds(2 * low, 2 * (high - low)), pl.ds(rows, 48), :]
        return wa.at[CROSS, pl.ds(2 * c + low, high - low), pl.ds(rows, 48), :]

    def own_share(g):
        if g >= UP:
            source = up_in if g == UP else down_in
            return source.at[c, pl.ds(aligned(q * 192, 16), 192), :]
        rows = pl.ds(aligned(q * 48, 16), 48)
        if g == SELF:
            return self_in.at[c, :, rows, :]
        return cross_in.at[pl.ds(2 * c, 2), rows, :]

    qx, qy = (1 - px) + 2 * py, px + 2 * (1 - py)
    qd = (1 - px) + 2 * (1 - py)
    items = [(g, m) for g in (CROSS, SELF, UP, DOWN) for m in range(1, 4)]
    z_ids = {item: new_id() for item in items}
    x_ids = {item: new_id() for item in items}
    y_ids = {item: new_id() for item in items}
    fx_ids = {item: new_id() for item in items}
    fy_ids = {item: new_id() for item in items}
    core_ids = {m: new_id() for m in range(1, 4)}

    def z_start(item):
        g, m = item
        send(own_share(g), share(g, t, q, 0, 2), at(d, (t + m) % 4), z_ids[item])

    def first(item):
        g, m = item
        shard = (t + 4 - m) % 4
        piece = share(g, shard, q, 0, 2)
        arrive(piece, z_ids[item])
        send(piece, piece, at(d_x, t), x_ids[item])
        send(piece, piece, at(d_y, t), y_ids[item])

    def second(item):
        g, m = item
        shard = (t + 4 - m) % 4
        arrive(share(g, shard, qx, 0, 2), x_ids[item])
        low = share(g, shard, qx, 0, 1)
        send(low, low, at(d_y, t), fy_ids[item])
        arrive(share(g, shard, qy, 0, 2), y_ids[item])
        high = share(g, shard, qy, 1, 2)
        send(high, high, at(d_x, t), fx_ids[item])

    def third(item):
        g, m = item
        shard = (t + 4 - m) % 4
        arrive(share(g, shard, qd, 0, 1), fy_ids[item])
        arrive(share(g, shard, qd, 1, 2), fx_ids[item])
        if g == CROSS:
            rows = pl.ds(aligned(shard * 192, 16), 192)
            whole = wa.at[CROSS, pl.ds(2 * c, 2), rows, :]
            send(whole, whole, at(d_core, t), core_ids[m])

    def last(m):
        shard = (t + 4 - m) % 4
        rows = pl.ds(aligned(shard * 192, 16), 192)
        arrive(wa.at[CROSS, pl.ds(2 * (1 - c), 2), rows, :], core_ids[m])

    for item in items:
        z_start(item)
    og_begin()

    steps = []
    position = {}
    for k in range(len(items) + 2):
        if k < len(items):
            steps.append(functools.partial(first, items[k]))
        if 0 <= k - 1 < len(items):
            steps.append(functools.partial(second, items[k - 1]))
        if 0 <= k - 2 < len(items):
            steps.append(functools.partial(third, items[k - 2]))
            position[items[k - 2]] = len(steps)
    done = [0]

    def advance(upto):
        while done[0] < min(upto, len(steps)):
            steps[done[0]]()
            done[0] += 1

    x_relay()
    x_finish()

    @pl.when(holder == c)
    def _():
        code_own.wait()
        remote(codes_in.at[turn], codes, at(d_core, t), code_ident).wait_send()

    @pl.when(holder != c)
    def _():
        arrive(codes, code_ident)

    def as_column(row):
        return jnp.transpose(jnp.broadcast_to(row, (128, BLOCK)))

    own_base = aligned(c * BLOCK, BLOCK)
    other_base = aligned((1 - c) * BLOCK, BLOCK)
    kcode[0, :BLOCK, :] = as_column(codes[0:1, pl.ds(other_base, BLOCK)])
    kcode[0, BLOCK:, :] = as_column(codes[pl.ds(c, 1), 512:768])
    kcode[1, :BLOCK, :] = as_column(codes[2:3, pl.ds(own_base, BLOCK)])
    kcode[1, BLOCK:, :] = as_column(codes[pl.ds(3 - c, 1), 512:768])

    lane = lax.broadcasted_iota(jnp.int32, (1, 128), 1)
    head_lanes = [
        (lane < HEAD_DIM).astype(F32).astype(BF16),
        (lane >= HEAD_DIM).astype(F32).astype(BF16),
    ]
    scaling = HEAD_DIM ** (-0.5)

    def project(source, base, weight, target, rows):
        left = source[pl.ds(base, BLOCK), :]
        for n in range(3):
            target[pl.ds(rows, BLOCK), 256 * n : 256 * n + 256] = dot_nt(
                left, weight[256 * n : 256 * n + 256, :]
            ).astype(BF16)

    def attend(which, qkv, code_row, pairs):
        def pair(k):
            lanes = pl.ds(aligned(k * 128, 128), 128)
            key = qkv[1, :, lanes]
            value_t = jnp.transpose(qkv[2, :, lanes])

            def block(i, rows):
                query = qkv[0, pl.ds(rows, BLOCK), lanes] * jnp.asarray(scaling, BF16)
                query_code = codes[
                    pl.ds(code_row, 1), pl.ds(aligned(own_base + rows, BLOCK), BLOCK)
                ]
                allowed = kcode[which, :, 0:1] == query_code
                for h in range(2):
                    scores = dot_nt(key, query * head_lanes[h])
                    scores = jnp.where(allowed, scores, -1e30)
                    top = jnp.max(scores, axis=0, keepdims=True)
                    exponent = jnp.exp(scores - top)
                    total = jnp.sum(exponent, axis=0, keepdims=True)
                    probs = (exponent * (1.0 / total)).astype(BF16)
                    lse[which, pl.ds(2 * k + h, 1), pl.ds(rows, BLOCK)] = top + jnp.log(total)
                    ctx_t[
                        which,
                        pl.ds(aligned(k * 128 + h * 64, 64), 64),
                        pl.ds(rows, BLOCK),
                    ] = dot_nn(value_t[64 * h : 64 * h + 64, :], probs).astype(BF16)

            blocks(block)

        def run(k, carry):
            pair(k)
            return carry

        lax.fori_loop(pairs[0], pairs[1], run, 0)

    def normalize(summed, index, slot, rows):
        center = summed - jnp.mean(summed, axis=-1, keepdims=True)
        inverse = lax.rsqrt(jnp.mean(center * center, axis=-1, keepdims=True) + NORM_EPSILON)
        normed = center * inverse
        xh[slot, pl.ds(rows, BLOCK), :] = normed.astype(BF16)
        rstd[slot, pl.ds(rows, BLOCK), :] = inverse
        return normed * gains[pl.ds(index, 1), :] + biases[pl.ds(index, 1), :]

    def attention_out(which, rows):
        context = jnp.transpose(ctx_t[which, :, pl.ds(rows, BLOCK)])
        return dot_nn(context, wa[which, 3])

    for copy in own_copies[:1]:
        copy.wait()
    advance(position[(CROSS, 3)])
    for m in range(1, 4):
        last(m)
    blocks(lambda i, rows: project(xrow, own_base + rows, wa.at[CROSS, 0], qkv1.at[0], rows))
    for k in range(1, 3):
        project(xrow, other_base, wa.at[CROSS, k], qkv1.at[k], 0)
        project(xrow, 512, wa.at[CROSS, k], qkv1.at[k], BLOCK)
    attend(0, qkv1, 0, (0, 3))
    advance(position[(SELF, 1)])
    attend(0, qkv1, 0, (3, 6))
    advance(position[(SELF, 2)])

    def cross_end(i, rows):
        stream = xrow[pl.ds(aligned(own_base + rows, BLOCK), BLOCK), :].astype(F32)
        section = normalize(stream + attention_out(0, rows), 0, 0, rows)
        res[pl.ds(rows, BLOCK), :] = section
        sb[0, pl.ds(rows, BLOCK), :] = section.astype(BF16)

    blocks(cross_end)

    own_copies[1].wait()
    advance(position[(SELF, 3)])
    for k in range(3):
        blocks(lambda i, rows: project(sb.at[0], rows, wa.at[SELF, k], qkv2.at[k], rows))
    attend(1, qkv2, 2, (0, 3))
    advance(position[(UP, 1)])
    attend(1, qkv2, 2, (3, 6))
    advance(position[(UP, 2)])

    def self_end(i, rows):
        summed = res[pl.ds(rows, BLOCK), :] + attention_out(1, rows)
        section = normalize(summed, 1 + c, 1, rows)
        res[pl.ds(rows, BLOCK), :] = section
        sb[1, pl.ds(rows, BLOCK), :] = section.astype(BF16)

    blocks(self_end)

    own_copies[2].wait()
    advance(position[(UP, 3)])

    def feed_up(shard):
        def block(i, rows):
            left = sb[1, pl.ds(rows, BLOCK), :]
            for n in range(3):
                cols = slice(256 * n, 256 * n + 256)
                upward = dot_nn(left, wf[0, shard, :, cols])
                cumulative = 0.5 * (1.0 + lax.erf(upward * (0.5**0.5)))
                density = jnp.exp(-0.5 * upward * upward) * 0.3989422804014327
                act[shard, pl.ds(rows, BLOCK), cols] = (upward * cumulative).astype(BF16)
                gp[shard, pl.ds(rows, BLOCK), cols] = (cumulative + upward * density).astype(BF16)

        blocks(block)

    times(2, feed_up)
    advance(position[(DOWN, 1)])
    lax.fori_loop(2, 4, lambda k, carry: (feed_up(k), carry)[1], 0)
    own_copies[3].wait()
    advance(position[(DOWN, 2)])
    og_relay()
    advance(len(steps))

    def feed_down(i, rows):
        acc[pl.ds(rows, BLOCK), :] = res[pl.ds(rows, BLOCK), :]

        def shard_step(shard):
            left = act[shard, pl.ds(rows, BLOCK), :]
            for n in range(3):
                cols = slice(256 * n, 256 * n + 256)
                acc[pl.ds(rows, BLOCK), cols] += dot_nn(left, wf[1, shard, :, cols])

        times(4, shard_step)
        result = normalize(acc[pl.ds(rows, BLOCK), :], 3 + c, 2, rows)
        yb[pl.ds(rows, BLOCK), :] = result.astype(BF16)

    blocks(feed_down)

    def return_row(target):
        idents = [[new_id() for _ in range(3)] for _ in range(2)]
        send_base = new_id(12)
        local_ids = [local_counter[0] + k for k in range(3)]
        local_counter[0] += 3

        def each(action):
            for k in range(12):
                source_core = 0 if k < 4 else 1
                slots, part = k // 3, k % 3
                src = yb.at[pl.ds(64 * k - 256 * source_core, 64), :]
                for r in range(2):
                    dst = target.at[r, pl.ds(64 * part, 64), :]
                    mine = jnp.logical_and(c == source_core, turn == r)
                    here = jnp.logical_and(holder == c, t == slots)

                    @pl.when(jnp.logical_and(mine, here))
                    def _():
                        copy = pltpu.make_async_copy(src, dst, local_sems.at[local_ids[part]])
                        if action == "start":
                            copy.start()
                        elif action == "wait":
                            copy.wait()

                    @pl.when(jnp.logical_and(mine, jnp.logical_not(here)))
                    def _():
                        copy = remote(
                            src, dst, at(d_holder, slots), send_base + k, idents[r][part]
                        )
                        if action == "start":
                            copy.start()
                        elif action == "wait":
                            copy.wait_send()

        def begin():
            each("start")

        def close():
            each("wait")
            for r in range(2):
                for part in range(3):
                    dst = target.at[r, pl.ds(64 * part, 64), :]
                    k = 3 * t + part
                    source_core = jnp.where(k < 4, 0, 1)
                    from_here = jnp.logical_and(
                        jnp.logical_and(source_core == c, turn == r), holder == c
                    )

                    @pl.when(jnp.logical_not(from_here))
                    def _():
                        arrive(dst, idents[r][part])

        return begin, close

    y_begin, y_close = return_row(y_out)
    y_begin()
    og_finish()

    def grad_view(g, shard, half, low, count):
        if g >= UP:
            rows = aligned(384 * half + 96 * low, 16)
            return wf.at[g - UP, shard, pl.ds(rows, 96 * count), :]
        rows = aligned(192 * shard + 48 * low, 16)
        if g == SELF:
            return wa.at[SELF, pl.ds(2 * half, 2), pl.ds(rows, 48 * count), :]
        return wa.at[CROSS, pl.ds(2 * c + half, 1), pl.ds(rows, 48 * count), :]

    def first_buffer(g, half, shard):
        if g >= UP:
            return r1f.at[g - UP, half, shard]
        if g == SELF:
            return gp.at[pl.ds(2 * half, 2), pl.ds(aligned(96 * shard, 16), 96), :]
        return ogrow.at[pl.ds(aligned(384 * half + 96 * shard, 16), 96), :]

    def second_buffer(g, half, shard):
        if g >= UP:
            return r2f.at[g - UP, half, shard]
        return (r2s if g == SELF else r2c).at[half, shard]

    def third_buffer(g, half, m):
        if g >= UP:
            return r3f.at[g - UP, m - 1, half]
        return (r3s if g == SELF else r3c).at[m - 1, half]

    def out_view(g, half, low, count, owner):
        if g >= UP:
            target = up_out if g == UP else down_out
            return target.at[owner, pl.ds(aligned(384 * half + 96 * low, 16), 96 * count), :]
        rows = pl.ds(aligned(48 * low, 16), 48 * count)
        if g == SELF:
            return self_out.at[owner, pl.ds(2 * half, 2), rows, :]
        return cross_out.at[pl.ds(2 * owner + half, 1), rows, :]

    def out_whole(g, owner):
        if g >= UP:
            return (up_out if g == UP else down_out).at[owner]
        if g == SELF:
            return self_out.at[owner]
        return cross_out.at[pl.ds(2 * owner, 2)]

    own_quarter = [2 * px + py, px + 2 * py]
    own_pair = [2 * px, 2 * py]
    far_pair = [2 * (1 - px), 2 * (1 - py)]
    far_quarter = [2 * px + (1 - py), (1 - px) + 2 * py]
    near_quarter = {
        "x": [2 * (1 - px) + py, (1 - px) + 2 * py],
        "y": [2 * px + (1 - py), px + 2 * (1 - py)],
    }
    opposite = [2 * (1 - px) + (1 - py), (1 - px) + 2 * (1 - py)]
    first_way = [d_x, d_y]
    second_way = [d_y, d_x]

    def fold(target, pieces):
        shape = target.shape
        if len(shape) == 3:
            for a in range(shape[0]):
                fold(target.at[a], [piece.at[a] for piece in pieces])
            return
        total = target[...].astype(F32)
        for piece in pieces:
            total = total + piece[...].astype(F32)
        target[...] = total.astype(BF16)

    class Sum:
        def __init__(self, g):
            self.g = g
            self.s1 = [[new_id() for _ in range(4)] for _ in range(2)]
            self.s2 = [[new_id() for _ in range(4)] for _ in range(2)]
            self.s3 = [[new_id() for _ in range(4)] for _ in range(2)]
            self.to_x = [new_id() for _ in range(2)]
            self.to_y = [new_id() for _ in range(2)]
            self.across = [new_id() for _ in range(2)]
            self.core = new_id()
            self.keep = [local_counter[0], local_counter[0] + 1]
            local_counter[0] += 2

        def buffer1(self, half, shard):
            ref = first_buffer(self.g, half, shard)
            return ref

        def start(self, half, shard):
            g = self.g
            src = grad_view(g, shard, half, far_pair[half], 2)
            if g == CROSS:
                src = wa.at[
                    CROSS, 2 * c + half, pl.ds(aligned(192 * shard + 48 * far_pair[half], 16), 96), :
                ]
            send(
                src,
                self.buffer1(half, shard),
                at(first_way[half], t),
                self.s1[half][shard],
            )

        def stage2(self, half):
            g = self.g
            for shard in range(4):
                buffer = self.buffer1(half, shard)
                arrive(buffer, self.s1[half][shard])
                target = grad_view(g, shard, half, own_pair[half], 2)
                if g == CROSS:
                    target = wa.at[
                        CROSS,
                        2 * c + half,
                        pl.ds(aligned(192 * shard + 48 * own_pair[half], 16), 96),
                        :,
                    ]
                fold(target, [buffer])
                send(
                    grad_view(g, shard, half, far_quarter[half], 1),
                    second_buffer(g, half, shard),
                    at(second_way[half], t),
                    self.s2[half][shard],
                )

        def stage3(self, half):
            g = self.g
            for shard in range(4):
                buffer = second_buffer(g, half, shard)
                arrive(buffer, self.s2[half][shard])
                fold(grad_view(g, shard, half, own_quarter[half], 1), [buffer])
            for m in range(1, 4):
                send(
                    grad_view(g, (t + m) % 4, half, own_quarter[half], 1),
                    third_buffer(g, half, m),
                    at(d, (t + m) % 4),
                    self.s3[half][m],
                )

        def stage4(self, half):
            g = self.g
            pieces = []
            for m in range(1, 4):
                buffer = third_buffer(g, half, m)
                arrive(buffer, self.s3[half][m])
                pieces.append(buffer)
            total = grad_view(g, t, half, own_quarter[half], 1)
            fold(total, pieces)
            spot = out_view(g, half, own_quarter[half], 1, c)
            copy = pltpu.make_async_copy(total, spot, local_sems.at[self.keep[half]])
            copy.start()
            self.copies = getattr(self, "copies", []) + [copy]
            send(total, spot, at(d_x, t), self.to_x[half])
            send(total, spot, at(d_y, t), self.to_y[half])

        def stage5(self):
            g = self.g
            for half, way, ids in ((0, "x", self.to_x), (1, "y", self.to_y)):
                for other in range(2):
                    arrive(out_view(g, other, near_quarter[way][other], 1, c), ids[other])
                piece = out_view(g, half, near_quarter[way][half], 1, c)
                send(piece, piece, at(d_y if way == "x" else d_x, t), self.across[half])

        def stage6(self):
            g = self.g
            for half in range(2):
                arrive(out_view(g, half, opposite[half], 1, c), self.across[half])
            for copy in self.copies:
                copy.wait()
            send(out_whole(g, c), out_whole(g, c), at(d_core, t), self.core)

        def stage7(self):
            arrive(out_whole(self.g, 1 - c), self.core)

        def after(self):
            return [
                lambda: self.stage2(0),
                lambda: self.stage2(1),
                lambda: self.stage3(0),
                lambda: self.stage3(1),
                lambda: self.stage4(0),
                lambda: self.stage4(1),
                self.stage5,
                self.stage6,
                self.stage7,
            ]

    sums = {g: Sum(g) for g in (DOWN, UP, SELF, CROSS)}
    down_after, up_after = sums[DOWN].after(), sums[UP].after()
    self_after, cross_after = sums[SELF].after(), sums[CROSS].after()

    def norm_back(upstream, index, slot, rows):
        normed = xh[slot, pl.ds(rows, BLOCK), :].astype(F32)
        nrm[pl.ds(index, 1), :] += jnp.sum(upstream * normed, axis=0, keepdims=True)
        nrm[pl.ds(index + 8, 1), :] += jnp.sum(upstream, axis=0, keepdims=True)
        scaled = upstream * gains[pl.ds(index, 1), :]
        grad = rstd[slot, pl.ds(rows, BLOCK), :] * (
            scaled
            - jnp.mean(scaled, axis=-1, keepdims=True)
            - normed * jnp.mean(scaled * normed, axis=-1, keepdims=True)
        )
        res[pl.ds(rows, BLOCK), :] = grad
        dzb[pl.ds(rows, BLOCK), :] = grad.astype(BF16)

    def out_back(i, rows):
        upstream = ogrow[pl.ds(aligned(own_base + rows, BLOCK), BLOCK), :].astype(F32)
        norm_back(upstream, 3 + c, 2, rows)

    blocks(out_back)
    og_close()
    for wait in pending:
        wait()
    pending.clear()
    for device in (d_x, d_y):
        pl.semaphore_signal(credit.at[0], inc=1, device_id=at(device, t), device_id_type=MESH)

    def down_back(shard):
        def block(i, rows):
            left = dzb[pl.ds(rows, BLOCK), :]
            for n in range(3):
                cols = slice(256 * n, 256 * n + 256)
                active_grad = dot_nt(left, wf[1, shard, cols, :])
                slope = gp[shard, pl.ds(rows, BLOCK), cols].astype(F32)
                gp[shard, pl.ds(rows, BLOCK), cols] = (active_grad * slope).astype(BF16)

        blocks(block)
        for n in range(3):
            cols = slice(256 * n, 256 * n + 256)
            left = jnp.transpose(act[shard, :, cols])
            for k in range(3):
                wide = slice(256 * k, 256 * k + 256)
                wf[1, shard, cols, wide] = dot_nn(left, dzb[:, wide]).astype(BF16)

    for shard in range(4):
        down_back(shard)
        for half in range(2):
            sums[DOWN].start(half, shard)

    def up_input(i, rows):
        for n in range(3):
            cols = slice(256 * n, 256 * n + 256)
            total = res[pl.ds(rows, BLOCK), cols]
            for shard in range(4):
                total = total + dot_nt(gp[shard, pl.ds(rows, BLOCK), :], wf[0, shard, cols, :])
            acc[pl.ds(rows, BLOCK), cols] = total

    blocks(up_input)
    tt[1] = jnp.transpose(sb[1])

    def up_weights(shard):
        for n in range(3):
            cols = slice(256 * n, 256 * n + 256)
            left = tt[1, cols, :]
            for k in range(3):
                wide = slice(256 * k, 256 * k + 256)
                wf[0, shard, cols, wide] = dot_nn(left, gp[shard, :, wide]).astype(BF16)

    for shard in range(4):
        up_weights(shard)
        for half in range(2):
            sums[UP].start(half, shard)
    for device in (d_x, d_y):
        pl.semaphore_signal(credit.at[1], inc=1, device_id=at(device, t), device_id_type=MESH)

    blocks(lambda i, rows: norm_back(acc[pl.ds(rows, BLOCK), :], 1 + c, 1, rows))

    dctx = act.at[0]

    def context_back(which):
        def block(i, rows):
            left = dzb[pl.ds(rows, BLOCK), :]
            for n in range(3):
                cols = slice(256 * n, 256 * n + 256)
                dctx[pl.ds(rows, BLOCK), cols] = dot_nt(left, wa[which, 3, cols, :]).astype(BF16)

        blocks(block)

    def weight_rows(which, member, left_ref, rights):
        def tile(n):
            rows = aligned(n * 256, 256)
            for k in range(3):
                wide = slice(256 * k, 256 * k + 256)
                total = None
                for low, size, ref in rights:
                    term = dot_nn(
                        left_ref[pl.ds(rows, 256), low : low + size], ref[:, wide]
                    )
                    total = term if total is None else total + term
                wa[which, member, pl.ds(rows, 256), wide] = total.astype(BF16)

        times(3, tile)

    def attend_back(which, qkv, code_row, pairs):
        def pair(k, carry):
            lanes = pl.ds(aligned(k * 128, 128), 128)
            key = qkv[1, :, lanes]
            value = qkv[2, :, lanes]
            key_t = jnp.transpose(key)
            kv_acc[...] = jnp.zeros_like(kv_acc)

            def block(i, rows):
                query = qkv[0, pl.ds(rows, BLOCK), lanes] * jnp.asarray(scaling, BF16)
                grad = dctx[pl.ds(rows, BLOCK), lanes]
                query_code = codes[
                    pl.ds(code_row, 1), pl.ds(aligned(own_base + rows, BLOCK), BLOCK)
                ]
                allowed = kcode[which, :, 0:1] == query_code
                for h in range(2):
                    query_h = query * head_lanes[h]
                    grad_h = grad * head_lanes[h]
                    scores = jnp.where(allowed, dot_nt(key, query_h), -1e30)
                    probs = jnp.exp(
                        scores - lse[which, pl.ds(2 * k + h, 1), pl.ds(rows, BLOCK)]
                    )
                    probs_grad = dot_nt(value, grad_h)
                    delta = jnp.sum(probs * probs_grad, axis=0, keepdims=True)
                    score_grad = (probs * (probs_grad - delta)).astype(BF16)
                    kv_acc[0] += dot_nn(score_grad, query_h)
                    kv_acc[1] += dot_nn(probs.astype(BF16), grad_h)
                    tt[
                        0, pl.ds(aligned(k * 128 + h * 64, 64), 64), pl.ds(rows, BLOCK)
                    ] = (dot_nn(key_t[64 * h : 64 * h + 64, :], score_grad) * scaling).astype(BF16)

            blocks(block)
            for m in range(2):
                tt[1 + m, pl.ds(aligned(k * 128, 128), 128), :] = jnp.transpose(
                    kv_acc[m]
                ).astype(BF16)
            return carry

        lax.fori_loop(pairs[0], pairs[1], pair, 0)

    queue = []

    def pump(count):
        for _ in range(count):
            if queue:
                queue.pop(0)()

    context_back(SELF)
    weight_rows(SELF, 3, ctx_t.at[1], [(0, 512, dzb)])
    queue += down_after[:2]
    attend_back(1, qkv2, 2, (0, 3))
    pump(2)
    queue += up_after[:2]
    attend_back(1, qkv2, 2, (3, 6))
    pump(2)
    queue += down_after[2:4]

    def self_input(i, rows):
        parts = [jnp.transpose(tt[m, :, pl.ds(rows, BLOCK)]) for m in range(3)]
        for n in range(3):
            cols = slice(256 * n, 256 * n + 256)
            total = res[pl.ds(rows, BLOCK), cols]
            for m in range(3):
                total = total + dot_nn(parts[m], wa[SELF, m, :, cols])
            acc[pl.ds(rows, BLOCK), cols] = total

    blocks(self_input)
    for m in range(3):
        weight_rows(SELF, m, tt.at[m], [(0, 512, sb.at[0])])
    pl.semaphore_wait(credit.at[1], 2)
    for half in range(2):
        for shard in range(4):
            sums[SELF].start(half, shard)
    pl.semaphore_signal(credit.at[2], inc=1, device_id=at(d_core, t), device_id_type=MESH)
    pump(2)
    queue += up_after[2:4] + down_after[4:6]

    blocks(lambda i, rows: norm_back(acc[pl.ds(rows, BLOCK), :], 0, 0, rows))

    norm_ids = [new_id() for _ in range(5)]
    norm_ways = [
        at(d_core, t),
        at(d_x, t),
        at(d_y, t),
        at(d, t + 1 - 2 * (t % 2)),
        at(d, (t + 2) % 4),
    ]
    norm_steps = []

    def norm_begin(k):
        send(nrm if k == 0 else nrm_recv.at[k - 1, 1], nrm_recv.at[k, 0], norm_ways[k], norm_ids[k])

    def norm_step(k):
        arrive(nrm_recv.at[k, 0], norm_ids[k])
        mine = nrm[...] if k == 0 else nrm_recv[k - 1, 1]
        total = mine + nrm_recv[k, 0]
        if k < 4:
            nrm_recv[k, 1] = total
            norm_begin(k + 1)
        else:
            norm_out[...] = total

    norm_begin(0)
    context_back(CROSS)
    weight_rows(CROSS, 3, ctx_t.at[0], [(0, 512, dzb)])
    norm_step(0)
    pump(2)
    attend_back(0, qkv1, 0, (0, 3))
    norm_step(1)
    pump(2)
    queue += self_after[:2]
    attend_back(0, qkv1, 0, (3, 6))
    norm_step(2)
    pump(2)
    queue += up_after[4:6] + down_after[6:7]

    key_ids = [new_id() for _ in range(2)]

    def key_input(j):
        parts = [jnp.transpose(tt[m, :, 256 * j : 256 * j + 256]) for m in (1, 2)]
        for n in range(3):
            cols = slice(256 * n, 256 * n + 256)
            act[1, 256 * j : 256 * j + 256, cols] = (
                dot_nn(parts[0], wa[CROSS, 1, :, cols]) + dot_nn(parts[1], wa[CROSS, 2, :, cols])
            ).astype(BF16)

    key_input(0)
    key_input(1)
    key_copies = [
        remote(
            act.at[1, pl.ds(256 * j, 256), :],
            dhk_recv.at[j],
            at(d_core, t),
            key_ids[j],
        )
        for j in range(2)
    ]
    key_copies[0].start()

    @pl.when(c == 0)
    def _():
        key_copies[1].start()

    def cross_input(i, rows):
        part = jnp.transpose(tt[0, :, pl.ds(rows, BLOCK)])
        for n in range(3):
            cols = slice(256 * n, 256 * n + 256)
            res[pl.ds(rows, BLOCK), cols] += dot_nn(part, wa[CROSS, 0, :, cols])

    blocks(cross_input)
    weight_rows(CROSS, 0, tt.at[0], [(0, 512, xrow.at[pl.ds(own_base, 512), :])])
    for m in range(1, 3):
        weight_rows(
            CROSS,
            m,
            tt.at[m],
            [
                (0, 256, xrow.at[pl.ds(other_base, 256), :]),
                (256, 256, xrow.at[pl.ds(512, 256), :]),
            ],
        )

    pl.semaphore_wait(credit.at[2], 1)
    core_sums = [(a, n, new_id()) for a in range(2) for n in range(3)]

    def core_slot(a, n):
        k = 3 * a + n
        return qkv2.at[k // 2, pl.ds(256 * (k % 2), 256), :]

    for a, n, ident in core_sums:
        send(
            wa.at[CROSS, 2 * (1 - c) + a, pl.ds(256 * n, 256), :],
            core_slot(a, n),
            at(d_core, t),
            ident,
        )
    norm_step(3)

    y_close()
    arrive(dhk_recv.at[0], key_ids[0])

    @pl.when(c == 1)
    def _():
        arrive(dhk_recv.at[1], key_ids[1])

    yb[:BLOCK, :] = (res[:BLOCK, :] + dhk_recv[0].astype(F32)).astype(BF16)

    @pl.when(c == 1)
    def _():
        own_part = act[1, BLOCK:, :].astype(F32)
        yb[BLOCK:, :] = (res[BLOCK:, :] + dhk_recv[1].astype(F32) + own_part).astype(BF16)

    dx_begin, dx_close = return_row(dx_out)
    dx_begin()

    for a, n, ident in core_sums:
        arrive(core_slot(a, n), ident)
        fold(wa.at[CROSS, 2 * c + a, pl.ds(256 * n, 256), :], [core_slot(a, n)])
    pl.semaphore_wait(credit.at[0], 2)
    for half in range(2):
        for shard in range(4):
            sums[CROSS].start(half, shard)
    norm_step(4)
    tail = {DOWN: down_after, UP: up_after, SELF: self_after, CROSS: cross_after}
    queue += tail[SELF][2:4] + tail[UP][6:7] + tail[DOWN][7:8] + tail[SELF][4:6]
    queue += tail[CROSS][:4] + tail[UP][7:8] + tail[SELF][6:7] + tail[CROSS][4:6]
    queue += tail[SELF][7:8] + tail[CROSS][6:8]
    queue += [tail[g][8] for g in (DOWN, UP, SELF, CROSS)]
    pump(len(queue))
    for wait in pending:
        wait()
    key_copies[0].wait_send()

    @pl.when(c == 0)
    def _():
        key_copies[1].wait_send()

    dx_close()
    if counter[0] > SEMAPHORES or local_counter[0] > LOCALS:
        raise ValueError((counter[0], local_counter[0]))


SEMAPHORES = 320
LOCALS = 40


def call_layer(*operands):
    def vmem(shape, dtype=BF16):
        return pltpu.VMEM(shape, dtype)

    anywhere = pl.BlockSpec(memory_space=pl.ANY)
    whole = pl.BlockSpec(memory_space=pltpu.VMEM)
    x_in = operands[0]
    return pl.pallas_call(
        layer_kernel,
        name="cross_modality_layer",
        out_shape=(
            jax.ShapeDtypeStruct(x_in.shape, BF16),
            jax.ShapeDtypeStruct(x_in.shape, BF16),
            jax.ShapeDtypeStruct((4, 192, 768), BF16),
            jax.ShapeDtypeStruct((2, 4, 192, 768), BF16),
            jax.ShapeDtypeStruct((2, 768, 768), BF16),
            jax.ShapeDtypeStruct((2, 768, 768), BF16),
            jax.ShapeDtypeStruct((16, 768), F32),
        ),
        in_specs=[anywhere] * 7 + [whole] * 2,
        out_specs=(anywhere,) * 6 + (whole,),
        scratch_shapes=[
            vmem((2, 4, 768, 768)),
            vmem((2, 4, 768, 768)),
            vmem((768, 768)),
            vmem((768, 768)),
            vmem((8, 768), F32),
            vmem((2, 512, 128), F32),
            vmem((3, 512, 768)),
            vmem((3, 512, 768)),
            vmem((2, 768, 512)),
            vmem((2, 16, 512), F32),
            vmem((3, 512, 768)),
            vmem((3, 512, 1), F32),
            vmem((2, 512, 768)),
            vmem((512, 768), F32),
            vmem((512, 768), F32),
            vmem((4, 512, 768)),
            vmem((4, 512, 768)),
            vmem((512, 768)),
            vmem((3, 768, 512)),
            vmem((512, 768)),
            vmem((2, 256, 768)),
            vmem((2, 512, 128), F32),
            vmem((16, 768), F32),
            vmem((5, 2, 16, 768), F32),
            vmem((2, 2, 4, 192, 768)),
            vmem((2, 2, 4, 96, 768)),
            vmem((2, 3, 2, 96, 768)),
            vmem((2, 4, 2, 48, 768)),
            vmem((3, 2, 2, 48, 768)),
            vmem((2, 4, 1, 48, 768)),
            vmem((3, 2, 1, 48, 768)),
            pltpu.SemaphoreType.DMA((SEMAPHORES,)),
            pltpu.SemaphoreType.DMA((SEMAPHORES,)),
            pltpu.SemaphoreType.DMA((LOCALS,)),
            pltpu.SemaphoreType.REGULAR((3,)),
        ],
        compiler_params=pltpu.CompilerParams(
            collective_id=0, has_side_effects=True, vmem_limit_bytes=64 * 1024 * 1024 - 512 * 1024
        ),
    )(*operands)


def solution(mesh):
    extra = []
    step = 8
    while step < mesh.shape["dp"]:
        extra.append(step)
        step *= 2

    def total(array):
        for step in extra:
            pairs = [(k, k ^ step) for k in range(mesh.shape["dp"])]
            array = array + lax.ppermute(array, "dp", pairs)
        return array

    def body(
        layer_input,
        word_segments,
        image_order,
        cross_qkv,
        cross_out,
        self_qkv,
        self_out,
        ffn_up,
        ffn_down,
        norm_gains,
        norm_biases,
        out_grad,
    ):
        rows = layer_input.shape[0]
        images = jnp.repeat(image_order, BOXES, axis=1)
        pads = jnp.full((rows, PADS), CAPTIONS, jnp.int32)
        none = jnp.full((rows, WORDS + REGIONS + PADS), -1, jnp.int32)
        groups = jnp.concatenate([word_segments, images, pads], axis=1)
        keys = jnp.concatenate([word_segments, none[:, :REGIONS], pads], axis=1)
        kinds = jnp.concatenate([word_segments, images + 16, pads + 32], axis=1)
        codes = jnp.stack([groups, keys, kinds, none, none, none, none, none], axis=1).astype(F32)
        cross = jnp.concatenate([jnp.swapaxes(cross_qkv, 1, 2), cross_out[None]], axis=0)
        own = jnp.concatenate([jnp.swapaxes(self_qkv, 2, 3), self_out[:, None]], axis=1)
        y, dx, d_cross, d_self, d_up, d_down, d_norm = call_layer(
            layer_input,
            out_grad,
            codes,
            cross,
            own,
            ffn_up,
            ffn_down,
            norm_gains,
            norm_biases,
        )
        d_cross, d_self, d_up, d_down = [
            total(array.astype(F32)) for array in (d_cross, d_self, d_up, d_down)
        ]
        d_norm = total(d_norm)
        return (
            y,
            dx.astype(F32),
            jnp.swapaxes(d_cross[:3], 1, 2),
            d_cross[3],
            jnp.swapaxes(d_self[:, :3], 2, 3),
            d_self[:, 3],
            d_up,
            d_down,
            d_norm[0:5],
            d_norm[8:13],
        )

    in_specs = (
        P("dp", "tensor", None),
        P("dp", None),
        P("dp", None),
        P(None, None, "tensor"),
        P("tensor", None),
        P(None, None, None, "tensor"),
        P(None, "tensor", None),
        P(None, None, "tensor"),
        P(None, "tensor", None),
        P(),
        P(),
        P("dp", "tensor", None),
    )
    out_specs = (
        P("dp", "tensor", None),
        P("dp", "tensor", None),
        P(None, None, "tensor"),
        P("tensor", None),
        P(None, None, None, "tensor"),
        P(None, "tensor", None),
        P(None, None, "tensor"),
        P(None, "tensor", None),
        P(),
        P(),
    )
    return jax.shard_map(body, mesh=mesh, in_specs=in_specs, out_specs=out_specs, check_vma=False)
```

```python
import functools

import jax
import jax.numpy as jnp
from jax import lax
from jax.experimental import pallas as pl
from jax.experimental.pallas import tpu as pltpu
from jax.sharding import PartitionSpec as P

HEAD_DIM = 64
WORDS = 256
CAPTIONS = 14
BOXES = 36
REGIONS = 504
PADS = 8
NORM_EPSILON = 1e-12
BLOCK = 256
BF16 = jnp.bfloat16
F32 = jnp.float32
MESH = pl.DeviceIdType.MESH
CROSS, SELF, UP, DOWN = 0, 1, 2, 3


def dot_nn(left, right):
    return jnp.dot(left, right, preferred_element_type=F32)


def dot_nt(left, right):
    return lax.dot_general(left, right, (((1,), (1,)), ((), ())), preferred_element_type=F32)


def aligned(value, step):
    return pl.multiple_of(value, step)


def layer_kernel(
    x_in,
    og_in,
    codes_in,
    cross_in,
    self_in,
    up_in,
    down_in,
    gains,
    biases,
    y_out,
    dx_out,
    cross_out,
    self_out,
    up_out,
    down_out,
    norm_out,
    wa,
    wf,
    xrow,
    ogrow,
    codes,
    kcode,
    qkv1,
    qkv2,
    ctx_t,
    lse,
    xh,
    rstd,
    sb,
    res,
    acc,
    act,
    gp,
    dzb,
    tt,
    yb,
    dhk_recv,
    kv_acc,
    nrm,
    nrm_recv,
    r1f,
    r2f,
    r3f,
    r2s,
    r3s,
    r2c,
    r3c,
    send_sems,
    recv_sems,
    local_sems,
    credit,
):
    d = lax.axis_index("dp")
    t = lax.axis_index("tensor")
    c = d % 2
    px = (d // 2) % 2
    py = (d // 4) % 2
    q = px + 2 * py
    d_core = d + 1 - 2 * c
    d_x = d + 2 - 4 * px
    d_y = d + 4 - 8 * py
    holder = t // 2
    d_holder = d - c + holder
    turn = t % 2
    nb = 1 + c
    near = {"x": d_x, "y": d_y, "core": d_core}

    def at(dp_index, tensor_index):
        return {"dp": dp_index, "tensor": tensor_index}

    counter = [0]
    local_counter = [0]
    pending = []

    def new_id(count=1):
        counter[0] += count
        return counter[0] - count

    def remote(src, dst, device, ident, arrival=None):
        return pltpu.make_async_remote_copy(
            src_ref=src,
            dst_ref=dst,
            send_sem=send_sems.at[ident],
            recv_sem=recv_sems.at[ident if arrival is None else arrival],
            device_id=device,
            device_id_type=MESH,
        )

    def send(src, dst, device, ident):
        copy = remote(src, dst, device, ident)
        copy.start()
        pending.append(copy.wait_send)

    def arrive(dst, ident):
        remote(dst, dst, at(d_core, t), ident).wait_recv()

    def local(src, dst):
        copy = pltpu.make_async_copy(src, dst, local_sems.at[local_counter[0]])
        local_counter[0] += 1
        return copy

    def blocks(body):
        def step(i, carry):
            body(i, aligned(i * BLOCK, BLOCK))
            return carry

        lax.fori_loop(0, nb, step, 0)

    def times(count, body):
        def step(i, carry):
            body(i)
            return carry

        lax.fori_loop(0, count, step, 0)

    barrier = pltpu.get_barrier_semaphore()
    partners = [at(d_core, t), at(d_x, t), at(d_y, t)]
    for m in range(1, 4):
        partners.append(at(d, (t + m) % 4))
        partners.append(at(d_core, (t + m) % 4))
    for partner in partners:
        pl.semaphore_signal(barrier, inc=1, device_id=partner, device_id_type=MESH)

    half_rows = aligned(t * 192, 16)
    own_copies = [
        local(cross_in, wa.at[CROSS, :, pl.ds(half_rows, 192), :]),
        local(self_in.at[c], wa.at[SELF, :, pl.ds(half_rows, 192), :]),
        local(up_in.at[c], wf.at[0, t]),
        local(down_in.at[c], wf.at[1, t]),
    ]
    for copy in own_copies:
        copy.start()

    zero_half = jnp.zeros((BLOCK, 768), BF16)

    @pl.when(c == 0)
    def _():
        for ref in (qkv2.at[1], qkv2.at[2], sb.at[0], sb.at[1], dzb):
            ref[BLOCK:, :] = zero_half
        for k in range(4):
            act[k, BLOCK:, :] = zero_half
            gp[k, BLOCK:, :] = zero_half
        for k in range(2):
            ctx_t[k, :, BLOCK:] = jnp.zeros((768, BLOCK), BF16)
        tt[0, :, BLOCK:] = jnp.zeros((768, BLOCK), BF16)

    nrm[...] = jnp.zeros_like(nrm)
    pl.semaphore_wait(barrier, len(partners))

    def spread_row(source, row):
        base = new_id(4)
        core_base = new_id(4)
        own = local(source.at[turn], row.at[pl.ds(half_rows, 192), :])

        def each_target(action):
            for r in range(2):
                target = 2 * c + r

                @pl.when(target != t)
                def _():
                    action(
                        remote(
                            source.at[r],
                            row.at[pl.ds(half_rows, 192), :],
                            at(d, target),
                            base + r,
                            base + t,
                        )
                    )

        def each_relay(action):
            @pl.when(holder == c)
            def _():
                for s in range(4):
                    part = row.at[pl.ds(192 * s, 192), :]
                    action(s, part, remote(part, part, at(d_core, t), core_base + s))

        def begin():
            each_target(lambda copy: copy.start())

            @pl.when(holder == c)
            def _():
                own.start()

        def relay():
            def action(s, part, copy):
                @pl.when(t == s)
                def _():
                    own.wait()

                @pl.when(t != s)
                def _():
                    arrive(part, base + s)

                copy.start()

            each_relay(action)

        def finish():
            @pl.when(holder != c)
            def _():
                for s in range(4):
                    arrive(row.at[pl.ds(192 * s, 192), :], core_base + s)

        def close():
            each_target(lambda copy: copy.wait_send())
            each_relay(lambda s, part, copy: copy.wait_send())

        return begin, relay, finish, close

    x_begin, x_relay, x_finish, x_close = spread_row(x_in, xrow)
    og_begin, og_relay, og_finish, og_close = spread_row(og_in, ogrow)
    pending.append(x_close)

    code_ident = new_id()
    code_own = local(codes_in.at[turn], codes)

    @pl.when(holder == c)
    def _():
        code_own.start()
        remote(codes_in.at[turn], codes, at(d_core, t), code_ident).start()

    def share(g, shard, quarter, low, high):
        if g >= UP:
            rows = aligned(quarter * 192 + low * 96, 16)
            return wf.at[g - UP, shard, pl.ds(rows, (high - low) * 96), :]
        rows = aligned(shard * 192 + quarter * 48, 16)
        if g == SELF:
            return wa.at[SELF, pl.ds(2 * low, 2 * (high - low)), pl.ds(rows, 48), :]
        return wa.at[CROSS, pl.ds(2 * c + low, high - low), pl.ds(rows, 48), :]

    def own_share(g):
        if g >= UP:
            source = up_in if g == UP else down_in
            return source.at[c, pl.ds(aligned(q * 192, 16), 192), :]
        rows = pl.ds(aligned(q * 48, 16), 48)
        if g == SELF:
            return self_in.at[c, :, rows, :]
        return cross_in.at[pl.ds(2 * c, 2), rows, :]

    qx, qy = (1 - px) + 2 * py, px + 2 * (1 - py)
    qd = (1 - px) + 2 * (1 - py)
    items = [(g, m) for g in (CROSS, SELF, UP, DOWN) for m in range(1, 4)]
    z_base = {g: new_id(4) for g in (CROSS, SELF, UP, DOWN)}
    own_ids = {g: new_id(2) for g in (CROSS, SELF, UP, DOWN)}
    pass_ids = {item: new_id() for item in items}
    x_ids = {item: new_id() for item in items}
    y_ids = {item: new_id() for item in items}
    fx_ids = {item: new_id() for item in items}
    fy_ids = {item: new_id() for item in items}
    core_ids = {m: new_id() for m in range(1, 4)}
    arrivals = {
        1: t + 1 - 2 * (t % 2),
        2: 2 - t // 2,
        3: 3 - 3 * (t // 2),
    }

    def z_way(g, way):
        exists = t > 0 if way == 0 else t < 3
        target = t - 1 + 2 * way

        def copy():
            return remote(
                own_share(g),
                share(g, t, q, 0, 2),
                at(d, target),
                own_ids[g] + way,
                z_base[g] + t,
            )

        @pl.when(exists)
        def _():
            copy().start()

        def close():
            @pl.when(exists)
            def _():
                copy().wait_send()

        pending.append(close)

    def z_own(g):
        for way in range(2):
            z_way(g, way)

    def first(item):
        g, m = item
        shard = arrivals[m]
        piece = share(g, shard, q, 0, 2)
        arrive(piece, z_base[g] + shard)
        inner = jnp.logical_and(t > 0, t < 3)
        target = jnp.where(shard < t, t + 1, t - 1)

        def copy():
            return remote(piece, piece, at(d, target), pass_ids[item], z_base[g] + shard)

        @pl.when(inner)
        def _():
            copy().start()

        def close():
            @pl.when(inner)
            def _():
                copy().wait_send()

        pending.append(close)
        send(piece, piece, at(d_x, t), x_ids[item])
        send(piece, piece, at(d_y, t), y_ids[item])
        if m == 1 and g < DOWN:
            z_own(g + 1)
        if g == CROSS and m == 1:
            x_begin()
        if item == (DOWN, 1):
            og_begin()

    def second(item):
        g, m = item
        shard = arrivals[m]
        arrive(share(g, shard, qx, 0, 2), x_ids[item])
        low = share(g, shard, qx, 0, 1)
        send(low, low, at(d_y, t), fy_ids[item])
        arrive(share(g, shard, qy, 0, 2), y_ids[item])
        high = share(g, shard, qy, 1, 2)
        send(high, high, at(d_x, t), fx_ids[item])

    def third(item):
        g, m = item
        shard = arrivals[m]
        arrive(share(g, shard, qd, 0, 1), fy_ids[item])
        arrive(share(g, shard, qd, 1, 2), fx_ids[item])
        if g == CROSS:
            rows = pl.ds(aligned(shard * 192, 16), 192)
            whole = wa.at[CROSS, pl.ds(2 * c, 2), rows, :]
            send(whole, whole, at(d_core, t), core_ids[m])

    def last(m):
        shard = arrivals[m]
        rows = pl.ds(aligned(shard * 192, 16), 192)
        arrive(wa.at[CROSS, pl.ds(2 * (1 - c), 2), rows, :], core_ids[m])

    z_own(CROSS)

    steps = []
    position = {}
    for k in range(len(items) + 2):
        if k < len(items):
            steps.append(functools.partial(first, items[k]))
        if 0 <= k - 1 < len(items):
            steps.append(functools.partial(second, items[k - 1]))
        if 0 <= k - 2 < len(items):
            steps.append(functools.partial(third, items[k - 2]))
            position[items[k - 2]] = len(steps)
    done = [0]

    def advance(upto):
        while done[0] < min(upto, len(steps)):
            steps[done[0]]()
            done[0] += 1

    advance(position[(CROSS, 2)])
    x_relay()
    x_finish()

    @pl.when(holder == c)
    def _():
        code_own.wait()
        remote(codes_in.at[turn], codes, at(d_core, t), code_ident).wait_send()

    @pl.when(holder != c)
    def _():
        arrive(codes, code_ident)

    def as_column(row):
        return jnp.transpose(jnp.broadcast_to(row, (128, BLOCK)))

    own_base = aligned(c * BLOCK, BLOCK)
    other_base = aligned((1 - c) * BLOCK, BLOCK)
    kcode[0, :BLOCK, :] = as_column(codes[0:1, pl.ds(other_base, BLOCK)])
    kcode[0, BLOCK:, :] = as_column(codes[pl.ds(c, 1), 512:768])
    kcode[1, :BLOCK, :] = as_column(codes[2:3, pl.ds(own_base, BLOCK)])
    kcode[1, BLOCK:, :] = as_column(codes[pl.ds(3 - c, 1), 512:768])

    lane = lax.broadcasted_iota(jnp.int32, (1, 128), 1)
    head_lanes = [
        (lane < HEAD_DIM).astype(F32).astype(BF16),
        (lane >= HEAD_DIM).astype(F32).astype(BF16),
    ]
    scaling = HEAD_DIM ** (-0.5)

    def project(source, base, weight, target, rows):
        left = source[pl.ds(base, BLOCK), :]
        for n in range(3):
            target[pl.ds(rows, BLOCK), 256 * n : 256 * n + 256] = dot_nt(
                left, weight[256 * n : 256 * n + 256, :]
            ).astype(BF16)

    def attend(which, qkv, code_row, pairs):
        def pair(k):
            lanes = pl.ds(aligned(k * 128, 128), 128)
            key = qkv[1, :, lanes]
            value_t = jnp.transpose(qkv[2, :, lanes])

            def block(i, rows):
                query = qkv[0, pl.ds(rows, BLOCK), lanes] * jnp.asarray(scaling, BF16)
                query_code = codes[
                    pl.ds(code_row, 1), pl.ds(aligned(own_base + rows, BLOCK), BLOCK)
                ]
                allowed = kcode[which, :, 0:1] == query_code
                for h in range(2):
                    scores = dot_nt(key, query * head_lanes[h])
                    scores = jnp.where(allowed, scores, -1e30)
                    top = jnp.max(scores, axis=0, keepdims=True)
                    exponent = jnp.exp(scores - top)
                    total = jnp.sum(exponent, axis=0, keepdims=True)
                    probs = (exponent * (1.0 / total)).astype(BF16)
                    lse[which, pl.ds(2 * k + h, 1), pl.ds(rows, BLOCK)] = top + jnp.log(total)
                    ctx_t[
                        which,
                        pl.ds(aligned(k * 128 + h * 64, 64), 64),
                        pl.ds(rows, BLOCK),
                    ] = dot_nn(value_t[64 * h : 64 * h + 64, :], probs).astype(BF16)

            blocks(block)

        def run(k, carry):
            pair(k)
            return carry

        lax.fori_loop(pairs[0], pairs[1], run, 0)

    def normalize(summed, index, slot, rows):
        center = summed - jnp.mean(summed, axis=-1, keepdims=True)
        inverse = lax.rsqrt(jnp.mean(center * center, axis=-1, keepdims=True) + NORM_EPSILON)
        normed = center * inverse
        xh[slot, pl.ds(rows, BLOCK), :] = normed.astype(BF16)
        rstd[slot, pl.ds(rows, BLOCK), :] = inverse
        return normed * gains[pl.ds(index, 1), :] + biases[pl.ds(index, 1), :]

    def attention_out(which, rows):
        context = jnp.transpose(ctx_t[which, :, pl.ds(rows, BLOCK)])
        return dot_nn(context, wa[which, 3])

    for copy in own_copies[:1]:
        copy.wait()
    advance(position[(CROSS, 3)])
    for m in range(1, 4):
        last(m)
    blocks(lambda i, rows: project(xrow, own_base + rows, wa.at[CROSS, 0], qkv1.at[0], rows))
    for k in range(1, 3):
        project(xrow, other_base, wa.at[CROSS, k], qkv1.at[k], 0)
        project(xrow, 512, wa.at[CROSS, k], qkv1.at[k], BLOCK)
    attend(0, qkv1, 0, (0, 3))
    advance(position[(SELF, 1)])
    attend(0, qkv1, 0, (3, 6))
    advance(position[(SELF, 2)])

    def cross_end(i, rows):
        stream = xrow[pl.ds(aligned(own_base + rows, BLOCK), BLOCK), :].astype(F32)
        section = normalize(stream + attention_out(0, rows), 0, 0, rows)
        res[pl.ds(rows, BLOCK), :] = section
        sb[0, pl.ds(rows, BLOCK), :] = section.astype(BF16)

    blocks(cross_end)

    own_copies[1].wait()
    advance(position[(SELF, 3)])
    for k in range(3):
        blocks(lambda i, rows: project(sb.at[0], rows, wa.at[SELF, k], qkv2.at[k], rows))
    attend(1, qkv2, 2, (0, 3))
    advance(position[(UP, 1)])
    attend(1, qkv2, 2, (3, 6))
    advance(position[(UP, 2)])

    def self_end(i, rows):
        summed = res[pl.ds(rows, BLOCK), :] + attention_out(1, rows)
        section = normalize(summed, 1 + c, 1, rows)
        res[pl.ds(rows, BLOCK), :] = section
        sb[1, pl.ds(rows, BLOCK), :] = section.astype(BF16)

    blocks(self_end)

    own_copies[2].wait()
    advance(position[(UP, 3)])

    def feed_up(shard):
        def block(i, rows):
            left = sb[1, pl.ds(rows, BLOCK), :]
            for n in range(3):
                cols = slice(256 * n, 256 * n + 256)
                upward = dot_nn(left, wf[0, shard, :, cols])
                cumulative = 0.5 * (1.0 + lax.erf(upward * (0.5**0.5)))
                density = jnp.exp(-0.5 * upward * upward) * 0.3989422804014327
                act[shard, pl.ds(rows, BLOCK), cols] = (upward * cumulative).astype(BF16)
                gp[shard, pl.ds(rows, BLOCK), cols] = (cumulative + upward * density).astype(BF16)

        blocks(block)

    times(2, feed_up)
    advance(position[(DOWN, 1)])
    lax.fori_loop(2, 4, lambda k, carry: (feed_up(k), carry)[1], 0)
    own_copies[3].wait()
    advance(position[(DOWN, 2)])
    og_relay()
    advance(len(steps))

    def feed_down(i, rows):
        acc[pl.ds(rows, BLOCK), :] = res[pl.ds(rows, BLOCK), :]

        def shard_step(shard):
            left = act[shard, pl.ds(rows, BLOCK), :]
            for n in range(3):
                cols = slice(256 * n, 256 * n + 256)
                acc[pl.ds(rows, BLOCK), cols] += dot_nn(left, wf[1, shard, :, cols])

        times(4, shard_step)
        result = normalize(acc[pl.ds(rows, BLOCK), :], 3 + c, 2, rows)
        yb[pl.ds(rows, BLOCK), :] = result.astype(BF16)

    blocks(feed_down)

    def return_row(target):
        idents = [[new_id() for _ in range(3)] for _ in range(2)]
        send_base = new_id(12)
        local_ids = [local_counter[0] + k for k in range(3)]
        local_counter[0] += 3

        def each(action):
            for k in range(12):
                source_core = 0 if k < 4 else 1
                slots, part = k // 3, k % 3
                src = yb.at[pl.ds(64 * k - 256 * source_core, 64), :]
                for r in range(2):
                    dst = target.at[r, pl.ds(64 * part, 64), :]
                    mine = jnp.logical_and(c == source_core, turn == r)
                    here = jnp.logical_and(holder == c, t == slots)

                    @pl.when(jnp.logical_and(mine, here))
                    def _():
                        copy = pltpu.make_async_copy(src, dst, local_sems.at[local_ids[part]])
                        if action == "start":
                            copy.start()
                        elif action == "wait":
                            copy.wait()

                    @pl.when(jnp.logical_and(mine, jnp.logical_not(here)))
                    def _():
                        copy = remote(
                            src, dst, at(d_holder, slots), send_base + k, idents[r][part]
                        )
                        if action == "start":
                            copy.start()
                        elif action == "wait":
                            copy.wait_send()

        def begin():
            each("start")

        def close():
            each("wait")
            for r in range(2):
                for part in range(3):
                    dst = target.at[r, pl.ds(64 * part, 64), :]
                    k = 3 * t + part
                    source_core = jnp.where(k < 4, 0, 1)
                    from_here = jnp.logical_and(
                        jnp.logical_and(source_core == c, turn == r), holder == c
                    )

                    @pl.when(jnp.logical_not(from_here))
                    def _():
                        arrive(dst, idents[r][part])

        return begin, close

    y_begin, y_close = return_row(y_out)
    y_begin()
    og_finish()

    def grad_view(g, shard, half, low, count):
        if g >= UP:
            rows = aligned(384 * half + 96 * low, 16)
            return wf.at[g - UP, shard, pl.ds(rows, 96 * count), :]
        rows = aligned(192 * shard + 48 * low, 16)
        if g == SELF:
            return wa.at[SELF, pl.ds(2 * half, 2), pl.ds(rows, 48 * count), :]
        return wa.at[CROSS, pl.ds(2 * c + half, 1), pl.ds(rows, 48 * count), :]

    def first_buffer(g, half, shard):
        if g >= UP:
            return r1f.at[g - UP, half, shard]
        if g == SELF:
            return gp.at[pl.ds(2 * half, 2), pl.ds(aligned(96 * shard, 16), 96), :]
        return ogrow.at[pl.ds(aligned(384 * half + 96 * shard, 16), 96), :]

    def second_buffer(g, half, shard):
        if g >= UP:
            return r2f.at[g - UP, half, shard]
        return (r2s if g == SELF else r2c).at[half, shard]

    def third_buffer(g, half, m):
        if g >= UP:
            return r3f.at[g - UP, m - 1, half]
        return (r3s if g == SELF else r3c).at[m - 1, half]

    def out_view(g, half, low, count, owner):
        if g >= UP:
            target = up_out if g == UP else down_out
            return target.at[owner, pl.ds(aligned(384 * half + 96 * low, 16), 96 * count), :]
        rows = pl.ds(aligned(48 * low, 16), 48 * count)
        if g == SELF:
            return self_out.at[owner, pl.ds(2 * half, 2), rows, :]
        return cross_out.at[pl.ds(2 * owner + half, 1), rows, :]

    def out_whole(g, owner):
        if g >= UP:
            return (up_out if g == UP else down_out).at[owner]
        if g == SELF:
            return self_out.at[owner]
        return cross_out.at[pl.ds(2 * owner, 2)]

    own_quarter = [2 * px + py, px + 2 * py]
    own_pair = [2 * px, 2 * py]
    far_pair = [2 * (1 - px), 2 * (1 - py)]
    far_quarter = [2 * px + (1 - py), (1 - px) + 2 * py]
    near_quarter = {
        "x": [2 * (1 - px) + py, (1 - px) + 2 * py],
        "y": [2 * px + (1 - py), px + 2 * (1 - py)],
    }
    opposite = [2 * (1 - px) + (1 - py), (1 - px) + 2 * (1 - py)]
    first_way = [d_x, d_y]
    second_way = [d_y, d_x]

    def fold(target, pieces):
        shape = target.shape
        if len(shape) == 3:
            for a in range(shape[0]):
                fold(target.at[a], [piece.at[a] for piece in pieces])
            return
        total = target[...].astype(F32)
        for piece in pieces:
            total = total + piece[...].astype(F32)
        target[...] = total.astype(BF16)

    class Sum:
        def __init__(self, g):
            self.g = g
            self.s1 = [[new_id() for _ in range(4)] for _ in range(2)]
            self.s2 = [[new_id() for _ in range(4)] for _ in range(2)]
            self.s3 = [[new_id() for _ in range(4)] for _ in range(2)]
            self.to_x = [new_id() for _ in range(2)]
            self.to_y = [new_id() for _ in range(2)]
            self.across = [new_id() for _ in range(2)]
            self.core = new_id()
            self.keep = [local_counter[0], local_counter[0] + 1]
            local_counter[0] += 2

        def buffer1(self, half, shard):
            ref = first_buffer(self.g, half, shard)
            return ref

        def start(self, half, shard):
            g = self.g
            src = grad_view(g, shard, half, far_pair[half], 2)
            if g == CROSS:
                src = wa.at[
                    CROSS, 2 * c + half, pl.ds(aligned(192 * shard + 48 * far_pair[half], 16), 96), :
                ]
            send(
                src,
                self.buffer1(half, shard),
                at(first_way[half], t),
                self.s1[half][shard],
            )

        def stage2(self, half):
            g = self.g
            for shard in range(4):
                buffer = self.buffer1(half, shard)
                arrive(buffer, self.s1[half][shard])
                target = grad_view(g, shard, half, own_pair[half], 2)
                if g == CROSS:
                    target = wa.at[
                        CROSS,
                        2 * c + half,
                        pl.ds(aligned(192 * shard + 48 * own_pair[half], 16), 96),
                        :,
                    ]
                fold(target, [buffer])
                send(
                    grad_view(g, shard, half, far_quarter[half], 1),
                    second_buffer(g, half, shard),
                    at(second_way[half], t),
                    self.s2[half][shard],
                )

        def stage3(self, half):
            g = self.g
            for shard in range(4):
                buffer = second_buffer(g, half, shard)
                arrive(buffer, self.s2[half][shard])
                fold(grad_view(g, shard, half, own_quarter[half], 1), [buffer])
            for m in range(1, 4):
                send(
                    grad_view(g, (t + m) % 4, half, own_quarter[half], 1),
                    third_buffer(g, half, m),
                    at(d, (t + m) % 4),
                    self.s3[half][m],
                )

        def stage4(self, half):
            g = self.g
            pieces = []
            for m in range(1, 4):
                buffer = third_buffer(g, half, m)
                arrive(buffer, self.s3[half][m])
                pieces.append(buffer)
            total = grad_view(g, t, half, own_quarter[half], 1)
            fold(total, pieces)
            spot = out_view(g, half, own_quarter[half], 1, c)
            copy = pltpu.make_async_copy(total, spot, local_sems.at[self.keep[half]])
            copy.start()
            self.copies = getattr(self, "copies", []) + [copy]
            send(total, spot, at(d_x, t), self.to_x[half])
            send(total, spot, at(d_y, t), self.to_y[half])

        def stage5(self):
            g = self.g
            for half, way, ids in ((0, "x", self.to_x), (1, "y", self.to_y)):
                for other in range(2):
                    arrive(out_view(g, other, near_quarter[way][other], 1, c), ids[other])
                piece = out_view(g, half, near_quarter[way][half], 1, c)
                send(piece, piece, at(d_y if way == "x" else d_x, t), self.across[half])

        def stage6(self):
            g = self.g
            for half in range(2):
                arrive(out_view(g, half, opposite[half], 1, c), self.across[half])
            for copy in self.copies:
                copy.wait()
            send(out_whole(g, c), out_whole(g, c), at(d_core, t), self.core)

        def stage7(self):
            arrive(out_whole(self.g, 1 - c), self.core)

        def after(self):
            return [
                lambda: self.stage2(0),
                lambda: self.stage2(1),
                lambda: self.stage3(0),
                lambda: self.stage3(1),
                lambda: self.stage4(0),
                lambda: self.stage4(1),
                self.stage5,
                self.stage6,
                self.stage7,
            ]

    sums = {g: Sum(g) for g in (DOWN, UP, SELF, CROSS)}
    down_after, up_after = sums[DOWN].after(), sums[UP].after()
    self_after, cross_after = sums[SELF].after(), sums[CROSS].after()

    def norm_back(upstream, index, slot, rows):
        normed = xh[slot, pl.ds(rows, BLOCK), :].astype(F32)
        nrm[pl.ds(index, 1), :] += jnp.sum(upstream * normed, axis=0, keepdims=True)
        nrm[pl.ds(index + 8, 1), :] += jnp.sum(upstream, axis=0, keepdims=True)
        scaled = upstream * gains[pl.ds(index, 1), :]
        grad = rstd[slot, pl.ds(rows, BLOCK), :] * (
            scaled
            - jnp.mean(scaled, axis=-1, keepdims=True)
            - normed * jnp.mean(scaled * normed, axis=-1, keepdims=True)
        )
        res[pl.ds(rows, BLOCK), :] = grad
        dzb[pl.ds(rows, BLOCK), :] = grad.astype(BF16)

    def out_back(i, rows):
        upstream = ogrow[pl.ds(aligned(own_base + rows, BLOCK), BLOCK), :].astype(F32)
        norm_back(upstream, 3 + c, 2, rows)

    blocks(out_back)
    og_close()
    for wait in pending:
        wait()
    pending.clear()
    for device in (d_x, d_y):
        pl.semaphore_signal(credit.at[0], inc=1, device_id=at(device, t), device_id_type=MESH)

    def down_back(shard):
        def block(i, rows):
            left = dzb[pl.ds(rows, BLOCK), :]
            for n in range(3):
                cols = slice(256 * n, 256 * n + 256)
                active_grad = dot_nt(left, wf[1, shard, cols, :])
                slope = gp[shard, pl.ds(rows, BLOCK), cols].astype(F32)
                gp[shard, pl.ds(rows, BLOCK), cols] = (active_grad * slope).astype(BF16)

        blocks(block)
        for n in range(3):
            cols = slice(256 * n, 256 * n + 256)
            left = jnp.transpose(act[shard, :, cols])
            for k in range(3):
                wide = slice(256 * k, 256 * k + 256)
                wf[1, shard, cols, wide] = dot_nn(left, dzb[:, wide]).astype(BF16)

    for shard in range(4):
        down_back(shard)
        for half in range(2):
            sums[DOWN].start(half, shard)

    def up_input(i, rows):
        for n in range(3):
            cols = slice(256 * n, 256 * n + 256)
            total = res[pl.ds(rows, BLOCK), cols]
            for shard in range(4):
                total = total + dot_nt(gp[shard, pl.ds(rows, BLOCK), :], wf[0, shard, cols, :])
            acc[pl.ds(rows, BLOCK), cols] = total

    blocks(up_input)
    tt[1] = jnp.transpose(sb[1])

    def up_weights(shard):
        for n in range(3):
            cols = slice(256 * n, 256 * n + 256)
            left = tt[1, cols, :]
            for k in range(3):
                wide = slice(256 * k, 256 * k + 256)
                wf[0, shard, cols, wide] = dot_nn(left, gp[shard, :, wide]).astype(BF16)

    for shard in range(4):
        up_weights(shard)
        for half in range(2):
            sums[UP].start(half, shard)
    for device in (d_x, d_y):
        pl.semaphore_signal(credit.at[1], inc=1, device_id=at(device, t), device_id_type=MESH)

    blocks(lambda i, rows: norm_back(acc[pl.ds(rows, BLOCK), :], 1 + c, 1, rows))

    dctx = act.at[0]

    def context_back(which):
        def block(i, rows):
            left = dzb[pl.ds(rows, BLOCK), :]
            for n in range(3):
                cols = slice(256 * n, 256 * n + 256)
                dctx[pl.ds(rows, BLOCK), cols] = dot_nt(left, wa[which, 3, cols, :]).astype(BF16)

        blocks(block)

    def weight_rows(which, member, left_ref, rights):
        def tile(n):
            rows = aligned(n * 256, 256)
            for k in range(3):
                wide = slice(256 * k, 256 * k + 256)
                total = None
                for low, size, ref in rights:
                    term = dot_nn(
                        left_ref[pl.ds(rows, 256), low : low + size], ref[:, wide]
                    )
                    total = term if total is None else total + term
                wa[which, member, pl.ds(rows, 256), wide] = total.astype(BF16)

        times(3, tile)

    def attend_back(which, qkv, code_row, pairs):
        def pair(k, carry):
            lanes = pl.ds(aligned(k * 128, 128), 128)
            key = qkv[1, :, lanes]
            value = qkv[2, :, lanes]
            key_t = jnp.transpose(key)
            kv_acc[...] = jnp.zeros_like(kv_acc)

            def block(i, rows):
                query = qkv[0, pl.ds(rows, BLOCK), lanes] * jnp.asarray(scaling, BF16)
                grad = dctx[pl.ds(rows, BLOCK), lanes]
                query_code = codes[
                    pl.ds(code_row, 1), pl.ds(aligned(own_base + rows, BLOCK), BLOCK)
                ]
                allowed = kcode[which, :, 0:1] == query_code
                for h in range(2):
                    query_h = query * head_lanes[h]
                    grad_h = grad * head_lanes[h]
                    scores = jnp.where(allowed, dot_nt(key, query_h), -1e30)
                    probs = jnp.exp(
                        scores - lse[which, pl.ds(2 * k + h, 1), pl.ds(rows, BLOCK)]
                    )
                    probs_grad = dot_nt(value, grad_h)
                    delta = jnp.sum(probs * probs_grad, axis=0, keepdims=True)
                    score_grad = (probs * (probs_grad - delta)).astype(BF16)
                    kv_acc[0] += dot_nn(score_grad, query_h)
                    kv_acc[1] += dot_nn(probs.astype(BF16), grad_h)
                    tt[
                        0, pl.ds(aligned(k * 128 + h * 64, 64), 64), pl.ds(rows, BLOCK)
                    ] = (dot_nn(key_t[64 * h : 64 * h + 64, :], score_grad) * scaling).astype(BF16)

            blocks(block)
            for m in range(2):
                tt[1 + m, pl.ds(aligned(k * 128, 128), 128), :] = jnp.transpose(
                    kv_acc[m]
                ).astype(BF16)
            return carry

        lax.fori_loop(pairs[0], pairs[1], pair, 0)

    queue = []

    def pump(count):
        for _ in range(count):
            if queue:
                queue.pop(0)()

    context_back(SELF)
    weight_rows(SELF, 3, ctx_t.at[1], [(0, 512, dzb)])
    queue += down_after[:2]
    attend_back(1, qkv2, 2, (0, 3))
    pump(2)
    queue += up_after[:2]
    attend_back(1, qkv2, 2, (3, 6))
    pump(2)
    queue += down_after[2:4]

    def self_input(i, rows):
        parts = [jnp.transpose(tt[m, :, pl.ds(rows, BLOCK)]) for m in range(3)]
        for n in range(3):
            cols = slice(256 * n, 256 * n + 256)
            total = res[pl.ds(rows, BLOCK), cols]
            for m in range(3):
                total = total + dot_nn(parts[m], wa[SELF, m, :, cols])
            acc[pl.ds(rows, BLOCK), cols] = total

    blocks(self_input)
    for m in range(3):
        weight_rows(SELF, m, tt.at[m], [(0, 512, sb.at[0])])
    pl.semaphore_wait(credit.at[1], 2)
    for half in range(2):
        for shard in range(4):
            sums[SELF].start(half, shard)
    pl.semaphore_signal(credit.at[2], inc=1, device_id=at(d_core, t), device_id_type=MESH)
    pump(2)
    queue += up_after[2:4] + down_after[4:6]

    blocks(lambda i, rows: norm_back(acc[pl.ds(rows, BLOCK), :], 0, 0, rows))

    norm_ids = [new_id() for _ in range(5)]
    norm_ways = [
        at(d_core, t),
        at(d_x, t),
        at(d_y, t),
        at(d, t + 1 - 2 * (t % 2)),
        at(d, (t + 2) % 4),
    ]
    norm_steps = []

    def norm_begin(k):
        send(nrm if k == 0 else nrm_recv.at[k - 1, 1], nrm_recv.at[k, 0], norm_ways[k], norm_ids[k])

    def norm_step(k):
        arrive(nrm_recv.at[k, 0], norm_ids[k])
        mine = nrm[...] if k == 0 else nrm_recv[k - 1, 1]
        total = mine + nrm_recv[k, 0]
        if k < 4:
            nrm_recv[k, 1] = total
            norm_begin(k + 1)
        else:
            norm_out[...] = total

    norm_begin(0)
    context_back(CROSS)
    weight_rows(CROSS, 3, ctx_t.at[0], [(0, 512, dzb)])
    norm_step(0)
    pump(2)
    attend_back(0, qkv1, 0, (0, 3))
    norm_step(1)
    pump(2)
    queue += self_after[:2]
    attend_back(0, qkv1, 0, (3, 6))
    norm_step(2)
    pump(2)
    queue += up_after[4:6] + down_after[6:7]

    key_ids = [new_id() for _ in range(2)]

    def key_input(j):
        parts = [jnp.transpose(tt[m, :, 256 * j : 256 * j + 256]) for m in (1, 2)]
        for n in range(3):
            cols = slice(256 * n, 256 * n + 256)
            act[1, 256 * j : 256 * j + 256, cols] = (
                dot_nn(parts[0], wa[CROSS, 1, :, cols]) + dot_nn(parts[1], wa[CROSS, 2, :, cols])
            ).astype(BF16)

    key_input(0)
    key_input(1)
    key_copies = [
        remote(
            act.at[1, pl.ds(256 * j, 256), :],
            dhk_recv.at[j],
            at(d_core, t),
            key_ids[j],
        )
        for j in range(2)
    ]
    key_copies[0].start()

    @pl.when(c == 0)
    def _():
        key_copies[1].start()

    def cross_input(i, rows):
        part = jnp.transpose(tt[0, :, pl.ds(rows, BLOCK)])
        for n in range(3):
            cols = slice(256 * n, 256 * n + 256)
            res[pl.ds(rows, BLOCK), cols] += dot_nn(part, wa[CROSS, 0, :, cols])

    blocks(cross_input)
    weight_rows(CROSS, 0, tt.at[0], [(0, 512, xrow.at[pl.ds(own_base, 512), :])])
    for m in range(1, 3):
        weight_rows(
            CROSS,
            m,
            tt.at[m],
            [
                (0, 256, xrow.at[pl.ds(other_base, 256), :]),
                (256, 256, xrow.at[pl.ds(512, 256), :]),
            ],
        )

    pl.semaphore_wait(credit.at[2], 1)
    core_sums = [(a, n, new_id()) for a in range(2) for n in range(3)]

    def core_slot(a, n):
        k = 3 * a + n
        return qkv2.at[k // 2, pl.ds(256 * (k % 2), 256), :]

    for a, n, ident in core_sums:
        send(
            wa.at[CROSS, 2 * (1 - c) + a, pl.ds(256 * n, 256), :],
            core_slot(a, n),
            at(d_core, t),
            ident,
        )
    norm_step(3)

    y_close()
    arrive(dhk_recv.at[0], key_ids[0])

    @pl.when(c == 1)
    def _():
        arrive(dhk_recv.at[1], key_ids[1])

    yb[:BLOCK, :] = (res[:BLOCK, :] + dhk_recv[0].astype(F32)).astype(BF16)

    @pl.when(c == 1)
    def _():
        own_part = act[1, BLOCK:, :].astype(F32)
        yb[BLOCK:, :] = (res[BLOCK:, :] + dhk_recv[1].astype(F32) + own_part).astype(BF16)

    dx_begin, dx_close = return_row(dx_out)
    dx_begin()

    for a, n, ident in core_sums:
        arrive(core_slot(a, n), ident)
        fold(wa.at[CROSS, 2 * c + a, pl.ds(256 * n, 256), :], [core_slot(a, n)])
    pl.semaphore_wait(credit.at[0], 2)
    for half in range(2):
        for shard in range(4):
            sums[CROSS].start(half, shard)
    norm_step(4)
    tail = {DOWN: down_after, UP: up_after, SELF: self_after, CROSS: cross_after}
    queue += tail[SELF][2:4] + tail[UP][6:7] + tail[DOWN][7:8] + tail[SELF][4:6]
    queue += tail[CROSS][:4] + tail[UP][7:8] + tail[SELF][6:7] + tail[CROSS][4:6]
    queue += tail[SELF][7:8] + tail[CROSS][6:8]
    queue += [tail[g][8] for g in (DOWN, UP, SELF, CROSS)]
    pump(len(queue))
    for wait in pending:
        wait()
    key_copies[0].wait_send()

    @pl.when(c == 0)
    def _():
        key_copies[1].wait_send()

    dx_close()
    if counter[0] > SEMAPHORES or local_counter[0] > LOCALS:
        raise ValueError((counter[0], local_counter[0]))


SEMAPHORES = 320
LOCALS = 40


def call_layer(*operands):
    def vmem(shape, dtype=BF16):
        return pltpu.VMEM(shape, dtype)

    anywhere = pl.BlockSpec(memory_space=pl.ANY)
    whole = pl.BlockSpec(memory_space=pltpu.VMEM)
    x_in = operands[0]
    return pl.pallas_call(
        layer_kernel,
        name="cross_modality_layer",
        out_shape=(
            jax.ShapeDtypeStruct(x_in.shape, BF16),
            jax.ShapeDtypeStruct(x_in.shape, BF16),
            jax.ShapeDtypeStruct((4, 192, 768), BF16),
            jax.ShapeDtypeStruct((2, 4, 192, 768), BF16),
            jax.ShapeDtypeStruct((2, 768, 768), BF16),
            jax.ShapeDtypeStruct((2, 768, 768), BF16),
            jax.ShapeDtypeStruct((16, 768), F32),
        ),
        in_specs=[anywhere] * 7 + [whole] * 2,
        out_specs=(anywhere,) * 6 + (whole,),
        scratch_shapes=[
            vmem((2, 4, 768, 768)),
            vmem((2, 4, 768, 768)),
            vmem((768, 768)),
            vmem((768, 768)),
            vmem((8, 768), F32),
            vmem((2, 512, 128), F32),
            vmem((3, 512, 768)),
            vmem((3, 512, 768)),
            vmem((2, 768, 512)),
            vmem((2, 16, 512), F32),
            vmem((3, 512, 768)),
            vmem((3, 512, 1), F32),
            vmem((2, 512, 768)),
            vmem((512, 768), F32),
            vmem((512, 768), F32),
            vmem((4, 512, 768)),
            vmem((4, 512, 768)),
            vmem((512, 768)),
            vmem((3, 768, 512)),
            vmem((512, 768)),
            vmem((2, 256, 768)),
            vmem((2, 512, 128), F32),
            vmem((16, 768), F32),
            vmem((5, 2, 16, 768), F32),
            vmem((2, 2, 4, 192, 768)),
            vmem((2, 2, 4, 96, 768)),
            vmem((2, 3, 2, 96, 768)),
            vmem((2, 4, 2, 48, 768)),
            vmem((3, 2, 2, 48, 768)),
            vmem((2, 4, 1, 48, 768)),
            vmem((3, 2, 1, 48, 768)),
            pltpu.SemaphoreType.DMA((SEMAPHORES,)),
            pltpu.SemaphoreType.DMA((SEMAPHORES,)),
            pltpu.SemaphoreType.DMA((LOCALS,)),
            pltpu.SemaphoreType.REGULAR((3,)),
        ],
        compiler_params=pltpu.CompilerParams(
            collective_id=0, has_side_effects=True, vmem_limit_bytes=64 * 1024 * 1024 - 512 * 1024
        ),
    )(*operands)


def solution(mesh):
    extra = []
    step = 8
    while step < mesh.shape["dp"]:
        extra.append(step)
        step *= 2

    def total(array):
        for step in extra:
            pairs = [(k, k ^ step) for k in range(mesh.shape["dp"])]
            array = array + lax.ppermute(array, "dp", pairs)
        return array

    def body(
        layer_input,
        word_segments,
        image_order,
        cross_qkv,
        cross_out,
        self_qkv,
        self_out,
        ffn_up,
        ffn_down,
        norm_gains,
        norm_biases,
        out_grad,
    ):
        rows = layer_input.shape[0]
        images = jnp.repeat(image_order, BOXES, axis=1)
        pads = jnp.full((rows, PADS), CAPTIONS, jnp.int32)
        none = jnp.full((rows, WORDS + REGIONS + PADS), -1, jnp.int32)
        groups = jnp.concatenate([word_segments, images, pads], axis=1)
        keys = jnp.concatenate([word_segments, none[:, :REGIONS], pads], axis=1)
        kinds = jnp.concatenate([word_segments, images + 16, pads + 32], axis=1)
        codes = jnp.stack([groups, keys, kinds, none, none, none, none, none], axis=1).astype(F32)
        cross = jnp.concatenate([jnp.swapaxes(cross_qkv, 1, 2), cross_out[None]], axis=0)
        own = jnp.concatenate([jnp.swapaxes(self_qkv, 2, 3), self_out[:, None]], axis=1)
        y, dx, d_cross, d_self, d_up, d_down, d_norm = call_layer(
            layer_input,
            out_grad,
            codes,
            cross,
            own,
            ffn_up,
            ffn_down,
            norm_gains,
            norm_biases,
        )
        d_cross, d_self, d_up, d_down = [
            total(array.astype(F32)) for array in (d_cross, d_self, d_up, d_down)
        ]
        d_norm = total(d_norm)
        return (
            y,
            dx.astype(F32),
            jnp.swapaxes(d_cross[:3], 1, 2),
            d_cross[3],
            jnp.swapaxes(d_self[:, :3], 2, 3),
            d_self[:, 3],
            d_up,
            d_down,
            d_norm[0:5],
            d_norm[8:13],
        )

    in_specs = (
        P("dp", "tensor", None),
        P("dp", None),
        P("dp", None),
        P(None, None, "tensor"),
        P("tensor", None),
        P(None, None, None, "tensor"),
        P(None, "tensor", None),
        P(None, None, "tensor"),
        P(None, "tensor", None),
        P(),
        P(),
        P("dp", "tensor", None),
    )
    out_specs = (
        P("dp", "tensor", None),
        P("dp", "tensor", None),
        P(None, None, "tensor"),
        P("tensor", None),
        P(None, None, None, "tensor"),
        P(None, "tensor", None),
        P(None, None, "tensor"),
        P(None, "tensor", None),
        P(),
        P(),
    )
    return jax.shard_map(body, mesh=mesh, in_specs=in_specs, out_specs=out_specs, check_vma=False)
```

```python
import functools

import jax
import jax.numpy as jnp
from jax import lax
from jax.experimental import pallas as pl
from jax.experimental.pallas import tpu as pltpu
from jax.sharding import PartitionSpec as P

HEAD_DIM = 64
WORDS = 256
CAPTIONS = 14
BOXES = 36
REGIONS = 504
PADS = 8
NORM_EPSILON = 1e-12
BLOCK = 256
BF16 = jnp.bfloat16
F32 = jnp.float32
MESH = pl.DeviceIdType.MESH
CROSS, SELF, UP, DOWN = 0, 1, 2, 3


def dot_nn(left, right):
    return jnp.dot(left, right, preferred_element_type=F32)


def dot_nt(left, right):
    return lax.dot_general(left, right, (((1,), (1,)), ((), ())), preferred_element_type=F32)


def aligned(value, step):
    return pl.multiple_of(value, step)


def layer_kernel(
    x_in,
    og_in,
    codes_in,
    cross_in,
    self_in,
    up_in,
    down_in,
    gains,
    biases,
    y_out,
    dx_out,
    cross_out,
    self_out,
    up_out,
    down_out,
    norm_out,
    wa,
    wf,
    xrow,
    ogrow,
    codes,
    kcode,
    qkv1,
    qkv2,
    ctx_t,
    lse,
    xh,
    rstd,
    sb,
    res,
    acc,
    act,
    gp,
    dzb,
    tt,
    yb,
    dhk_recv,
    kv_acc,
    nrm,
    nrm_recv,
    s2all,
    zall,
    qacc,
    rq,
    r2s,
    r3s,
    r2c,
    r3c,
    send_sems,
    recv_sems,
    local_sems,
    credit,
):
    d = lax.axis_index("dp")
    t = lax.axis_index("tensor")
    c = d % 2
    px = (d // 2) % 2
    py = (d // 4) % 2
    q = px + 2 * py
    d_core = d + 1 - 2 * c
    d_x = d + 2 - 4 * px
    d_y = d + 4 - 8 * py
    holder = t // 2
    d_holder = d - c + holder
    turn = t % 2
    nb = 1 + c
    near = {"x": d_x, "y": d_y, "core": d_core}

    def at(dp_index, tensor_index):
        return {"dp": dp_index, "tensor": tensor_index}

    counter = [0]
    local_counter = [0]
    pending = []

    def new_id(count=1):
        counter[0] += count
        return counter[0] - count

    def remote(src, dst, device, ident, arrival=None):
        return pltpu.make_async_remote_copy(
            src_ref=src,
            dst_ref=dst,
            send_sem=send_sems.at[ident],
            recv_sem=recv_sems.at[ident if arrival is None else arrival],
            device_id=device,
            device_id_type=MESH,
        )

    def send(src, dst, device, ident):
        copy = remote(src, dst, device, ident)
        copy.start()
        pending.append(copy.wait_send)

    def arrive(dst, ident):
        remote(dst, dst, at(d_core, t), ident).wait_recv()

    def local(src, dst):
        copy = pltpu.make_async_copy(src, dst, local_sems.at[local_counter[0]])
        local_counter[0] += 1
        return copy

    def blocks(body):
        def step(i, carry):
            body(i, aligned(i * BLOCK, BLOCK))
            return carry

        lax.fori_loop(0, nb, step, 0)

    def times(count, body):
        def step(i, carry):
            body(i)
            return carry

        lax.fori_loop(0, count, step, 0)

    barrier = pltpu.get_barrier_semaphore()
    partners = [at(d_core, t), at(d_x, t), at(d_y, t)]
    for m in range(1, 4):
        partners.append(at(d, (t + m) % 4))
        partners.append(at(d_core, (t + m) % 4))
    for partner in partners:
        pl.semaphore_signal(barrier, inc=1, device_id=partner, device_id_type=MESH)

    half_rows = aligned(t * 192, 16)
    own_copies = [
        local(cross_in, wa.at[CROSS, :, pl.ds(half_rows, 192), :]),
        local(self_in.at[c], wa.at[SELF, :, pl.ds(half_rows, 192), :]),
        local(down_in.at[c], wf.at[1, t]),
    ]
    up_copies = [
        local(up_in.at[c, pl.ds(0, 512), :], qkv1.at[0]),
        local(up_in.at[c, pl.ds(512, 256), :], qkv1.at[1, pl.ds(0, 256), :]),
    ]
    for copy in own_copies + up_copies:
        copy.start()

    zero_half = jnp.zeros((BLOCK, 768), BF16)

    @pl.when(c == 0)
    def _():
        for ref in (qkv2.at[1], qkv2.at[2], sb, dzb):
            ref[BLOCK:, :] = zero_half
        for k in range(2):
            ctx_t[k, :, BLOCK:] = jnp.zeros((768, BLOCK), BF16)
        tt[0, :, BLOCK:] = jnp.zeros((768, BLOCK), BF16)

    nrm[...] = jnp.zeros_like(nrm)
    pl.semaphore_wait(barrier, len(partners))

    def spread_row(source, row):
        base = new_id(4)
        core_base = new_id(4)
        own = local(source.at[turn], row.at[pl.ds(half_rows, 192), :])

        def each_target(action):
            for r in range(2):
                target = 2 * c + r

                @pl.when(target != t)
                def _():
                    action(
                        remote(
                            source.at[r],
                            row.at[pl.ds(half_rows, 192), :],
                            at(d, target),
                            base + r,
                            base + t,
                        )
                    )

        def each_relay(action):
            @pl.when(holder == c)
            def _():
                for s in range(4):
                    part = row.at[pl.ds(192 * s, 192), :]
                    action(s, part, remote(part, part, at(d_core, t), core_base + s))

        def begin():
            each_target(lambda copy: copy.start())

            @pl.when(holder == c)
            def _():
                own.start()

        def relay():
            def action(s, part, copy):
                @pl.when(t == s)
                def _():
                    own.wait()

                @pl.when(t != s)
                def _():
                    arrive(part, base + s)

                copy.start()

            each_relay(action)

        def finish():
            @pl.when(holder != c)
            def _():
                for s in range(4):
                    arrive(row.at[pl.ds(192 * s, 192), :], core_base + s)

        def close():
            each_target(lambda copy: copy.wait_send())
            each_relay(lambda s, part, copy: copy.wait_send())

        return begin, relay, finish, close

    x_begin, x_relay, x_finish, x_close = spread_row(x_in, xrow)
    og_begin, og_relay, og_finish, og_close = spread_row(og_in, ogrow)
    pending.append(x_close)

    code_ident = new_id()
    code_own = local(codes_in.at[turn], codes)

    @pl.when(holder == c)
    def _():
        code_own.start()
        remote(codes_in.at[turn], codes, at(d_core, t), code_ident).start()

    def share(g, shard, quarter, low, high):
        if g >= UP:
            rows = aligned(quarter * 192 + low * 96, 16)
            return wf.at[g - UP, shard, pl.ds(rows, (high - low) * 96), :]
        rows = aligned(shard * 192 + quarter * 48, 16)
        if g == SELF:
            return wa.at[SELF, pl.ds(2 * low, 2 * (high - low)), pl.ds(rows, 48), :]
        return wa.at[CROSS, pl.ds(2 * c + low, high - low), pl.ds(rows, 48), :]

    def own_share(g):
        if g >= UP:
            rows = pl.ds(aligned(q * 192, 16), 192)
            return wf.at[0, t, rows, :] if g == UP else down_in.at[c, rows, :]
        rows = pl.ds(aligned(q * 48, 16), 48)
        if g == SELF:
            return self_in.at[c, :, rows, :]
        return cross_in.at[pl.ds(2 * c, 2), rows, :]

    qx, qy = (1 - px) + 2 * py, px + 2 * (1 - py)
    qd = (1 - px) + 2 * (1 - py)
    items = [(g, m) for g in (CROSS, SELF, UP, DOWN) for m in range(1, 4)]
    z_base = {g: new_id(4) for g in (CROSS, SELF, UP, DOWN)}
    own_ids = {g: new_id(2) for g in (CROSS, SELF, UP, DOWN)}
    pass_ids = {item: new_id() for item in items}
    x_ids = {item: new_id() for item in items}
    y_ids = {item: new_id() for item in items}
    fx_ids = {item: new_id() for item in items}
    fy_ids = {item: new_id() for item in items}
    core_ids = {m: new_id() for m in range(1, 4)}
    arrivals = {
        1: t + 1 - 2 * (t % 2),
        2: 2 - t // 2,
        3: 3 - 3 * (t // 2),
    }

    def z_way(g, way):
        exists = t > 0 if way == 0 else t < 3
        target = t - 1 + 2 * way

        def copy():
            return remote(
                own_share(g),
                share(g, t, q, 0, 2),
                at(d, target),
                own_ids[g] + way,
                z_base[g] + t,
            )

        @pl.when(exists)
        def _():
            copy().start()

        def close():
            @pl.when(exists)
            def _():
                copy().wait_send()

        pending.append(close)

    def z_own(g):
        for way in range(2):
            z_way(g, way)

    def first(item):
        g, m = item
        shard = arrivals[m]
        piece = share(g, shard, q, 0, 2)
        arrive(piece, z_base[g] + shard)
        inner = jnp.logical_and(t > 0, t < 3)
        target = jnp.where(shard < t, t + 1, t - 1)

        def copy():
            return remote(piece, piece, at(d, target), pass_ids[item], z_base[g] + shard)

        @pl.when(inner)
        def _():
            copy().start()

        def close():
            @pl.when(inner)
            def _():
                copy().wait_send()

        pending.append(close)
        send(piece, piece, at(d_x, t), x_ids[item])
        send(piece, piece, at(d_y, t), y_ids[item])
        if m == 1 and g < DOWN:
            z_own(g + 1)
        if g == CROSS and m == 1:
            x_begin()
        if item == (DOWN, 1):
            og_begin()

    def second(item):
        g, m = item
        shard = arrivals[m]
        arrive(share(g, shard, qx, 0, 2), x_ids[item])
        low = share(g, shard, qx, 0, 1)
        send(low, low, at(d_y, t), fy_ids[item])
        arrive(share(g, shard, qy, 0, 2), y_ids[item])
        high = share(g, shard, qy, 1, 2)
        send(high, high, at(d_x, t), fx_ids[item])

    def third(item):
        g, m = item
        shard = arrivals[m]
        arrive(share(g, shard, qd, 0, 1), fy_ids[item])
        arrive(share(g, shard, qd, 1, 2), fx_ids[item])
        if g == CROSS:
            rows = pl.ds(aligned(shard * 192, 16), 192)
            whole = wa.at[CROSS, pl.ds(2 * c, 2), rows, :]
            send(whole, whole, at(d_core, t), core_ids[m])

    def last(m):
        shard = arrivals[m]
        rows = pl.ds(aligned(shard * 192, 16), 192)
        arrive(wa.at[CROSS, pl.ds(2 * (1 - c), 2), rows, :], core_ids[m])

    z_own(CROSS)
    for copy in up_copies:
        copy.wait()
    wf[0, t, :, 0:512] = jnp.transpose(qkv1[0])
    wf[0, t, :, 512:768] = jnp.transpose(qkv1[1, 0:256, :])

    steps = []
    position = {}
    for k in range(len(items) + 2):
        if k < len(items):
            steps.append(functools.partial(first, items[k]))
        if 0 <= k - 1 < len(items):
            steps.append(functools.partial(second, items[k - 1]))
        if 0 <= k - 2 < len(items):
            steps.append(functools.partial(third, items[k - 2]))
            position[items[k - 2]] = len(steps)
    done = [0]

    def advance(upto):
        while done[0] < min(upto, len(steps)):
            steps[done[0]]()
            done[0] += 1

    advance(position[(CROSS, 2)])
    x_relay()
    x_finish()

    @pl.when(holder == c)
    def _():
        code_own.wait()
        remote(codes_in.at[turn], codes, at(d_core, t), code_ident).wait_send()

    @pl.when(holder != c)
    def _():
        arrive(codes, code_ident)

    def as_column(row):
        return jnp.transpose(jnp.broadcast_to(row, (128, BLOCK)))

    own_base = aligned(c * BLOCK, BLOCK)
    other_base = aligned((1 - c) * BLOCK, BLOCK)
    kcode[0, :BLOCK, :] = as_column(codes[0:1, pl.ds(other_base, BLOCK)])
    kcode[0, BLOCK:, :] = as_column(codes[pl.ds(c, 1), 512:768])
    kcode[1, :BLOCK, :] = as_column(codes[2:3, pl.ds(own_base, BLOCK)])
    kcode[1, BLOCK:, :] = as_column(codes[pl.ds(3 - c, 1), 512:768])

    lane = lax.broadcasted_iota(jnp.int32, (1, 128), 1)
    head_lanes = [
        (lane < HEAD_DIM).astype(F32).astype(BF16),
        (lane >= HEAD_DIM).astype(F32).astype(BF16),
    ]
    scaling = HEAD_DIM ** (-0.5)

    def project(source, base, weight, target, rows):
        left = source[pl.ds(base, BLOCK), :]
        for n in range(3):
            target[pl.ds(rows, BLOCK), 256 * n : 256 * n + 256] = dot_nt(
                left, weight[256 * n : 256 * n + 256, :]
            ).astype(BF16)

    def attend(which, qkv, code_row, pairs):
        def pair(k):
            lanes = pl.ds(aligned(k * 128, 128), 128)
            key = qkv[1, :, lanes]
            value_t = jnp.transpose(qkv[2, :, lanes])

            def block(i, rows):
                query = qkv[0, pl.ds(rows, BLOCK), lanes] * jnp.asarray(scaling, BF16)
                query_code = codes[
                    pl.ds(code_row, 1), pl.ds(aligned(own_base + rows, BLOCK), BLOCK)
                ]
                allowed = kcode[which, :, 0:1] == query_code
                for h in range(2):
                    scores = dot_nt(key, query * head_lanes[h])
                    scores = jnp.where(allowed, scores, -1e30)
                    top = jnp.max(scores, axis=0, keepdims=True)
                    exponent = jnp.exp(scores - top)
                    total = jnp.sum(exponent, axis=0, keepdims=True)
                    probs = (exponent * (1.0 / total)).astype(BF16)
                    lse[which, pl.ds(2 * k + h, 1), pl.ds(rows, BLOCK)] = top + jnp.log(total)
                    ctx_t[
                        which,
                        pl.ds(aligned(k * 128 + h * 64, 64), 64),
                        pl.ds(rows, BLOCK),
                    ] = dot_nn(value_t[64 * h : 64 * h + 64, :], probs).astype(BF16)

            blocks(block)

        def run(k, carry):
            pair(k)
            return carry

        lax.fori_loop(pairs[0], pairs[1], run, 0)

    def normalize(summed, index, slot, rows):
        center = summed - jnp.mean(summed, axis=-1, keepdims=True)
        inverse = lax.rsqrt(jnp.mean(center * center, axis=-1, keepdims=True) + NORM_EPSILON)
        normed = center * inverse
        xh[slot, pl.ds(rows, BLOCK), :] = normed.astype(BF16)
        rstd[slot, pl.ds(rows, BLOCK), :] = inverse
        return normed * gains[pl.ds(index, 1), :] + biases[pl.ds(index, 1), :]

    def attention_out(which, rows):
        context = jnp.transpose(ctx_t[which, :, pl.ds(rows, BLOCK)])
        return dot_nn(context, wa[which, 3])

    for copy in own_copies[:1]:
        copy.wait()
    advance(position[(CROSS, 3)])
    for m in range(1, 4):
        last(m)
    blocks(lambda i, rows: project(xrow, own_base + rows, wa.at[CROSS, 0], qkv1.at[0], rows))
    for k in range(1, 3):
        project(xrow, other_base, wa.at[CROSS, k], qkv1.at[k], 0)
        project(xrow, 512, wa.at[CROSS, k], qkv1.at[k], BLOCK)
    attend(0, qkv1, 0, (0, 3))
    advance(position[(SELF, 1)])
    attend(0, qkv1, 0, (3, 6))
    advance(position[(SELF, 2)])

    def cross_end(i, rows):
        stream = xrow[pl.ds(aligned(own_base + rows, BLOCK), BLOCK), :].astype(F32)
        section = normalize(stream + attention_out(0, rows), 0, 0, rows)
        res[pl.ds(rows, BLOCK), :] = section
        sb[pl.ds(rows, BLOCK), :] = section.astype(BF16)

    blocks(cross_end)

    own_copies[1].wait()
    advance(position[(SELF, 3)])
    for k in range(3):
        blocks(lambda i, rows: project(sb, rows, wa.at[SELF, k], qkv2.at[k], rows))
    attend(1, qkv2, 2, (0, 3))
    advance(position[(UP, 1)])
    attend(1, qkv2, 2, (3, 6))
    advance(position[(UP, 2)])

    def self_end(i, rows):
        summed = res[pl.ds(rows, BLOCK), :] + attention_out(1, rows)
        section = normalize(summed, 1 + c, 1, rows)
        res[pl.ds(rows, BLOCK), :] = section
        s2all[0, pl.ds(rows, BLOCK), :] = section.astype(BF16)

    blocks(self_end)

    late = []

    def plane_gather(buffer):
        to_x, to_y, from_x, from_y = new_id(), new_id(), new_id(), new_id()

        def sized(action):
            for core in range(2):

                @pl.when(c == core)
                def _():
                    action(BLOCK * (core + 1))

        def part(k, low, size):
            return buffer.at[k, pl.ds(low, size), :]

        def firsts(size):
            return [
                remote(part(0, 0, size), part(1, 0, size), at(d_x, t), to_x),
                remote(part(0, 0, size), part(2, 0, size), at(d_y, t), to_y),
            ]

        def seconds(size):
            half = size // 2
            return [
                remote(part(1, 0, half), part(3, 0, half), at(d_y, t), from_x),
                remote(part(2, half, half), part(3, half, half), at(d_x, t), from_y),
            ]

        def begin():
            sized(lambda size: [copy.start() for copy in firsts(size)])

        def relay():
            def action(size):
                onward = seconds(size)
                arrive(part(1, 0, size), to_x)
                onward[0].start()
                arrive(part(2, 0, size), to_y)
                onward[1].start()

            sized(action)

        def finish():
            def action(size):
                half = size // 2
                arrive(part(3, 0, half), from_x)
                arrive(part(3, half, half), from_y)

            sized(action)

        def close():
            sized(lambda size: [copy.wait_send() for copy in firsts(size) + seconds(size)])

        late.append(close)
        return begin, relay, finish

    s2_begin, s2_relay, s2_finish = plane_gather(s2all)
    z3_begin, z3_relay, z3_finish = plane_gather(zall)
    def feed_up(shard):
        def block(i, rows):
            left = s2all[0, pl.ds(rows, BLOCK), :]
            for n in range(3):
                cols = slice(256 * n, 256 * n + 256)
                upward = dot_nt(left, wf[0, shard, cols, :])
                cumulative = 0.5 * (1.0 + lax.erf(upward * (0.5**0.5)))
                density = jnp.exp(-0.5 * upward * upward) * 0.3989422804014327
                act[shard, pl.ds(rows, BLOCK), cols] = (upward * cumulative).astype(BF16)
                gp[shard, pl.ds(rows, BLOCK), cols] = (cumulative + upward * density).astype(BF16)

        blocks(block)

    feed_up(t)
    for m in range(1, 4):
        advance(position[(UP, m)])
        feed_up(arrivals[m])

    def feed_down(shard):
        def block(i, rows):
            left = act[shard, pl.ds(rows, BLOCK), :]
            for n in range(3):
                cols = slice(256 * n, 256 * n + 256)
                res[pl.ds(rows, BLOCK), cols] += dot_nn(left, wf[1, shard, :, cols])

        blocks(block)

    own_copies[2].wait()
    feed_down(t)
    for m in range(1, 4):
        advance(position[(DOWN, m)])
        if m == 3:
            s2_begin()
            og_relay()
        feed_down(arrivals[m])

    def layer_end(i, rows):
        result = normalize(res[pl.ds(rows, BLOCK), :], 3 + c, 2, rows)
        yb[pl.ds(rows, BLOCK), :] = result.astype(BF16)

    blocks(layer_end)

    def return_row(target):
        idents = [[new_id() for _ in range(3)] for _ in range(2)]
        send_base = new_id(12)
        local_ids = [local_counter[0] + k for k in range(3)]
        local_counter[0] += 3

        def each(action):
            for k in range(12):
                source_core = 0 if k < 4 else 1
                slots, part = k // 3, k % 3
                src = yb.at[pl.ds(64 * k - 256 * source_core, 64), :]
                for r in range(2):
                    dst = target.at[r, pl.ds(64 * part, 64), :]
                    mine = jnp.logical_and(c == source_core, turn == r)
                    here = jnp.logical_and(holder == c, t == slots)

                    @pl.when(jnp.logical_and(mine, here))
                    def _():
                        copy = pltpu.make_async_copy(src, dst, local_sems.at[local_ids[part]])
                        if action == "start":
                            copy.start()
                        elif action == "wait":
                            copy.wait()

                    @pl.when(jnp.logical_and(mine, jnp.logical_not(here)))
                    def _():
                        copy = remote(
                            src, dst, at(d_holder, slots), send_base + k, idents[r][part]
                        )
                        if action == "start":
                            copy.start()
                        elif action == "wait":
                            copy.wait_send()

        def begin():
            each("start")

        def close():
            each("wait")
            for r in range(2):
                for part in range(3):
                    dst = target.at[r, pl.ds(64 * part, 64), :]
                    k = 3 * t + part
                    source_core = jnp.where(k < 4, 0, 1)
                    from_here = jnp.logical_and(
                        jnp.logical_and(source_core == c, turn == r), holder == c
                    )

                    @pl.when(jnp.logical_not(from_here))
                    def _():
                        arrive(dst, idents[r][part])

        return begin, close

    y_begin, y_close = return_row(y_out)
    y_begin()
    og_finish()

    def grad_view(g, unit, shard, half, low, count):
        rows = pl.ds(aligned(192 * shard + unit * low, 16), unit * count)
        if g == SELF:
            return wa.at[SELF, pl.ds(2 * half, 2), rows, :]
        return wa.at[CROSS, 2 * c + half, rows, :]

    def out_view(g, unit, half, low):
        rows = pl.ds(aligned(unit * low, 16), unit)
        if g == SELF:
            return self_out.at[c, pl.ds(2 * half, 2), rows, :]
        return cross_out.at[2 * c + half, rows, :]

    def out_whole(g, owner):
        if g == SELF:
            return self_out.at[owner]
        return cross_out.at[pl.ds(2 * owner, 2)]

    buffers = {
        "self": (
            lambda half, shard: gp.at[pl.ds(2 * half, 2), pl.ds(96 * shard, 96), :],
            lambda half, shard: r2s.at[half, shard],
            lambda half, m: r3s.at[m - 1, half],
        ),
        "cross": (
            lambda half, shard: ogrow.at[pl.ds(384 * half + 96 * shard, 96), :],
            lambda half, shard: r2c.at[half, shard],
            lambda half, m: r3c.at[m - 1, half],
        ),
    }

    own_quarter = [2 * px + py, px + 2 * py]
    own_pair = [2 * px, 2 * py]
    far_pair = [2 * (1 - px), 2 * (1 - py)]
    far_quarter = [2 * px + (1 - py), (1 - px) + 2 * py]
    near_quarter = {
        "x": [2 * (1 - px) + py, (1 - px) + 2 * py],
        "y": [2 * px + (1 - py), px + 2 * (1 - py)],
    }
    opposite = [2 * (1 - px) + (1 - py), (1 - px) + 2 * (1 - py)]
    first_way = [d_x, d_y]
    second_way = [d_y, d_x]

    def fold(target, pieces):
        shape = target.shape
        if len(shape) == 3:
            for a in range(shape[0]):
                fold(target.at[a], [piece.at[a] for piece in pieces])
            return
        for low in range(0, shape[0], 96):
            rows = slice(low, min(low + 96, shape[0]))
            total = target[rows, :].astype(F32)
            for piece in pieces:
                total = total + piece[rows, :].astype(F32)
            target[rows, :] = total.astype(BF16)

    class Sum:
        def __init__(self, name, g, unit):
            self.g, self.unit = g, unit
            self.first, self.second, self.third = buffers[name]
            self.shards = [0, 1, 2, 3]
            self.s1 = [new_id(4) for _ in range(2)]
            self.s2 = [new_id(4) for _ in range(2)]
            self.s3 = [new_id(4) for _ in range(2)]
            self.to_x = [new_id() for _ in range(2)]
            self.to_y = [new_id() for _ in range(2)]
            self.across = [new_id() for _ in range(2)]
            self.core = new_id()
            self.keep = local_counter[0]
            local_counter[0] += 2
            self.copies = []

        def grad(self, shard, half, low, count):
            return grad_view(self.g, self.unit, shard, half, low, count)

        def out(self, half, low):
            return out_view(self.g, self.unit, half, low)

        def start(self, half, k):
            send(
                self.grad(self.shards[k], half, far_pair[half], 2),
                self.first(half, k),
                at(first_way[half], t),
                self.s1[half] + k,
            )

        def start_all(self):
            for k in range(len(self.shards)):
                for half in range(2):
                    self.start(half, k)

        def stage2(self, half):
            for k, shard in enumerate(self.shards):
                buffer = self.first(half, k)
                arrive(buffer, self.s1[half] + k)
                fold(self.grad(shard, half, far_quarter[half], 1), [self.part(buffer, half, 1)])
                send(
                    self.grad(shard, half, far_quarter[half], 1),
                    self.second(half, k),
                    at(second_way[half], t),
                    self.s2[half] + k,
                )
            for k, shard in enumerate(self.shards):
                buffer = self.first(half, k)
                fold(self.grad(shard, half, own_quarter[half], 1), [self.part(buffer, half, 0)])

        def part(self, buffer, half, other):
            inner = py if half == 0 else px
            low = aligned(self.unit * ((1 - inner) if other else inner), 16)
            rows = pl.ds(low, self.unit)
            if self.g == SELF:
                return buffer.at[:, rows, :]
            return buffer.at[rows, :]

        def stage3(self, half):
            for k, shard in enumerate(self.shards):
                buffer = self.second(half, k)
                arrive(buffer, self.s2[half] + k)
                fold(self.grad(shard, half, own_quarter[half], 1), [buffer])
            for m in range(1, 4):
                send(
                    self.grad((t + m) % 4, half, own_quarter[half], 1),
                    self.third(half, m),
                    at(d, (t + m) % 4),
                    self.s3[half] + m,
                )

        def stage4(self, half):
            pieces = []
            for m in range(1, 4):
                buffer = self.third(half, m)
                arrive(buffer, self.s3[half] + m)
                pieces.append(buffer)
            fold(self.grad(t, half, own_quarter[half], 1), pieces)
            self.publish(half)

        def publish(self, half):
            total = self.grad(t, half, own_quarter[half], 1)
            spot = self.out(half, own_quarter[half])
            copy = pltpu.make_async_copy(total, spot, local_sems.at[self.keep + half])
            copy.start()
            self.copies.append(copy)
            send(total, spot, at(d_x, t), self.to_x[half])
            send(total, spot, at(d_y, t), self.to_y[half])

        def stage5(self):
            for half, way, ids in ((0, "x", self.to_x), (1, "y", self.to_y)):
                for other in range(2):
                    arrive(self.out(other, near_quarter[way][other]), ids[other])
                piece = self.out(half, near_quarter[way][half])
                send(piece, piece, at(d_y if way == "x" else d_x, t), self.across[half])

        def stage6(self):
            for half in range(2):
                arrive(self.out(half, opposite[half]), self.across[half])
            for copy in self.copies:
                copy.wait()
            mine = out_whole(self.g, c)
            send(mine, mine, at(d_core, t), self.core)

        def stage7(self):
            arrive(out_whole(self.g, 1 - c), self.core)

        def both(self, stage):
            return [functools.partial(stage, 0), functools.partial(stage, 1)]

    sum_self = Sum("self", SELF, 48)
    sum_cross = Sum("cross", CROSS, 48)

    class Quarter:
        def __init__(self, k, target):
            self.k, self.target = k, target
            self.base = new_id(4)
            self.to_x, self.to_y = new_id(), new_id()
            self.from_x, self.from_y = new_id(), new_id()
            self.core = new_id()
            self.keep = local_counter[0]
            local_counter[0] += 1

        def rows(self, quarter, low=0, size=192):
            return pl.ds(aligned(192 * quarter + low, 16), size)

        def start(self, m):
            shard = (t + m) % 4
            send(
                wf.at[self.k, shard, self.rows(q), :],
                rq.at[self.k, m - 1],
                at(d, shard),
                self.base + m,
            )

        def collect(self):
            for m in range(1, 4):
                arrive(rq.at[self.k, m - 1], self.base + m)
            total = wf.at[self.k, t, self.rows(q), :]
            fold(total, [rq.at[self.k, m] for m in range(3)])
            spot = self.target.at[c, self.rows(q), :]
            self.copy = pltpu.make_async_copy(total, spot, local_sems.at[self.keep])
            self.copy.start()
            send(total, spot, at(d_x, t), self.to_x)
            send(total, spot, at(d_y, t), self.to_y)

        def relay(self):
            arrive(self.target.at[c, self.rows(qx), :], self.to_x)
            part = self.target.at[c, self.rows(qx, 0, 96), :]
            send(part, part, at(d_y, t), self.from_x)
            arrive(self.target.at[c, self.rows(qy), :], self.to_y)
            part = self.target.at[c, self.rows(qy, 96, 96), :]
            send(part, part, at(d_x, t), self.from_y)

        def swap(self):
            arrive(self.target.at[c, self.rows(qd, 0, 96), :], self.from_x)
            arrive(self.target.at[c, self.rows(qd, 96, 96), :], self.from_y)
            self.copy.wait()
            send(self.target.at[c], self.target.at[c], at(d_core, t), self.core)

        def end(self):
            arrive(self.target.at[1 - c], self.core)

    quarters = [Quarter(0, up_out), Quarter(1, down_out)]

    def quarter_grads(m):
        shard = (t + m) % 4
        own_rows = pl.ds(aligned(192 * q, 16), 192)
        qacc[...] = jnp.zeros_like(qacc)

        def row(r):
            def block(i, rows):
                section = s2all[r, pl.ds(rows, BLOCK), :]
                grad = zall[r, pl.ds(rows, BLOCK), :]
                upward = dot_nt(wf[0, shard, own_rows, :], section)
                cumulative = 0.5 * (1.0 + lax.erf(upward * (0.5**0.5)))
                density = jnp.exp(-0.5 * upward * upward) * 0.3989422804014327
                active = (upward * cumulative).astype(BF16)
                slope = cumulative + upward * density
                up_grad = (dot_nt(wf[1, shard, own_rows, :], grad) * slope).astype(BF16)
                for n in range(3):
                    cols = slice(256 * n, 256 * n + 256)
                    qacc[0, :, cols] += dot_nn(up_grad, section[:, cols])
                    qacc[1, :, cols] += dot_nn(active, grad[:, cols])

            blocks(block)

        times(4, row)
        for k in range(2):
            wf[k, shard, own_rows, :] = qacc[k].astype(BF16)
            if m:
                quarters[k].start(m)

    def norm_back(upstream, index, slot, rows, target):
        normed = xh[slot, pl.ds(rows, BLOCK), :].astype(F32)
        nrm[pl.ds(index, 1), :] += jnp.sum(upstream * normed, axis=0, keepdims=True)
        nrm[pl.ds(index + 8, 1), :] += jnp.sum(upstream, axis=0, keepdims=True)
        scaled = upstream * gains[pl.ds(index, 1), :]
        grad = rstd[slot, pl.ds(rows, BLOCK), :] * (
            scaled
            - jnp.mean(scaled, axis=-1, keepdims=True)
            - normed * jnp.mean(scaled * normed, axis=-1, keepdims=True)
        )
        res[pl.ds(rows, BLOCK), :] = grad
        target[pl.ds(rows, BLOCK), :] = grad.astype(BF16)

    def out_back(i, rows):
        upstream = ogrow[pl.ds(aligned(own_base + rows, BLOCK), BLOCK), :].astype(F32)
        norm_back(upstream, 3 + c, 2, rows, zall.at[0])

    blocks(out_back)
    z3_begin()
    og_close()
    for device in (d_x, d_y):
        pl.semaphore_signal(credit.at[0], inc=1, device_id=at(device, t), device_id_type=MESH)

    def down_back(shard):
        def block(i, rows):
            left = zall[0, pl.ds(rows, BLOCK), :]
            for n in range(3):
                cols = slice(256 * n, 256 * n + 256)
                active_grad = dot_nt(left, wf[1, shard, cols, :])
                slope = gp[shard, pl.ds(rows, BLOCK), cols].astype(F32)
                gp[shard, pl.ds(rows, BLOCK), cols] = (active_grad * slope).astype(BF16)

        blocks(block)

    times(4, down_back)
    s2_relay()

    def up_input(i, rows):
        for n in range(3):
            cols = slice(256 * n, 256 * n + 256)
            total = res[pl.ds(rows, BLOCK), cols]
            for shard in range(4):
                total = total + dot_nn(gp[shard, pl.ds(rows, BLOCK), :], wf[0, shard, :, cols])
            acc[pl.ds(rows, BLOCK), cols] = total

    blocks(up_input)
    z3_relay()
    for device in (d_x, d_y):
        pl.semaphore_signal(credit.at[1], inc=1, device_id=at(device, t), device_id_type=MESH)

    blocks(lambda i, rows: norm_back(acc[pl.ds(rows, BLOCK), :], 1 + c, 1, rows, dzb))

    dctx = act.at[0]

    def context_back(which):
        def block(i, rows):
            left = dzb[pl.ds(rows, BLOCK), :]
            for n in range(3):
                cols = slice(256 * n, 256 * n + 256)
                dctx[pl.ds(rows, BLOCK), cols] = dot_nt(left, wa[which, 3, cols, :]).astype(BF16)

        blocks(block)

    def weight_rows(which, member, left_ref, rights):
        def tile(n):
            rows = aligned(n * 256, 256)
            for k in range(3):
                wide = slice(256 * k, 256 * k + 256)
                total = None
                for low, size, ref in rights:
                    term = dot_nn(
                        left_ref[pl.ds(rows, 256), low : low + size], ref[:, wide]
                    )
                    total = term if total is None else total + term
                wa[which, member, pl.ds(rows, 256), wide] = total.astype(BF16)

        times(3, tile)

    def attend_back(which, qkv, code_row, pairs):
        def pair(k, carry):
            lanes = pl.ds(aligned(k * 128, 128), 128)
            key = qkv[1, :, lanes]
            value = qkv[2, :, lanes]
            key_t = jnp.transpose(key)
            kv_acc[...] = jnp.zeros_like(kv_acc)

            def block(i, rows):
                query = qkv[0, pl.ds(rows, BLOCK), lanes] * jnp.asarray(scaling, BF16)
                grad = dctx[pl.ds(rows, BLOCK), lanes]
                query_code = codes[
                    pl.ds(code_row, 1), pl.ds(aligned(own_base + rows, BLOCK), BLOCK)
                ]
                allowed = kcode[which, :, 0:1] == query_code
                for h in range(2):
                    query_h = query * head_lanes[h]
                    grad_h = grad * head_lanes[h]
                    scores = jnp.where(allowed, dot_nt(key, query_h), -1e30)
                    probs = jnp.exp(
                        scores - lse[which, pl.ds(2 * k + h, 1), pl.ds(rows, BLOCK)]
                    )
                    probs_grad = dot_nt(value, grad_h)
                    delta = jnp.sum(probs * probs_grad, axis=0, keepdims=True)
                    score_grad = (probs * (probs_grad - delta)).astype(BF16)
                    kv_acc[0] += dot_nn(score_grad, query_h)
                    kv_acc[1] += dot_nn(probs.astype(BF16), grad_h)
                    tt[
                        0, pl.ds(aligned(k * 128 + h * 64, 64), 64), pl.ds(rows, BLOCK)
                    ] = (dot_nn(key_t[64 * h : 64 * h + 64, :], score_grad) * scaling).astype(BF16)

            blocks(block)
            for m in range(2):
                tt[1 + m, pl.ds(aligned(k * 128, 128), 128), :] = jnp.transpose(
                    kv_acc[m]
                ).astype(BF16)
            return carry

        lax.fori_loop(pairs[0], pairs[1], pair, 0)

    def pump(*steps):
        for step in steps:
            step()

    context_back(SELF)
    for wait in pending:
        wait()
    pending.clear()
    weight_rows(SELF, 3, ctx_t.at[1], [(0, 512, dzb)])
    attend_back(1, qkv2, 2, (0, 6))

    def self_input(i, rows):
        parts = [jnp.transpose(tt[m, :, pl.ds(rows, BLOCK)]) for m in range(3)]
        for n in range(3):
            cols = slice(256 * n, 256 * n + 256)
            total = res[pl.ds(rows, BLOCK), cols]
            for m in range(3):
                total = total + dot_nn(parts[m], wa[SELF, m, :, cols])
            acc[pl.ds(rows, BLOCK), cols] = total

    blocks(self_input)
    for m in range(3):
        weight_rows(SELF, m, tt.at[m], [(0, 512, sb)])
    pl.semaphore_wait(credit.at[1], 2)
    sum_self.start_all()
    pl.semaphore_signal(credit.at[2], inc=1, device_id=at(d_core, t), device_id_type=MESH)

    s2_finish()
    z3_finish()
    quarter_grads(1)
    quarter_grads(2)
    pump(*sum_self.both(sum_self.stage2))
    quarter_grads(3)
    quarter_grads(0)
    pump(*sum_self.both(sum_self.stage3))

    blocks(lambda i, rows: norm_back(acc[pl.ds(rows, BLOCK), :], 0, 0, rows, dzb))

    norm_ids = [new_id() for _ in range(5)]
    norm_ways = [
        at(d_core, t),
        at(d_x, t),
        at(d_y, t),
        at(d, t + 1 - 2 * (t % 2)),
        at(d, (t + 2) % 4),
    ]
    norm_steps = []

    def norm_begin(k):
        send(nrm if k == 0 else nrm_recv.at[k - 1, 1], nrm_recv.at[k, 0], norm_ways[k], norm_ids[k])

    def norm_step(k):
        arrive(nrm_recv.at[k, 0], norm_ids[k])
        mine = nrm[...] if k == 0 else nrm_recv[k - 1, 1]
        total = mine + nrm_recv[k, 0]
        if k < 4:
            nrm_recv[k, 1] = total
            norm_begin(k + 1)
        else:
            norm_out[...] = total

    norm_begin(0)
    context_back(CROSS)
    weight_rows(CROSS, 3, ctx_t.at[0], [(0, 512, dzb)])
    norm_step(0)
    attend_back(0, qkv1, 0, (0, 3))
    norm_step(1)
    pump(*[one.collect for one in quarters])
    attend_back(0, qkv1, 0, (3, 6))
    norm_step(2)
    pump(*sum_self.both(sum_self.stage4), *[one.relay for one in quarters])

    key_ids = [new_id() for _ in range(2)]

    def key_input(j):
        parts = [jnp.transpose(tt[m, :, 256 * j : 256 * j + 256]) for m in (1, 2)]
        for n in range(3):
            cols = slice(256 * n, 256 * n + 256)
            act[1, 256 * j : 256 * j + 256, cols] = (
                dot_nn(parts[0], wa[CROSS, 1, :, cols]) + dot_nn(parts[1], wa[CROSS, 2, :, cols])
            ).astype(BF16)

    key_input(0)
    key_input(1)
    key_copies = [
        remote(
            act.at[1, pl.ds(256 * j, 256), :],
            dhk_recv.at[j],
            at(d_core, t),
            key_ids[j],
        )
        for j in range(2)
    ]
    key_copies[0].start()

    @pl.when(c == 0)
    def _():
        key_copies[1].start()

    def cross_input(i, rows):
        part = jnp.transpose(tt[0, :, pl.ds(rows, BLOCK)])
        for n in range(3):
            cols = slice(256 * n, 256 * n + 256)
            res[pl.ds(rows, BLOCK), cols] += dot_nn(part, wa[CROSS, 0, :, cols])

    blocks(cross_input)
    weight_rows(CROSS, 0, tt.at[0], [(0, 512, xrow.at[pl.ds(own_base, 512), :])])
    for m in range(1, 3):
        weight_rows(
            CROSS,
            m,
            tt.at[m],
            [
                (0, 256, xrow.at[pl.ds(other_base, 256), :]),
                (256, 256, xrow.at[pl.ds(512, 256), :]),
            ],
        )

    pl.semaphore_wait(credit.at[2], 1)
    core_sums = [(a, n, new_id()) for a in range(2) for n in range(3)]

    def core_slot(a, n):
        k = 3 * a + n
        return qkv2.at[k // 2, pl.ds(256 * (k % 2), 256), :]

    for a, n, ident in core_sums:
        send(
            wa.at[CROSS, 2 * (1 - c) + a, pl.ds(256 * n, 256), :],
            core_slot(a, n),
            at(d_core, t),
            ident,
        )
    norm_step(3)

    y_close()
    arrive(dhk_recv.at[0], key_ids[0])

    @pl.when(c == 1)
    def _():
        arrive(dhk_recv.at[1], key_ids[1])

    yb[:BLOCK, :] = (res[:BLOCK, :] + dhk_recv[0].astype(F32)).astype(BF16)

    @pl.when(c == 1)
    def _():
        own_part = act[1, BLOCK:, :].astype(F32)
        yb[BLOCK:, :] = (res[BLOCK:, :] + dhk_recv[1].astype(F32) + own_part).astype(BF16)

    dx_begin, dx_close = return_row(dx_out)
    dx_begin()

    for a, n, ident in core_sums:
        arrive(core_slot(a, n), ident)
        fold(wa.at[CROSS, 2 * c + a, pl.ds(256 * n, 256), :], [core_slot(a, n)])
    pl.semaphore_wait(credit.at[0], 2)
    sum_cross.start_all()
    norm_step(4)
    pump(
        *[one.swap for one in quarters],
        sum_self.stage5,
        *sum_cross.both(sum_cross.stage2),
        sum_self.stage6,
        *sum_cross.both(sum_cross.stage3),
        *sum_cross.both(sum_cross.stage4),
        sum_cross.stage5,
        sum_cross.stage6,
        *[one.end for one in quarters],
        sum_self.stage7,
        sum_cross.stage7,
    )
    for wait in pending + late:
        wait()
    key_copies[0].wait_send()

    @pl.when(c == 0)
    def _():
        key_copies[1].wait_send()

    dx_close()
    if counter[0] > SEMAPHORES or local_counter[0] > LOCALS:
        raise ValueError((counter[0], local_counter[0]))


SEMAPHORES = 320
LOCALS = 40


def call_layer(*operands):
    def vmem(shape, dtype=BF16):
        return pltpu.VMEM(shape, dtype)

    anywhere = pl.BlockSpec(memory_space=pl.ANY)
    whole = pl.BlockSpec(memory_space=pltpu.VMEM)
    x_in = operands[0]
    return pl.pallas_call(
        layer_kernel,
        name="cross_modality_layer",
        out_shape=(
            jax.ShapeDtypeStruct(x_in.shape, BF16),
            jax.ShapeDtypeStruct(x_in.shape, BF16),
            jax.ShapeDtypeStruct((4, 192, 768), BF16),
            jax.ShapeDtypeStruct((2, 4, 192, 768), BF16),
            jax.ShapeDtypeStruct((2, 768, 768), BF16),
            jax.ShapeDtypeStruct((2, 768, 768), BF16),
            jax.ShapeDtypeStruct((16, 768), F32),
        ),
        in_specs=[anywhere] * 7 + [whole] * 2,
        out_specs=(anywhere,) * 6 + (whole,),
        scratch_shapes=[
            vmem((2, 4, 768, 768)),
            vmem((2, 4, 768, 768)),
            vmem((768, 768)),
            vmem((768, 768)),
            vmem((8, 768), F32),
            vmem((2, 512, 128), F32),
            vmem((3, 512, 768)),
            vmem((3, 512, 768)),
            vmem((2, 768, 512)),
            vmem((2, 16, 512), F32),
            vmem((3, 512, 768)),
            vmem((3, 512, 1), F32),
            vmem((512, 768)),
            vmem((512, 768), F32),
            vmem((512, 768), F32),
            vmem((4, 512, 768)),
            vmem((4, 512, 768)),
            vmem((512, 768)),
            vmem((3, 768, 512)),
            vmem((512, 768)),
            vmem((2, 256, 768)),
            vmem((2, 512, 128), F32),
            vmem((16, 768), F32),
            vmem((5, 2, 16, 768), F32),
            vmem((4, 512, 768)),
            vmem((4, 512, 768)),
            vmem((2, 192, 768), F32),
            vmem((2, 3, 192, 768)),
            vmem((2, 4, 2, 48, 768)),
            vmem((3, 2, 2, 48, 768)),
            vmem((2, 4, 48, 768)),
            vmem((3, 2, 48, 768)),
            pltpu.SemaphoreType.DMA((SEMAPHORES,)),
            pltpu.SemaphoreType.DMA((SEMAPHORES,)),
            pltpu.SemaphoreType.DMA((LOCALS,)),
            pltpu.SemaphoreType.REGULAR((3,)),
        ],
        compiler_params=pltpu.CompilerParams(
            collective_id=0, has_side_effects=True, vmem_limit_bytes=64 * 1024 * 1024 - 512 * 1024
        ),
    )(*operands)


def solution(mesh):
    extra = []
    step = 8
    while step < mesh.shape["dp"]:
        extra.append(step)
        step *= 2

    def total(array):
        for step in extra:
            pairs = [(k, k ^ step) for k in range(mesh.shape["dp"])]
            array = array + lax.ppermute(array, "dp", pairs)
        return array

    def body(
        layer_input,
        word_segments,
        image_order,
        cross_qkv,
        cross_out,
        self_qkv,
        self_out,
        ffn_up,
        ffn_down,
        norm_gains,
        norm_biases,
        out_grad,
    ):
        rows = layer_input.shape[0]
        images = jnp.repeat(image_order, BOXES, axis=1)
        pads = jnp.full((rows, PADS), CAPTIONS, jnp.int32)
        none = jnp.full((rows, WORDS + REGIONS + PADS), -1, jnp.int32)
        groups = jnp.concatenate([word_segments, images, pads], axis=1)
        keys = jnp.concatenate([word_segments, none[:, :REGIONS], pads], axis=1)
        kinds = jnp.concatenate([word_segments, images + 16, pads + 32], axis=1)
        codes = jnp.stack([groups, keys, kinds, none, none, none, none, none], axis=1).astype(F32)
        cross = jnp.concatenate([jnp.swapaxes(cross_qkv, 1, 2), cross_out[None]], axis=0)
        own = jnp.concatenate([jnp.swapaxes(self_qkv, 2, 3), self_out[:, None]], axis=1)
        y, dx, d_cross, d_self, d_up, d_down, d_norm = call_layer(
            layer_input,
            out_grad,
            codes,
            cross,
            own,
            ffn_up,
            ffn_down,
            norm_gains,
            norm_biases,
        )
        d_cross, d_self, d_up, d_down = [
            total(array.astype(F32)) for array in (d_cross, d_self, d_up, d_down)
        ]
        d_norm = total(d_norm)
        return (
            y,
            dx.astype(F32),
            jnp.swapaxes(d_cross[:3], 1, 2),
            d_cross[3],
            jnp.swapaxes(d_self[:, :3], 2, 3),
            d_self[:, 3],
            jnp.swapaxes(d_up, 1, 2),
            d_down,
            d_norm[0:5],
            d_norm[8:13],
        )

    in_specs = (
        P("dp", "tensor", None),
        P("dp", None),
        P("dp", None),
        P(None, None, "tensor"),
        P("tensor", None),
        P(None, None, None, "tensor"),
        P(None, "tensor", None),
        P(None, None, "tensor"),
        P(None, "tensor", None),
        P(),
        P(),
        P("dp", "tensor", None),
    )
    out_specs = (
        P("dp", "tensor", None),
        P("dp", "tensor", None),
        P(None, None, "tensor"),
        P("tensor", None),
        P(None, None, None, "tensor"),
        P(None, "tensor", None),
        P(None, None, "tensor"),
        P(None, "tensor", None),
        P(),
        P(),
    )
    return jax.shard_map(body, mesh=mesh, in_specs=in_specs, out_specs=out_specs, check_vma=False)
```

```python
import functools

import jax
import jax.numpy as jnp
from jax import lax
from jax.experimental import pallas as pl
from jax.experimental.pallas import tpu as pltpu
from jax.sharding import PartitionSpec as P

HEAD_DIM = 64
WORDS = 256
CAPTIONS = 14
BOXES = 36
REGIONS = 504
PADS = 8
NORM_EPSILON = 1e-12
BLOCK = 256
BF16 = jnp.bfloat16
F32 = jnp.float32
MESH = pl.DeviceIdType.MESH
CROSS, SELF, UP, DOWN = 0, 1, 2, 3


def dot_nn(left, right):
    return jnp.dot(left, right, preferred_element_type=F32)


def dot_nt(left, right):
    return lax.dot_general(left, right, (((1,), (1,)), ((), ())), preferred_element_type=F32)


def aligned(value, step):
    return pl.multiple_of(value, step)


def layer_kernel(
    x_in,
    og_in,
    codes_in,
    cross_in,
    cross_out_in,
    self_in,
    self_out_in,
    up_in,
    down_in,
    gains,
    biases,
    y_out,
    dx_out,
    cross_out,
    self_out,
    up_out,
    down_out,
    norm_out,
    wa,
    wf,
    xrow,
    ogrow,
    codes,
    kcode,
    qkv1,
    qkv2,
    ctx_t,
    lse,
    xh,
    rstd,
    sb,
    res,
    acc,
    act,
    gp,
    dzb,
    tt,
    yb,
    dhk_recv,
    kv_acc,
    nrm,
    nrm_recv,
    s2all,
    zall,
    qacc,
    rq,
    r2s,
    r3s,
    r2c,
    r3c,
    send_sems,
    recv_sems,
    local_sems,
    credit,
):
    d = lax.axis_index("dp")
    t = lax.axis_index("tensor")
    c = d % 2
    px = (d // 2) % 2
    py = (d // 4) % 2
    q = px + 2 * py
    d_core = d + 1 - 2 * c
    d_x = d + 2 - 4 * px
    d_y = d + 4 - 8 * py
    holder = t // 2
    d_holder = d - c + holder
    turn = t % 2
    nb = 1 + c
    near = {"x": d_x, "y": d_y, "core": d_core}

    def at(dp_index, tensor_index):
        return {"dp": dp_index, "tensor": tensor_index}

    counter = [0]
    local_counter = [0]
    pending = []

    def new_id(count=1):
        counter[0] += count
        return counter[0] - count

    def remote(src, dst, device, ident, arrival=None):
        return pltpu.make_async_remote_copy(
            src_ref=src,
            dst_ref=dst,
            send_sem=send_sems.at[ident],
            recv_sem=recv_sems.at[ident if arrival is None else arrival],
            device_id=device,
            device_id_type=MESH,
        )

    def send(src, dst, device, ident):
        copy = remote(src, dst, device, ident)
        copy.start()
        pending.append(copy.wait_send)

    def arrive(dst, ident):
        remote(dst, dst, at(d_core, t), ident).wait_recv()

    def local(src, dst):
        copy = pltpu.make_async_copy(src, dst, local_sems.at[local_counter[0]])
        local_counter[0] += 1
        return copy

    def blocks(body):
        def step(i, carry):
            body(i, aligned(i * BLOCK, BLOCK))
            return carry

        lax.fori_loop(0, nb, step, 0)

    def times(count, body):
        def step(i, carry):
            body(i)
            return carry

        lax.fori_loop(0, count, step, 0)

    barrier = pltpu.get_barrier_semaphore()
    partners = [at(d_core, t), at(d_x, t), at(d_y, t)]
    for m in range(1, 4):
        partners.append(at(d, (t + m) % 4))
        partners.append(at(d_core, (t + m) % 4))
    for partner in partners:
        pl.semaphore_signal(barrier, inc=1, device_id=partner, device_id_type=MESH)

    half_rows = aligned(t * 192, 16)
    own_copies = [
        local(cross_out_in, wa.at[CROSS, 3, pl.ds(half_rows, 192), :]),
        local(self_out_in.at[c], wa.at[SELF, 3, pl.ds(half_rows, 192), :]),
        local(down_in.at[c], wf.at[1, t]),
    ]
    raw_copies = [
        local(cross_in, wa.at[CROSS, pl.ds(0, 3), pl.ds(half_rows, 192), :]),
        local(self_in.at[c], wa.at[SELF, pl.ds(0, 3), pl.ds(half_rows, 192), :]),
    ]
    up_copies = [
        local(up_in.at[c, pl.ds(0, 512), :], qkv1.at[0]),
        local(up_in.at[c, pl.ds(512, 256), :], qkv1.at[1, pl.ds(0, 256), :]),
    ]
    for copy in raw_copies + own_copies + up_copies:
        copy.start()

    zero_half = jnp.zeros((BLOCK, 768), BF16)

    @pl.when(c == 0)
    def _():
        for ref in (qkv2.at[1], qkv2.at[2], sb, dzb):
            ref[BLOCK:, :] = zero_half
        for k in range(2):
            ctx_t[k, :, BLOCK:] = jnp.zeros((768, BLOCK), BF16)
        tt[0, :, BLOCK:] = jnp.zeros((768, BLOCK), BF16)

    nrm[...] = jnp.zeros_like(nrm)
    for g in (CROSS, SELF):
        raw_copies[g].wait()
        own_copies[g].wait()
    pl.semaphore_wait(barrier, len(partners))

    def spread_row(source, row):
        base = new_id(4)
        core_base = new_id(4)
        own = local(source.at[turn], row.at[pl.ds(half_rows, 192), :])

        def each_target(action):
            for r in range(2):
                target = 2 * c + r

                @pl.when(target != t)
                def _():
                    action(
                        remote(
                            source.at[r],
                            row.at[pl.ds(half_rows, 192), :],
                            at(d, target),
                            base + r,
                            base + t,
                        )
                    )

        def each_relay(action):
            @pl.when(holder == c)
            def _():
                for s in range(4):
                    part = row.at[pl.ds(192 * s, 192), :]
                    action(s, part, remote(part, part, at(d_core, t), core_base + s))

        def begin():
            each_target(lambda copy: copy.start())

            @pl.when(holder == c)
            def _():
                own.start()

        def relay():
            def action(s, part, copy):
                @pl.when(t == s)
                def _():
                    own.wait()

                @pl.when(t != s)
                def _():
                    arrive(part, base + s)

                copy.start()

            each_relay(action)

        def finish():
            @pl.when(holder != c)
            def _():
                for s in range(4):
                    arrive(row.at[pl.ds(192 * s, 192), :], core_base + s)

        def close():
            each_target(lambda copy: copy.wait_send())
            each_relay(lambda s, part, copy: copy.wait_send())

        return begin, relay, finish, close

    x_begin, x_relay, x_finish, x_close = spread_row(x_in, xrow)
    og_begin, og_relay, og_finish, og_close = spread_row(og_in, ogrow)
    pending.append(x_close)

    code_ident = new_id()
    code_own = local(codes_in.at[turn], codes)

    @pl.when(holder == c)
    def _():
        code_own.start()
        remote(codes_in.at[turn], codes, at(d_core, t), code_ident).start()

    def share(g, shard, quarter, low, high):
        if g >= UP:
            rows = aligned(quarter * 192 + low * 96, 16)
            return wf.at[g - UP, shard, pl.ds(rows, (high - low) * 96), :]
        rows = aligned(shard * 192 + quarter * 48, 16)
        if g == SELF:
            return wa.at[SELF, pl.ds(2 * low, 2 * (high - low)), pl.ds(rows, 48), :]
        return wa.at[CROSS, pl.ds(2 * c + low, high - low), pl.ds(rows, 48), :]

    def own_share(g):
        if g >= UP:
            rows = pl.ds(aligned(q * 192, 16), 192)
            return wf.at[0, t, rows, :] if g == UP else down_in.at[c, rows, :]
        return share(g, t, q, 0, 2)

    qx, qy = (1 - px) + 2 * py, px + 2 * (1 - py)
    qd = (1 - px) + 2 * (1 - py)
    items = [(g, m) for g in (CROSS, SELF, UP, DOWN) for m in range(1, 4)]
    z_base = {g: new_id(4) for g in (CROSS, SELF, UP, DOWN)}
    own_ids = {g: new_id(2) for g in (CROSS, SELF, UP, DOWN)}
    pass_ids = {item: new_id() for item in items}
    x_ids = {item: new_id() for item in items}
    y_ids = {item: new_id() for item in items}
    fx_ids = {item: new_id() for item in items}
    fy_ids = {item: new_id() for item in items}
    core_ids = {m: new_id() for m in range(1, 4)}
    arrivals = {
        1: t + 1 - 2 * (t % 2),
        2: 2 - t // 2,
        3: 3 - 3 * (t // 2),
    }

    def z_way(g, way):
        exists = t > 0 if way == 0 else t < 3
        target = t - 1 + 2 * way

        def copy():
            return remote(
                own_share(g),
                share(g, t, q, 0, 2),
                at(d, target),
                own_ids[g] + way,
                z_base[g] + t,
            )

        @pl.when(exists)
        def _():
            copy().start()

        def close():
            @pl.when(exists)
            def _():
                copy().wait_send()

        pending.append(close)

    def z_own(g):
        for way in range(2):
            z_way(g, way)

    def first(item):
        g, m = item
        shard = arrivals[m]
        piece = share(g, shard, q, 0, 2)
        arrive(piece, z_base[g] + shard)
        inner = jnp.logical_and(t > 0, t < 3)
        target = jnp.where(shard < t, t + 1, t - 1)

        def copy():
            return remote(piece, piece, at(d, target), pass_ids[item], z_base[g] + shard)

        @pl.when(inner)
        def _():
            copy().start()

        def close():
            @pl.when(inner)
            def _():
                copy().wait_send()

        pending.append(close)
        send(piece, piece, at(d_x, t), x_ids[item])
        send(piece, piece, at(d_y, t), y_ids[item])
        if m == 1 and g < DOWN:
            z_own(g + 1)
        if g == CROSS and m == 1:
            x_begin()
        if item == (DOWN, 1):
            og_begin()

    def second(item):
        g, m = item
        shard = arrivals[m]
        arrive(share(g, shard, qx, 0, 2), x_ids[item])
        low = share(g, shard, qx, 0, 1)
        send(low, low, at(d_y, t), fy_ids[item])
        arrive(share(g, shard, qy, 0, 2), y_ids[item])
        high = share(g, shard, qy, 1, 2)
        send(high, high, at(d_x, t), fx_ids[item])

    def third(item):
        g, m = item
        shard = arrivals[m]
        arrive(share(g, shard, qd, 0, 1), fy_ids[item])
        arrive(share(g, shard, qd, 1, 2), fx_ids[item])
        if g == CROSS:
            rows = pl.ds(aligned(shard * 192, 16), 192)
            whole = wa.at[CROSS, pl.ds(2 * c, 2), rows, :]
            send(whole, whole, at(d_core, t), core_ids[m])

    def last(m):
        shard = arrivals[m]
        rows = pl.ds(aligned(shard * 192, 16), 192)
        arrive(wa.at[CROSS, pl.ds(2 * (1 - c), 2), rows, :], core_ids[m])

    z_own(CROSS)
    for copy in up_copies:
        copy.wait()
    wf[0, t, :, 0:512] = jnp.transpose(qkv1[0])
    wf[0, t, :, 512:768] = jnp.transpose(qkv1[1, 0:256, :])

    steps = []
    position = {}
    for k in range(len(items) + 2):
        if k < len(items):
            steps.append(functools.partial(first, items[k]))
        if 0 <= k - 1 < len(items):
            steps.append(functools.partial(second, items[k - 1]))
        if 0 <= k - 2 < len(items):
            steps.append(functools.partial(third, items[k - 2]))
            position[items[k - 2]] = len(steps)
    done = [0]

    def advance(upto):
        while done[0] < min(upto, len(steps)):
            steps[done[0]]()
            done[0] += 1

    advance(position[(CROSS, 2)])
    x_relay()
    x_finish()

    @pl.when(holder == c)
    def _():
        code_own.wait()
        remote(codes_in.at[turn], codes, at(d_core, t), code_ident).wait_send()

    @pl.when(holder != c)
    def _():
        arrive(codes, code_ident)

    def as_column(row):
        return jnp.transpose(jnp.broadcast_to(row, (128, BLOCK)))

    own_base = aligned(c * BLOCK, BLOCK)
    other_base = aligned((1 - c) * BLOCK, BLOCK)
    kcode[0, :BLOCK, :] = as_column(codes[0:1, pl.ds(other_base, BLOCK)])
    kcode[0, BLOCK:, :] = as_column(codes[pl.ds(c, 1), 512:768])
    kcode[1, :BLOCK, :] = as_column(codes[2:3, pl.ds(own_base, BLOCK)])
    kcode[1, BLOCK:, :] = as_column(codes[pl.ds(3 - c, 1), 512:768])

    lane = lax.broadcasted_iota(jnp.int32, (1, 128), 1)
    head_lanes = [
        (lane < HEAD_DIM).astype(F32).astype(BF16),
        (lane >= HEAD_DIM).astype(F32).astype(BF16),
    ]
    scaling = HEAD_DIM ** (-0.5)

    def project(source, base, weight, target, rows):
        left = source[pl.ds(base, BLOCK), :]
        for n in range(3):
            target[pl.ds(rows, BLOCK), 256 * n : 256 * n + 256] = dot_nt(
                left, weight[256 * n : 256 * n + 256, :]
            ).astype(BF16)

    def attend(which, qkv, code_row, pairs):
        def pair(k):
            lanes = pl.ds(aligned(k * 128, 128), 128)
            key = qkv[1, :, lanes]
            value_t = jnp.transpose(qkv[2, :, lanes])

            def block(i, rows):
                query = qkv[0, pl.ds(rows, BLOCK), lanes] * jnp.asarray(scaling, BF16)
                query_code = codes[
                    pl.ds(code_row, 1), pl.ds(aligned(own_base + rows, BLOCK), BLOCK)
                ]
                allowed = kcode[which, :, 0:1] == query_code
                for h in range(2):
                    scores = dot_nt(key, query * head_lanes[h])
                    scores = jnp.where(allowed, scores, -1e30)
                    top = jnp.max(scores, axis=0, keepdims=True)
                    exponent = jnp.exp(scores - top)
                    total = jnp.sum(exponent, axis=0, keepdims=True)
                    probs = (exponent * (1.0 / total)).astype(BF16)
                    lse[which, pl.ds(2 * k + h, 1), pl.ds(rows, BLOCK)] = top + jnp.log(total)
                    ctx_t[
                        which,
                        pl.ds(aligned(k * 128 + h * 64, 64), 64),
                        pl.ds(rows, BLOCK),
                    ] = dot_nn(value_t[64 * h : 64 * h + 64, :], probs).astype(BF16)

            blocks(block)

        def run(k, carry):
            pair(k)
            return carry

        lax.fori_loop(pairs[0], pairs[1], run, 0)

    def normalize(summed, index, slot, rows):
        center = summed - jnp.mean(summed, axis=-1, keepdims=True)
        inverse = lax.rsqrt(jnp.mean(center * center, axis=-1, keepdims=True) + NORM_EPSILON)
        normed = center * inverse
        xh[slot, pl.ds(rows, BLOCK), :] = normed.astype(BF16)
        rstd[slot, pl.ds(rows, BLOCK), :] = inverse
        return normed * gains[pl.ds(index, 1), :] + biases[pl.ds(index, 1), :]

    def attention_out(which, rows):
        context = jnp.transpose(ctx_t[which, :, pl.ds(rows, BLOCK)])
        return dot_nn(context, wa[which, 3])

    advance(position[(CROSS, 3)])
    for m in range(1, 4):
        last(m)
    blocks(lambda i, rows: project(xrow, own_base + rows, wa.at[CROSS, 0], qkv1.at[0], rows))
    for k in range(1, 3):
        project(xrow, other_base, wa.at[CROSS, k], qkv1.at[k], 0)
        project(xrow, 512, wa.at[CROSS, k], qkv1.at[k], BLOCK)
    attend(0, qkv1, 0, (0, 3))
    advance(position[(SELF, 1)])
    attend(0, qkv1, 0, (3, 6))
    advance(position[(SELF, 2)])

    def cross_end(i, rows):
        stream = xrow[pl.ds(aligned(own_base + rows, BLOCK), BLOCK), :].astype(F32)
        section = normalize(stream + attention_out(0, rows), 0, 0, rows)
        res[pl.ds(rows, BLOCK), :] = section
        sb[pl.ds(rows, BLOCK), :] = section.astype(BF16)

    blocks(cross_end)

    advance(position[(SELF, 3)])
    for k in range(3):
        blocks(lambda i, rows: project(sb, rows, wa.at[SELF, k], qkv2.at[k], rows))
    attend(1, qkv2, 2, (0, 3))
    advance(position[(UP, 1)])
    attend(1, qkv2, 2, (3, 6))
    advance(position[(UP, 2)])

    def self_end(i, rows):
        summed = res[pl.ds(rows, BLOCK), :] + attention_out(1, rows)
        section = normalize(summed, 1 + c, 1, rows)
        res[pl.ds(rows, BLOCK), :] = section
        s2all[0, pl.ds(rows, BLOCK), :] = section.astype(BF16)

    blocks(self_end)

    late = []

    def plane_gather(buffer):
        to_x, to_y, from_x, from_y = new_id(), new_id(), new_id(), new_id()

        def sized(action):
            for core in range(2):

                @pl.when(c == core)
                def _():
                    action(BLOCK * (core + 1))

        def part(k, low, size):
            return buffer.at[k, pl.ds(low, size), :]

        def firsts(size):
            return [
                remote(part(0, 0, size), part(1, 0, size), at(d_x, t), to_x),
                remote(part(0, 0, size), part(2, 0, size), at(d_y, t), to_y),
            ]

        def seconds(size):
            half = size // 2
            return [
                remote(part(1, 0, half), part(3, 0, half), at(d_y, t), from_x),
                remote(part(2, half, half), part(3, half, half), at(d_x, t), from_y),
            ]

        def begin():
            sized(lambda size: [copy.start() for copy in firsts(size)])

        def relay():
            def action(size):
                onward = seconds(size)
                arrive(part(1, 0, size), to_x)
                onward[0].start()
                arrive(part(2, 0, size), to_y)
                onward[1].start()

            sized(action)

        def finish():
            def action(size):
                half = size // 2
                arrive(part(3, 0, half), from_x)
                arrive(part(3, half, half), from_y)

            sized(action)

        def close():
            sized(lambda size: [copy.wait_send() for copy in firsts(size) + seconds(size)])

        late.append(close)
        return begin, relay, finish

    s2_begin, s2_relay, s2_finish = plane_gather(s2all)
    z3_begin, z3_relay, z3_finish = plane_gather(zall)
    def feed_up(shard):
        def block(i, rows):
            left = s2all[0, pl.ds(rows, BLOCK), :]
            for n in range(3):
                cols = slice(256 * n, 256 * n + 256)
                upward = dot_nt(left, wf[0, shard, cols, :])
                cumulative = 0.5 * (1.0 + lax.erf(upward * (0.5**0.5)))
                density = jnp.exp(-0.5 * upward * upward) * 0.3989422804014327
                act[shard, pl.ds(rows, BLOCK), cols] = (upward * cumulative).astype(BF16)
                gp[shard, pl.ds(rows, BLOCK), cols] = (cumulative + upward * density).astype(BF16)

        blocks(block)

    feed_up(t)
    for m in range(1, 4):
        advance(position[(UP, m)])
        feed_up(arrivals[m])

    def feed_down(shard):
        def block(i, rows):
            left = act[shard, pl.ds(rows, BLOCK), :]
            for n in range(3):
                cols = slice(256 * n, 256 * n + 256)
                res[pl.ds(rows, BLOCK), cols] += dot_nn(left, wf[1, shard, :, cols])

        blocks(block)

    own_copies[2].wait()
    feed_down(t)
    for m in range(1, 4):
        advance(position[(DOWN, m)])
        if m == 3:
            s2_begin()
            og_relay()
        feed_down(arrivals[m])

    def layer_end(i, rows):
        result = normalize(res[pl.ds(rows, BLOCK), :], 3 + c, 2, rows)
        yb[pl.ds(rows, BLOCK), :] = result.astype(BF16)

    blocks(layer_end)

    def return_row(target):
        idents = [[new_id() for _ in range(3)] for _ in range(2)]
        send_base = new_id(12)
        local_ids = [local_counter[0] + k for k in range(3)]
        local_counter[0] += 3

        def each(action):
            for k in range(12):
                source_core = 0 if k < 4 else 1
                slots, part = k // 3, k % 3
                src = yb.at[pl.ds(64 * k - 256 * source_core, 64), :]
                for r in range(2):
                    dst = target.at[r, pl.ds(64 * part, 64), :]
                    mine = jnp.logical_and(c == source_core, turn == r)
                    here = jnp.logical_and(holder == c, t == slots)

                    @pl.when(jnp.logical_and(mine, here))
                    def _():
                        copy = pltpu.make_async_copy(src, dst, local_sems.at[local_ids[part]])
                        if action == "start":
                            copy.start()
                        elif action == "wait":
                            copy.wait()

                    @pl.when(jnp.logical_and(mine, jnp.logical_not(here)))
                    def _():
                        copy = remote(
                            src, dst, at(d_holder, slots), send_base + k, idents[r][part]
                        )
                        if action == "start":
                            copy.start()
                        elif action == "wait":
                            copy.wait_send()

        def begin():
            each("start")

        def close():
            each("wait")
            for r in range(2):
                for part in range(3):
                    dst = target.at[r, pl.ds(64 * part, 64), :]
                    k = 3 * t + part
                    source_core = jnp.where(k < 4, 0, 1)
                    from_here = jnp.logical_and(
                        jnp.logical_and(source_core == c, turn == r), holder == c
                    )

                    @pl.when(jnp.logical_not(from_here))
                    def _():
                        arrive(dst, idents[r][part])

        return begin, close

    y_begin, y_close = return_row(y_out)
    y_begin()
    og_finish()

    def grad_view(g, unit, shard, half, low, count):
        rows = pl.ds(aligned(192 * shard + unit * low, 16), unit * count)
        if g == SELF:
            return wa.at[SELF, pl.ds(2 * half, 2), rows, :]
        return wa.at[CROSS, 2 * c + half, rows, :]

    def out_view(g, unit, half, low):
        rows = pl.ds(aligned(unit * low, 16), unit)
        if g == SELF:
            return self_out.at[c, pl.ds(2 * half, 2), rows, :]
        return cross_out.at[2 * c + half, rows, :]

    def out_whole(g, owner):
        if g == SELF:
            return self_out.at[owner]
        return cross_out.at[pl.ds(2 * owner, 2)]

    buffers = {
        "self": (
            lambda half, shard: gp.at[pl.ds(2 * half, 2), pl.ds(96 * shard, 96), :],
            lambda half, shard: r2s.at[half, shard],
            lambda half, m: r3s.at[m - 1, half],
        ),
        "cross": (
            lambda half, shard: ogrow.at[pl.ds(384 * half + 96 * shard, 96), :],
            lambda half, shard: r2c.at[half, shard],
            lambda half, m: r3c.at[m - 1, half],
        ),
    }

    own_quarter = [2 * px + py, px + 2 * py]
    own_pair = [2 * px, 2 * py]
    far_pair = [2 * (1 - px), 2 * (1 - py)]
    far_quarter = [2 * px + (1 - py), (1 - px) + 2 * py]
    near_quarter = {
        "x": [2 * (1 - px) + py, (1 - px) + 2 * py],
        "y": [2 * px + (1 - py), px + 2 * (1 - py)],
    }
    opposite = [2 * (1 - px) + (1 - py), (1 - px) + 2 * (1 - py)]
    first_way = [d_x, d_y]
    t_pair, t_far, t_cross = t + 1 - 2 * (t % 2), (t + 2) % 4, 3 - t
    second_way = [d_y, d_x]

    def fold(target, pieces):
        shape = target.shape
        if len(shape) == 3:
            for a in range(shape[0]):
                fold(target.at[a], [piece.at[a] for piece in pieces])
            return
        for low in range(0, shape[0], 96):
            rows = slice(low, min(low + 96, shape[0]))
            total = target[rows, :].astype(F32)
            for piece in pieces:
                total = total + piece[rows, :].astype(F32)
            target[rows, :] = total.astype(BF16)

    class Sum:
        def __init__(self, name, g, unit):
            self.g, self.unit = g, unit
            self.first, self.second, self.third = buffers[name]
            self.shards = [0, 1, 2, 3]
            self.s1 = [new_id(4) for _ in range(2)]
            self.s2 = [new_id(4) for _ in range(2)]
            self.s3 = [new_id(4) for _ in range(2)]
            self.to_x = [new_id() for _ in range(2)]
            self.to_y = [new_id() for _ in range(2)]
            self.across = [new_id() for _ in range(2)]
            self.core = new_id()
            self.keep = local_counter[0]
            local_counter[0] += 2
            self.copies = []

        def grad(self, shard, half, low, count):
            return grad_view(self.g, self.unit, shard, half, low, count)

        def out(self, half, low):
            return out_view(self.g, self.unit, half, low)

        def start(self, half, k):
            send(
                self.grad(self.shards[k], half, far_pair[half], 2),
                self.first(half, k),
                at(first_way[half], t),
                self.s1[half] + k,
            )

        def start_all(self):
            for k in range(len(self.shards)):
                for half in range(2):
                    self.start(half, k)

        def stage2(self, half):
            for k, shard in enumerate(self.shards):
                buffer = self.first(half, k)
                arrive(buffer, self.s1[half] + k)
                fold(self.grad(shard, half, far_quarter[half], 1), [self.part(buffer, half, 1)])
                send(
                    self.grad(shard, half, far_quarter[half], 1),
                    self.second(half, k),
                    at(second_way[half], t),
                    self.s2[half] + k,
                )
            for k, shard in enumerate(self.shards):
                buffer = self.first(half, k)
                fold(self.grad(shard, half, own_quarter[half], 1), [self.part(buffer, half, 0)])

        def part(self, buffer, half, other):
            inner = py if half == 0 else px
            low = aligned(self.unit * ((1 - inner) if other else inner), 16)
            rows = pl.ds(low, self.unit)
            if self.g == SELF:
                return buffer.at[:, rows, :]
            return buffer.at[rows, :]

        def stage3(self, half):
            for k, shard in enumerate(self.shards):
                buffer = self.second(half, k)
                arrive(buffer, self.s2[half] + k)
                fold(self.grad(shard, half, own_quarter[half], 1), [buffer])
            for k, shard in enumerate((t_pair, t_cross)):
                send(
                    self.grad(shard, half, own_quarter[half], 1),
                    self.third(half, 1 + k),
                    at(d, t_pair),
                    self.s3[half] + k,
                )

        def stage4(self, half):
            for k, shard in ((1, t_far), (0, t)):
                buffer = self.third(half, 1 + k)
                arrive(buffer, self.s3[half] + k)
                fold(self.grad(shard, half, own_quarter[half], 1), [buffer])
                if k:
                    send(
                        self.grad(t_far, half, own_quarter[half], 1),
                        self.third(half, 3),
                        at(d, t_far),
                        self.s3[half] + 2,
                    )

        def stage4_end(self, half):
            buffer = self.third(half, 3)
            arrive(buffer, self.s3[half] + 2)
            fold(self.grad(t, half, own_quarter[half], 1), [buffer])
            self.publish(half)

        def publish(self, half):
            total = self.grad(t, half, own_quarter[half], 1)
            spot = self.out(half, own_quarter[half])
            copy = pltpu.make_async_copy(total, spot, local_sems.at[self.keep + half])
            copy.start()
            self.copies.append(copy)
            send(total, spot, at(d_x, t), self.to_x[half])
            send(total, spot, at(d_y, t), self.to_y[half])

        def stage5(self):
            for half, way, ids in ((0, "x", self.to_x), (1, "y", self.to_y)):
                for other in range(2):
                    arrive(self.out(other, near_quarter[way][other]), ids[other])
                piece = self.out(half, near_quarter[way][half])
                send(piece, piece, at(d_y if way == "x" else d_x, t), self.across[half])

        def stage6(self):
            for half in range(2):
                arrive(self.out(half, opposite[half]), self.across[half])
            for copy in self.copies:
                copy.wait()
            mine = out_whole(self.g, c)
            send(mine, mine, at(d_core, t), self.core)

        def stage7(self):
            arrive(out_whole(self.g, 1 - c), self.core)

        def both(self, stage):
            return [functools.partial(stage, 0), functools.partial(stage, 1)]

    sum_self = Sum("self", SELF, 48)
    sum_cross = Sum("cross", CROSS, 48)

    class Quarter:
        def __init__(self, k, target):
            self.k, self.target = k, target
            self.base = new_id(4)
            self.to_x, self.to_y = new_id(), new_id()
            self.from_x, self.from_y = new_id(), new_id()
            self.core = new_id()
            self.keep = local_counter[0]
            local_counter[0] += 1

        def rows(self, quarter, low=0, size=192):
            return pl.ds(aligned(192 * quarter + low, 16), size)

        def piece(self, shard):
            return wf.at[self.k, shard, self.rows(q), :]

        def start(self):
            for k, shard in enumerate((t_pair, t_cross)):
                send(self.piece(shard), rq.at[self.k, k], at(d, t_pair), self.base + k)

        def middle(self):
            arrive(rq.at[self.k, 1], self.base + 1)
            fold(self.piece(t_far), [rq.at[self.k, 1]])
            send(self.piece(t_far), rq.at[self.k, 2], at(d, t_far), self.base + 2)

        def collect(self):
            for k in (0, 2):
                arrive(rq.at[self.k, k], self.base + k)
            total = self.piece(t)
            fold(total, [rq.at[self.k, 0], rq.at[self.k, 2]])
            spot = self.target.at[c, self.rows(q), :]
            self.copy = pltpu.make_async_copy(total, spot, local_sems.at[self.keep])
            self.copy.start()
            send(total, spot, at(d_x, t), self.to_x)
            send(total, spot, at(d_y, t), self.to_y)

        def relay(self):
            arrive(self.target.at[c, self.rows(qx), :], self.to_x)
            part = self.target.at[c, self.rows(qx, 0, 96), :]
            send(part, part, at(d_y, t), self.from_x)
            arrive(self.target.at[c, self.rows(qy), :], self.to_y)
            part = self.target.at[c, self.rows(qy, 96, 96), :]
            send(part, part, at(d_x, t), self.from_y)

        def swap(self):
            arrive(self.target.at[c, self.rows(qd, 0, 96), :], self.from_x)
            arrive(self.target.at[c, self.rows(qd, 96, 96), :], self.from_y)
            self.copy.wait()
            send(self.target.at[c], self.target.at[c], at(d_core, t), self.core)

        def end(self):
            arrive(self.target.at[1 - c], self.core)

    quarters = [Quarter(0, up_out), Quarter(1, down_out)]

    def quarter_grads(shard):
        own_rows = pl.ds(aligned(192 * q, 16), 192)
        qacc[...] = jnp.zeros_like(qacc)

        def row(r):
            def block(i, rows):
                section = s2all[r, pl.ds(rows, BLOCK), :]
                grad = zall[r, pl.ds(rows, BLOCK), :]
                upward = dot_nt(wf[0, shard, own_rows, :], section)
                cumulative = 0.5 * (1.0 + lax.erf(upward * (0.5**0.5)))
                density = jnp.exp(-0.5 * upward * upward) * 0.3989422804014327
                active = (upward * cumulative).astype(BF16)
                slope = cumulative + upward * density
                up_grad = (dot_nt(wf[1, shard, own_rows, :], grad) * slope).astype(BF16)
                for n in range(3):
                    cols = slice(256 * n, 256 * n + 256)
                    qacc[0, :, cols] += dot_nn(up_grad, section[:, cols])
                    qacc[1, :, cols] += dot_nn(active, grad[:, cols])

            blocks(block)

        times(4, row)
        for k in range(2):
            wf[k, shard, own_rows, :] = qacc[k].astype(BF16)

    def norm_back(upstream, index, slot, rows, target):
        normed = xh[slot, pl.ds(rows, BLOCK), :].astype(F32)
        nrm[pl.ds(index, 1), :] += jnp.sum(upstream * normed, axis=0, keepdims=True)
        nrm[pl.ds(index + 8, 1), :] += jnp.sum(upstream, axis=0, keepdims=True)
        scaled = upstream * gains[pl.ds(index, 1), :]
        grad = rstd[slot, pl.ds(rows, BLOCK), :] * (
            scaled
            - jnp.mean(scaled, axis=-1, keepdims=True)
            - normed * jnp.mean(scaled * normed, axis=-1, keepdims=True)
        )
        res[pl.ds(rows, BLOCK), :] = grad
        target[pl.ds(rows, BLOCK), :] = grad.astype(BF16)

    def out_back(i, rows):
        upstream = ogrow[pl.ds(aligned(own_base + rows, BLOCK), BLOCK), :].astype(F32)
        norm_back(upstream, 3 + c, 2, rows, zall.at[0])

    blocks(out_back)
    z3_begin()
    og_close()
    for device in (d_x, d_y):
        pl.semaphore_signal(credit.at[0], inc=1, device_id=at(device, t), device_id_type=MESH)

    def down_back(shard):
        def block(i, rows):
            left = zall[0, pl.ds(rows, BLOCK), :]
            for n in range(3):
                cols = slice(256 * n, 256 * n + 256)
                active_grad = dot_nt(left, wf[1, shard, cols, :])
                slope = gp[shard, pl.ds(rows, BLOCK), cols].astype(F32)
                gp[shard, pl.ds(rows, BLOCK), cols] = (active_grad * slope).astype(BF16)

        blocks(block)

    times(4, down_back)

    def up_input(i, rows):
        for n in range(3):
            cols = slice(256 * n, 256 * n + 256)
            total = res[pl.ds(rows, BLOCK), cols]
            for shard in range(4):
                total = total + dot_nn(gp[shard, pl.ds(rows, BLOCK), :], wf[0, shard, :, cols])
            acc[pl.ds(rows, BLOCK), cols] = total

    blocks(up_input)
    for device in (d_x, d_y):
        pl.semaphore_signal(credit.at[1], inc=1, device_id=at(device, t), device_id_type=MESH)

    blocks(lambda i, rows: norm_back(acc[pl.ds(rows, BLOCK), :], 1 + c, 1, rows, dzb))
    s2_relay()

    dctx = act.at[0]

    def context_back(which):
        def block(i, rows):
            left = dzb[pl.ds(rows, BLOCK), :]
            for n in range(3):
                cols = slice(256 * n, 256 * n + 256)
                dctx[pl.ds(rows, BLOCK), cols] = dot_nt(left, wa[which, 3, cols, :]).astype(BF16)

        blocks(block)

    def weight_rows(which, member, left_ref, rights):
        def tile(n):
            rows = aligned(n * 256, 256)
            for k in range(3):
                wide = slice(256 * k, 256 * k + 256)
                total = None
                for low, size, ref in rights:
                    term = dot_nn(
                        left_ref[pl.ds(rows, 256), low : low + size], ref[:, wide]
                    )
                    total = term if total is None else total + term
                wa[which, member, pl.ds(rows, 256), wide] = total.astype(BF16)

        times(3, tile)

    def attend_back(which, qkv, code_row, pairs):
        def pair(k, carry):
            lanes = pl.ds(aligned(k * 128, 128), 128)
            key = qkv[1, :, lanes]
            value = qkv[2, :, lanes]
            key_t = jnp.transpose(key)
            kv_acc[...] = jnp.zeros_like(kv_acc)

            def block(i, rows):
                query = qkv[0, pl.ds(rows, BLOCK), lanes] * jnp.asarray(scaling, BF16)
                grad = dctx[pl.ds(rows, BLOCK), lanes]
                query_code = codes[
                    pl.ds(code_row, 1), pl.ds(aligned(own_base + rows, BLOCK), BLOCK)
                ]
                allowed = kcode[which, :, 0:1] == query_code
                for h in range(2):
                    query_h = query * head_lanes[h]
                    grad_h = grad * head_lanes[h]
                    scores = jnp.where(allowed, dot_nt(key, query_h), -1e30)
                    probs = jnp.exp(
                        scores - lse[which, pl.ds(2 * k + h, 1), pl.ds(rows, BLOCK)]
                    )
                    probs_grad = dot_nt(value, grad_h)
                    delta = jnp.sum(probs * probs_grad, axis=0, keepdims=True)
                    score_grad = (probs * (probs_grad - delta)).astype(BF16)
                    kv_acc[0] += dot_nn(score_grad, query_h)
                    kv_acc[1] += dot_nn(probs.astype(BF16), grad_h)
                    tt[
                        0, pl.ds(aligned(k * 128 + h * 64, 64), 64), pl.ds(rows, BLOCK)
                    ] = (dot_nn(key_t[64 * h : 64 * h + 64, :], score_grad) * scaling).astype(BF16)

            blocks(block)
            for m in range(2):
                tt[1 + m, pl.ds(aligned(k * 128, 128), 128), :] = jnp.transpose(
                    kv_acc[m]
                ).astype(BF16)
            return carry

        lax.fori_loop(pairs[0], pairs[1], pair, 0)

    def pump(*steps):
        for step in steps:
            step()

    context_back(SELF)
    for wait in pending:
        wait()
    pending.clear()
    weight_rows(SELF, 3, ctx_t.at[1], [(0, 512, dzb)])
    attend_back(1, qkv2, 2, (0, 6))
    z3_relay()

    def self_input(i, rows):
        parts = [jnp.transpose(tt[m, :, pl.ds(rows, BLOCK)]) for m in range(3)]
        for n in range(3):
            cols = slice(256 * n, 256 * n + 256)
            total = res[pl.ds(rows, BLOCK), cols]
            for m in range(3):
                total = total + dot_nn(parts[m], wa[SELF, m, :, cols])
            acc[pl.ds(rows, BLOCK), cols] = total

    blocks(self_input)
    for m in range(3):
        weight_rows(SELF, m, tt.at[m], [(0, 512, sb)])
    pl.semaphore_wait(credit.at[1], 2)
    sum_self.start_all()
    pl.semaphore_signal(credit.at[2], inc=1, device_id=at(d_core, t), device_id_type=MESH)

    s2_finish()
    z3_finish()
    quarter_grads(t_pair)
    quarter_grads(t_cross)
    pump(*[one.start for one in quarters])
    quarter_grads(t_far)

    blocks(lambda i, rows: norm_back(acc[pl.ds(rows, BLOCK), :], 0, 0, rows, dzb))

    norm_ids = [new_id() for _ in range(5)]
    norm_ways = [
        at(d_core, t),
        at(d_x, t),
        at(d_y, t),
        at(d, t + 1 - 2 * (t % 2)),
        at(d, (t + 2) % 4),
    ]
    norm_steps = []

    def norm_begin(k):
        send(nrm if k == 0 else nrm_recv.at[k - 1, 1], nrm_recv.at[k, 0], norm_ways[k], norm_ids[k])

    def norm_step(k):
        arrive(nrm_recv.at[k, 0], norm_ids[k])
        mine = nrm[...] if k == 0 else nrm_recv[k - 1, 1]
        total = mine + nrm_recv[k, 0]
        if k < 4:
            nrm_recv[k, 1] = total
            norm_begin(k + 1)
        else:
            norm_out[...] = total

    norm_begin(0)
    context_back(CROSS)
    weight_rows(CROSS, 3, ctx_t.at[0], [(0, 512, dzb)])
    norm_step(0)
    attend_back(0, qkv1, 0, (0, 3))
    norm_step(1)
    pump(*sum_self.both(sum_self.stage2))
    attend_back(0, qkv1, 0, (3, 6))
    norm_step(2)
    pump(*[one.middle for one in quarters])

    key_ids = [new_id() for _ in range(2)]

    def key_input(j):
        parts = [jnp.transpose(tt[m, :, 256 * j : 256 * j + 256]) for m in (1, 2)]
        for n in range(3):
            cols = slice(256 * n, 256 * n + 256)
            act[1, 256 * j : 256 * j + 256, cols] = (
                dot_nn(parts[0], wa[CROSS, 1, :, cols]) + dot_nn(parts[1], wa[CROSS, 2, :, cols])
            ).astype(BF16)

    key_input(0)
    key_input(1)
    key_copies = [
        remote(
            act.at[1, pl.ds(256 * j, 256), :],
            dhk_recv.at[j],
            at(d_core, t),
            key_ids[j],
        )
        for j in range(2)
    ]
    key_copies[0].start()

    @pl.when(c == 0)
    def _():
        key_copies[1].start()

    def cross_input(i, rows):
        part = jnp.transpose(tt[0, :, pl.ds(rows, BLOCK)])
        for n in range(3):
            cols = slice(256 * n, 256 * n + 256)
            res[pl.ds(rows, BLOCK), cols] += dot_nn(part, wa[CROSS, 0, :, cols])

    blocks(cross_input)
    weight_rows(CROSS, 0, tt.at[0], [(0, 512, xrow.at[pl.ds(own_base, 512), :])])
    for m in range(1, 3):
        weight_rows(
            CROSS,
            m,
            tt.at[m],
            [
                (0, 256, xrow.at[pl.ds(other_base, 256), :]),
                (256, 256, xrow.at[pl.ds(512, 256), :]),
            ],
        )

    pump(*sum_self.both(sum_self.stage3))

    pl.semaphore_wait(credit.at[2], 1)
    core_sums = [(a, n, new_id()) for a in range(2) for n in range(3)]

    def core_slot(a, n):
        k = 3 * a + n
        return qkv2.at[k // 2, pl.ds(256 * (k % 2), 256), :]

    for a, n, ident in core_sums:
        send(
            wa.at[CROSS, 2 * (1 - c) + a, pl.ds(256 * n, 256), :],
            core_slot(a, n),
            at(d_core, t),
            ident,
        )
    norm_step(3)

    y_close()
    arrive(dhk_recv.at[0], key_ids[0])

    @pl.when(c == 1)
    def _():
        arrive(dhk_recv.at[1], key_ids[1])

    yb[:BLOCK, :] = (res[:BLOCK, :] + dhk_recv[0].astype(F32)).astype(BF16)

    @pl.when(c == 1)
    def _():
        own_part = act[1, BLOCK:, :].astype(F32)
        yb[BLOCK:, :] = (res[BLOCK:, :] + dhk_recv[1].astype(F32) + own_part).astype(BF16)

    dx_begin, dx_close = return_row(dx_out)

    for a, n, ident in core_sums:
        arrive(core_slot(a, n), ident)
        fold(wa.at[CROSS, 2 * c + a, pl.ds(256 * n, 256), :], [core_slot(a, n)])
    pl.semaphore_wait(credit.at[0], 2)
    sum_cross.start_all()
    norm_step(4)
    quarter_grads(t)
    pump(
        *[one.collect for one in quarters],
        *sum_cross.both(sum_cross.stage2),
        *sum_self.both(sum_self.stage4),
        *[one.relay for one in quarters],
        *sum_cross.both(sum_cross.stage3),
        dx_begin,
        *sum_self.both(sum_self.stage4_end),
        *sum_cross.both(sum_cross.stage4),
        *[one.swap for one in quarters],
        sum_self.stage5,
        *sum_cross.both(sum_cross.stage4_end),
        sum_self.stage6,
        sum_cross.stage5,
        sum_cross.stage6,
        *[one.end for one in quarters],
        sum_self.stage7,
        sum_cross.stage7,
    )
    for wait in pending + late:
        wait()
    key_copies[0].wait_send()

    @pl.when(c == 0)
    def _():
        key_copies[1].wait_send()

    dx_close()
    if counter[0] > SEMAPHORES or local_counter[0] > LOCALS:
        raise ValueError((counter[0], local_counter[0]))


SEMAPHORES = 320
LOCALS = 40


def call_layer(*operands):
    def vmem(shape, dtype=BF16):
        return pltpu.VMEM(shape, dtype)

    anywhere = pl.BlockSpec(memory_space=pl.ANY)
    whole = pl.BlockSpec(memory_space=pltpu.VMEM)
    x_in = operands[0]
    return pl.pallas_call(
        layer_kernel,
        name="cross_modality_layer",
        out_shape=(
            jax.ShapeDtypeStruct(x_in.shape, BF16),
            jax.ShapeDtypeStruct(x_in.shape, BF16),
            jax.ShapeDtypeStruct((4, 192, 768), BF16),
            jax.ShapeDtypeStruct((2, 4, 192, 768), BF16),
            jax.ShapeDtypeStruct((2, 768, 768), BF16),
            jax.ShapeDtypeStruct((2, 768, 768), BF16),
            jax.ShapeDtypeStruct((16, 768), F32),
        ),
        in_specs=[anywhere] * 9 + [whole] * 2,
        out_specs=(anywhere,) * 6 + (whole,),
        scratch_shapes=[
            vmem((2, 4, 768, 768)),
            vmem((2, 4, 768, 768)),
            vmem((768, 768)),
            vmem((768, 768)),
            vmem((8, 768), F32),
            vmem((2, 512, 128), F32),
            vmem((3, 512, 768)),
            vmem((3, 512, 768)),
            vmem((2, 768, 512)),
            vmem((2, 16, 512), F32),
            vmem((3, 512, 768)),
            vmem((3, 512, 1), F32),
            vmem((512, 768)),
            vmem((512, 768), F32),
            vmem((512, 768), F32),
            vmem((4, 512, 768)),
            vmem((4, 512, 768)),
            vmem((512, 768)),
            vmem((3, 768, 512)),
            vmem((512, 768)),
            vmem((2, 256, 768)),
            vmem((2, 512, 128), F32),
            vmem((16, 768), F32),
            vmem((5, 2, 16, 768), F32),
            vmem((4, 512, 768)),
            vmem((4, 512, 768)),
            vmem((2, 192, 768), F32),
            vmem((2, 3, 192, 768)),
            vmem((2, 4, 2, 48, 768)),
            vmem((3, 2, 2, 48, 768)),
            vmem((2, 4, 48, 768)),
            vmem((3, 2, 48, 768)),
            pltpu.SemaphoreType.DMA((SEMAPHORES,)),
            pltpu.SemaphoreType.DMA((SEMAPHORES,)),
            pltpu.SemaphoreType.DMA((LOCALS,)),
            pltpu.SemaphoreType.REGULAR((3,)),
        ],
        compiler_params=pltpu.CompilerParams(
            collective_id=0, has_side_effects=True, vmem_limit_bytes=64 * 1024 * 1024 - 512 * 1024
        ),
    )(*operands)


def results_kernel(
    cross, own, up, down, dx, norm,
    dx_out, cross_qkv, cross_out, self_qkv, self_out, up_out, down_out, gains, biases,
    v_cross, v_own, v_up, v_down, v_dx, v_norm,
    w_dx, w_cross_qkv, w_cross_out, w_self_qkv, w_self_out, w_up, w_down,
    in_sems, out_sems,
):
    sources = [
        (down.at[0], v_down.at[0]),
        (down.at[1], v_down.at[1]),
        (up.at[0], v_up.at[0]),
        (up.at[1], v_up.at[1]),
        (own.at[0], v_own.at[0]),
        (own.at[1], v_own.at[1]),
        (cross, v_cross),
        (dx, v_dx),
        (norm, v_norm),
    ]
    loads = [
        pltpu.make_async_copy(src, dst, in_sems.at[k]) for k, (src, dst) in enumerate(sources)
    ]
    for load in loads:
        load.start()
    stores = []

    def store(src, dst):
        copy = pltpu.make_async_copy(src, dst, out_sems.at[len(stores)])
        copy.start()
        stores.append(copy)

    for k in range(2):
        loads[k].wait()
        w_down[k] = v_down[k].astype(F32)
        store(w_down.at[k], down_out.at[k])
    for k in range(2):
        loads[2 + k].wait()
        for n in range(3):
            cols = slice(256 * n, 256 * n + 256)
            w_up[k, cols, :] = jnp.transpose(v_up[k, :, cols]).astype(F32)
        store(w_up.at[k], up_out.at[k])
    for k in range(2):
        loads[4 + k].wait()
        for n in range(3):
            w_self_qkv[k, n] = v_own[k, n].astype(F32)
        w_self_out[k] = v_own[k, 3].astype(F32)
        store(w_self_qkv.at[k], self_qkv.at[k])
        store(w_self_out.at[k], self_out.at[k])
    loads[6].wait()
    for n in range(3):
        w_cross_qkv[n] = v_cross[n].astype(F32)
    w_cross_out[...] = v_cross[3].astype(F32)
    store(w_cross_qkv, cross_qkv)
    store(w_cross_out, cross_out)
    loads[7].wait()
    w_dx[...] = v_dx[...].astype(F32)
    store(w_dx, dx_out)
    loads[8].wait()
    gains[...] = v_norm[0:5, :]
    biases[...] = v_norm[8:13, :]
    for copy in stores:
        copy.wait()


def call_results(cross, own, up, down, dx, norm):
    anywhere = pl.BlockSpec(memory_space=pl.ANY)
    whole = pl.BlockSpec(memory_space=pltpu.VMEM)

    def out(shape):
        return jax.ShapeDtypeStruct(shape, F32)

    shapes = [
        dx.shape,
        (3, 192, 768),
        (192, 768),
        (2, 3, 192, 768),
        (2, 192, 768),
        (2, 768, 768),
        (2, 768, 768),
    ]
    return pl.pallas_call(
        results_kernel,
        name="results",
        out_shape=tuple(out(shape) for shape in shapes) + (out((5, 768)), out((5, 768))),
        in_specs=[anywhere] * 6,
        out_specs=(anywhere,) * 7 + (whole,) * 2,
        scratch_shapes=[pltpu.VMEM(ref.shape, ref.dtype) for ref in (cross, own, up, down, dx, norm)]
        + [pltpu.VMEM(shape, F32) for shape in shapes]
        + [pltpu.SemaphoreType.DMA((9,)), pltpu.SemaphoreType.DMA((11,))],
        compiler_params=pltpu.CompilerParams(vmem_limit_bytes=56 * 1024 * 1024),
    )(cross, own, up, down, dx, norm)


def solution(mesh):
    extra = []
    step = 8
    while step < mesh.shape["dp"]:
        extra.append(step)
        step *= 2

    def total(array):
        for step in extra:
            pairs = [(k, k ^ step) for k in range(mesh.shape["dp"])]
            array = array + lax.ppermute(array, "dp", pairs)
        return array

    def body(
        layer_input,
        word_segments,
        image_order,
        cross_qkv,
        cross_out,
        self_qkv,
        self_out,
        ffn_up,
        ffn_down,
        norm_gains,
        norm_biases,
        out_grad,
    ):
        rows = layer_input.shape[0]
        images = jnp.repeat(image_order, BOXES, axis=1)
        pads = jnp.full((rows, PADS), CAPTIONS, jnp.int32)
        none = jnp.full((rows, WORDS + REGIONS + PADS), -1, jnp.int32)
        groups = jnp.concatenate([word_segments, images, pads], axis=1)
        keys = jnp.concatenate([word_segments, none[:, :REGIONS], pads], axis=1)
        kinds = jnp.concatenate([word_segments, images + 16, pads + 32], axis=1)
        codes = jnp.stack([groups, keys, kinds, none, none, none, none, none], axis=1).astype(F32)
        y, dx, d_cross, d_self, d_up, d_down, d_norm = call_layer(
            layer_input,
            out_grad,
            codes,
            jnp.swapaxes(cross_qkv, 1, 2),
            cross_out,
            jnp.swapaxes(self_qkv, 2, 3),
            self_out,
            ffn_up,
            ffn_down,
            norm_gains,
            norm_biases,
        )
        dx, *grads = call_results(d_cross, d_self, d_up, d_down, dx, d_norm)
        grads = [total(array) for array in grads]
        grads[0] = jnp.swapaxes(grads[0], 1, 2)
        grads[2] = jnp.swapaxes(grads[2], 2, 3)
        return (y, dx, *grads)

    in_specs = (
        P("dp", "tensor", None),
        P("dp", None),
        P("dp", None),
        P(None, None, "tensor"),
        P("tensor", None),
        P(None, None, None, "tensor"),
        P(None, "tensor", None),
        P(None, None, "tensor"),
        P(None, "tensor", None),
        P(),
        P(),
        P("dp", "tensor", None),
    )
    out_specs = (
        P("dp", "tensor", None),
        P("dp", "tensor", None),
        P(None, None, "tensor"),
        P("tensor", None),
        P(None, None, None, "tensor"),
        P(None, "tensor", None),
        P(None, None, "tensor"),
        P(None, "tensor", None),
        P(),
        P(),
    )
    return jax.shard_map(body, mesh=mesh, in_specs=in_specs, out_specs=out_specs, check_vma=False)
```

```python
import functools

import jax
import jax.numpy as jnp
from jax import lax
from jax.experimental import pallas as pl
from jax.experimental.pallas import tpu as pltpu
from jax.sharding import PartitionSpec as P

HEAD_DIM = 64
WORDS = 256
CAPTIONS = 14
BOXES = 36
REGIONS = 504
PADS = 8
NORM_EPSILON = 1e-12
BLOCK = 256
BF16 = jnp.bfloat16
F32 = jnp.float32
MESH = pl.DeviceIdType.MESH
CROSS, SELF, UP, DOWN = 0, 1, 2, 3


def dot_nn(left, right):
    return jnp.dot(left, right, preferred_element_type=F32)


def dot_nt(left, right):
    return lax.dot_general(left, right, (((1,), (1,)), ((), ())), preferred_element_type=F32)


def aligned(value, step):
    return pl.multiple_of(value, step)


def layer_kernel(
    x_in,
    og_in,
    codes_in,
    cross_in,
    cross_out_in,
    self_in,
    self_out_in,
    up_in,
    down_in,
    gains,
    biases,
    y_out,
    dx_out,
    cross_out,
    self_out,
    up_out,
    down_out,
    norm_out,
    wa,
    wf,
    xrow,
    ogrow,
    codes,
    kcode,
    qkv1,
    qkv2,
    ctx_t,
    lse,
    xh,
    rstd,
    sb,
    res,
    acc,
    act,
    gp,
    dzb,
    tt,
    yb,
    dhk_recv,
    kv_acc,
    nrm,
    nrm_recv,
    s2all,
    zall,
    units,
    rq,
    r2s,
    r3s,
    r2c,
    r3c,
    send_sems,
    recv_sems,
    local_sems,
    credit,
):
    d = lax.axis_index("dp")
    t = lax.axis_index("tensor")
    c = d % 2
    px = (d // 2) % 2
    py = (d // 4) % 2
    q = px + 2 * py
    d_core = d + 1 - 2 * c
    d_x = d + 2 - 4 * px
    d_y = d + 4 - 8 * py
    holder = t // 2
    d_holder = d - c + holder
    turn = t % 2
    nb = 1 + c
    near = {"x": d_x, "y": d_y, "core": d_core}

    def at(dp_index, tensor_index):
        return {"dp": dp_index, "tensor": tensor_index}

    counter = [0]
    local_counter = [0]
    pending = []

    def new_id(count=1):
        counter[0] += count
        return counter[0] - count

    def remote(src, dst, device, ident, arrival=None):
        return pltpu.make_async_remote_copy(
            src_ref=src,
            dst_ref=dst,
            send_sem=send_sems.at[ident],
            recv_sem=recv_sems.at[ident if arrival is None else arrival],
            device_id=device,
            device_id_type=MESH,
        )

    def send(src, dst, device, ident):
        copy = remote(src, dst, device, ident)
        copy.start()
        pending.append(copy.wait_send)

    def arrive(dst, ident):
        remote(dst, dst, at(d_core, t), ident).wait_recv()

    def local(src, dst):
        copy = pltpu.make_async_copy(src, dst, local_sems.at[local_counter[0]])
        local_counter[0] += 1
        return copy

    def blocks(body):
        def step(i, carry):
            body(i, aligned(i * BLOCK, BLOCK))
            return carry

        lax.fori_loop(0, nb, step, 0)

    def times(count, body):
        def step(i, carry):
            body(i)
            return carry

        lax.fori_loop(0, count, step, 0)

    barrier = pltpu.get_barrier_semaphore()
    partners = [at(d_core, t), at(d_x, t), at(d_y, t)]
    for m in range(1, 4):
        partners.append(at(d, (t + m) % 4))
        partners.append(at(d_core, (t + m) % 4))
    for partner in partners:
        pl.semaphore_signal(barrier, inc=1, device_id=partner, device_id_type=MESH)

    half_rows = aligned(t * 192, 16)
    own_copies = [
        local(cross_out_in, wa.at[CROSS, 3, pl.ds(half_rows, 192), :]),
        local(self_out_in.at[c], wa.at[SELF, 3, pl.ds(half_rows, 192), :]),
        local(down_in.at[c], wf.at[1, t]),
    ]
    raw_copies = [
        local(cross_in, wa.at[CROSS, pl.ds(0, 3), pl.ds(half_rows, 192), :]),
        local(self_in.at[c], wa.at[SELF, pl.ds(0, 3), pl.ds(half_rows, 192), :]),
    ]
    up_copies = [
        local(up_in.at[c, pl.ds(0, 512), :], qkv1.at[0]),
        local(up_in.at[c, pl.ds(512, 256), :], qkv1.at[1, pl.ds(0, 256), :]),
    ]
    for copy in raw_copies + own_copies + up_copies:
        copy.start()

    zero_half = jnp.zeros((BLOCK, 768), BF16)

    @pl.when(c == 0)
    def _():
        for ref in (qkv2.at[1], qkv2.at[2], sb, dzb):
            ref[BLOCK:, :] = zero_half
        for k in range(2):
            ctx_t[k, :, BLOCK:] = jnp.zeros((768, BLOCK), BF16)
        tt[0, :, BLOCK:] = jnp.zeros((768, BLOCK), BF16)
        for r in range(4):
            s2all[r, BLOCK:, :] = zero_half
            zall[r, BLOCK:, :] = zero_half
            for k in range(2):
                units[k, :, 512 * r + BLOCK : 512 * r + 512] = jnp.zeros((192, BLOCK), BF16)

    nrm[...] = jnp.zeros_like(nrm)
    for g in (CROSS, SELF):
        raw_copies[g].wait()
        own_copies[g].wait()
    pl.semaphore_wait(barrier, len(partners))

    def spread_row(source, row):
        base = new_id(4)
        core_base = new_id(4)
        own = local(source.at[turn], row.at[pl.ds(half_rows, 192), :])

        def each_target(action):
            for r in range(2):
                target = 2 * c + r

                @pl.when(target != t)
                def _():
                    action(
                        remote(
                            source.at[r],
                            row.at[pl.ds(half_rows, 192), :],
                            at(d, target),
                            base + r,
                            base + t,
                        )
                    )

        def each_relay(action):
            @pl.when(holder == c)
            def _():
                for s in range(4):
                    part = row.at[pl.ds(192 * s, 192), :]
                    action(s, part, remote(part, part, at(d_core, t), core_base + s))

        def begin():
            each_target(lambda copy: copy.start())

            @pl.when(holder == c)
            def _():
                own.start()

        def relay():
            def action(s, part, copy):
                @pl.when(t == s)
                def _():
                    own.wait()

                @pl.when(t != s)
                def _():
                    arrive(part, base + s)

                copy.start()

            each_relay(action)

        def finish():
            @pl.when(holder != c)
            def _():
                for s in range(4):
                    arrive(row.at[pl.ds(192 * s, 192), :], core_base + s)

        def close():
            each_target(lambda copy: copy.wait_send())
            each_relay(lambda s, part, copy: copy.wait_send())

        return begin, relay, finish, close

    x_begin, x_relay, x_finish, x_close = spread_row(x_in, xrow)
    og_begin, og_relay, og_finish, og_close = spread_row(og_in, ogrow)
    pending.append(x_close)

    code_ident = new_id()
    code_own = local(codes_in.at[turn], codes)

    @pl.when(holder == c)
    def _():
        code_own.start()
        remote(codes_in.at[turn], codes, at(d_core, t), code_ident).start()

    def share(g, shard, quarter, low, high):
        if g >= UP:
            rows = aligned(quarter * 192 + low * 96, 16)
            return wf.at[g - UP, shard, pl.ds(rows, (high - low) * 96), :]
        rows = aligned(shard * 192 + quarter * 48, 16)
        if g == SELF:
            return wa.at[SELF, pl.ds(2 * low, 2 * (high - low)), pl.ds(rows, 48), :]
        return wa.at[CROSS, pl.ds(2 * c + low, high - low), pl.ds(rows, 48), :]

    def own_share(g):
        if g >= UP:
            rows = pl.ds(aligned(q * 192, 16), 192)
            return wf.at[0, t, rows, :] if g == UP else down_in.at[c, rows, :]
        return share(g, t, q, 0, 2)

    qx, qy = (1 - px) + 2 * py, px + 2 * (1 - py)
    qd = (1 - px) + 2 * (1 - py)
    items = [(g, m) for g in (CROSS, SELF, UP, DOWN) for m in range(1, 4)]
    z_base = {g: new_id(4) for g in (CROSS, SELF, UP, DOWN)}
    own_ids = {g: new_id(2) for g in (CROSS, SELF, UP, DOWN)}
    pass_ids = {item: new_id() for item in items}
    x_ids = {item: new_id() for item in items}
    y_ids = {item: new_id() for item in items}
    fx_ids = {item: new_id() for item in items}
    fy_ids = {item: new_id() for item in items}
    core_ids = {m: new_id() for m in range(1, 4)}
    arrivals = {
        1: t + 1 - 2 * (t % 2),
        2: 2 - t // 2,
        3: 3 - 3 * (t // 2),
    }

    def z_way(g, way):
        exists = t > 0 if way == 0 else t < 3
        target = t - 1 + 2 * way

        def copy():
            return remote(
                own_share(g),
                share(g, t, q, 0, 2),
                at(d, target),
                own_ids[g] + way,
                z_base[g] + t,
            )

        @pl.when(exists)
        def _():
            copy().start()

        def close():
            @pl.when(exists)
            def _():
                copy().wait_send()

        pending.append(close)

    def z_own(g):
        for way in range(2):
            z_way(g, way)

    def first(item):
        g, m = item
        shard = arrivals[m]
        piece = share(g, shard, q, 0, 2)
        arrive(piece, z_base[g] + shard)
        inner = jnp.logical_and(t > 0, t < 3)
        target = jnp.where(shard < t, t + 1, t - 1)

        def copy():
            return remote(piece, piece, at(d, target), pass_ids[item], z_base[g] + shard)

        @pl.when(inner)
        def _():
            copy().start()

        def close():
            @pl.when(inner)
            def _():
                copy().wait_send()

        pending.append(close)
        send(piece, piece, at(d_x, t), x_ids[item])
        send(piece, piece, at(d_y, t), y_ids[item])
        if (g, m) == (CROSS, 3):
            for part in up_copies:
                part.wait()
            wf[0, t, :, 0:512] = jnp.transpose(qkv1[0])
            wf[0, t, :, 512:768] = jnp.transpose(qkv1[1, 0:256, :])
        if m == 1 and g < DOWN:
            z_own(g + 1)
        if g == CROSS and m == 1:
            x_begin()
        if item == (DOWN, 1):
            og_begin()

    def second(item):
        g, m = item
        shard = arrivals[m]
        arrive(share(g, shard, qx, 0, 2), x_ids[item])
        low = share(g, shard, qx, 0, 1)
        send(low, low, at(d_y, t), fy_ids[item])
        arrive(share(g, shard, qy, 0, 2), y_ids[item])
        high = share(g, shard, qy, 1, 2)
        send(high, high, at(d_x, t), fx_ids[item])

    def third(item):
        g, m = item
        shard = arrivals[m]
        arrive(share(g, shard, qd, 0, 1), fy_ids[item])
        arrive(share(g, shard, qd, 1, 2), fx_ids[item])
        if g == CROSS:
            rows = pl.ds(aligned(shard * 192, 16), 192)
            whole = wa.at[CROSS, pl.ds(2 * c, 2), rows, :]
            send(whole, whole, at(d_core, t), core_ids[m])

    def last(m):
        shard = arrivals[m]
        rows = pl.ds(aligned(shard * 192, 16), 192)
        arrive(wa.at[CROSS, pl.ds(2 * (1 - c), 2), rows, :], core_ids[m])

    z_own(CROSS)

    steps = []
    position = {}
    for k in range(len(items) + 2):
        if k < len(items):
            steps.append(functools.partial(first, items[k]))
        if 0 <= k - 1 < len(items):
            steps.append(functools.partial(second, items[k - 1]))
        if 0 <= k - 2 < len(items):
            steps.append(functools.partial(third, items[k - 2]))
            position[items[k - 2]] = len(steps)
    done = [0]

    def advance(upto):
        while done[0] < min(upto, len(steps)):
            steps[done[0]]()
            done[0] += 1

    advance(position[(CROSS, 2)])
    x_relay()
    x_finish()

    @pl.when(holder == c)
    def _():
        code_own.wait()
        remote(codes_in.at[turn], codes, at(d_core, t), code_ident).wait_send()

    @pl.when(holder != c)
    def _():
        arrive(codes, code_ident)

    def as_column(row):
        return jnp.transpose(jnp.broadcast_to(row, (128, BLOCK)))

    own_base = aligned(c * BLOCK, BLOCK)
    other_base = aligned((1 - c) * BLOCK, BLOCK)
    kcode[0, :BLOCK, :] = as_column(codes[0:1, pl.ds(other_base, BLOCK)])
    kcode[0, BLOCK:, :] = as_column(codes[pl.ds(c, 1), 512:768])
    kcode[1, :BLOCK, :] = as_column(codes[2:3, pl.ds(own_base, BLOCK)])
    kcode[1, BLOCK:, :] = as_column(codes[pl.ds(3 - c, 1), 512:768])

    lane = lax.broadcasted_iota(jnp.int32, (1, 128), 1)
    head_lanes = [
        (lane < HEAD_DIM).astype(F32).astype(BF16),
        (lane >= HEAD_DIM).astype(F32).astype(BF16),
    ]
    scaling = HEAD_DIM ** (-0.5)

    def project(source, base, weight, target, rows):
        left = source[pl.ds(base, BLOCK), :]
        for n in range(3):
            target[pl.ds(rows, BLOCK), 256 * n : 256 * n + 256] = dot_nt(
                left, weight[256 * n : 256 * n + 256, :]
            ).astype(BF16)

    def query_blocks(which, piece):
        if which == SELF:
            blocks(lambda i, rows: piece(rows, [pl.ds(aligned(i * 128, 128), SPAN)]))
            return

        @pl.when(c == 0)
        def _():
            piece(0, [pl.ds(0, 512)])

        @pl.when(c == 1)
        def _():
            piece(0, [pl.ds(0, 256)])
            piece(BLOCK, [pl.ds(0, 256), pl.ds(384, 128)])

    def gathered(ref, spans, *rest):
        parts = [ref[(span, *rest)] for span in spans]
        return parts[0] if len(parts) == 1 else jnp.concatenate(parts, axis=0)

    def attend(which, qkv, code_row, pairs):
        def pair(k):
            lanes = pl.ds(aligned(k * 128, 128), 128)

            def piece(rows, spans):
                key = gathered(qkv.at[1], spans, lanes)
                value_t = jnp.transpose(gathered(qkv.at[2], spans, lanes))
                query = qkv[0, pl.ds(rows, BLOCK), lanes] * jnp.asarray(scaling, BF16)
                query_code = codes[
                    pl.ds(code_row, 1), pl.ds(aligned(own_base + rows, BLOCK), BLOCK)
                ]
                allowed = gathered(kcode.at[which], spans, slice(None))[:, 0:1] == query_code
                for h in range(2):
                    scores = dot_nt(key, query * head_lanes[h])
                    scores = jnp.where(allowed, scores, -1e30)
                    top = jnp.max(scores, axis=0, keepdims=True)
                    exponent = jnp.exp(scores - top)
                    total = jnp.sum(exponent, axis=0, keepdims=True)
                    probs = (exponent * (1.0 / total)).astype(BF16)
                    lse[which, pl.ds(2 * k + h, 1), pl.ds(rows, BLOCK)] = top + jnp.log(total)
                    ctx_t[
                        which,
                        pl.ds(aligned(k * 128 + h * 64, 64), 64),
                        pl.ds(rows, BLOCK),
                    ] = dot_nn(value_t[64 * h : 64 * h + 64, :], probs).astype(BF16)

            query_blocks(which, piece)

        def run(k, carry):
            pair(k)
            return carry

        lax.fori_loop(pairs[0], pairs[1], run, 0)

    def normalize(summed, index, slot, rows):
        center = summed - jnp.mean(summed, axis=-1, keepdims=True)
        inverse = lax.rsqrt(jnp.mean(center * center, axis=-1, keepdims=True) + NORM_EPSILON)
        normed = center * inverse
        xh[slot, pl.ds(rows, BLOCK), :] = normed.astype(BF16)
        rstd[slot, pl.ds(rows, BLOCK), :] = inverse
        return normed * gains[pl.ds(index, 1), :] + biases[pl.ds(index, 1), :]

    def attention_out(which, rows):
        context = jnp.transpose(ctx_t[which, :, pl.ds(rows, BLOCK)])
        return dot_nn(context, wa[which, 3])

    advance(position[(CROSS, 3)])
    for m in range(1, 4):
        last(m)
    blocks(lambda i, rows: project(xrow, own_base + rows, wa.at[CROSS, 0], qkv1.at[0], rows))
    for k in range(1, 3):
        project(xrow, other_base, wa.at[CROSS, k], qkv1.at[k], 0)
        project(xrow, 512, wa.at[CROSS, k], qkv1.at[k], BLOCK)
    attend(0, qkv1, 0, (0, 3))
    advance(position[(SELF, 1)])
    attend(0, qkv1, 0, (3, 6))
    advance(position[(SELF, 2)])

    def cross_end(i, rows):
        stream = xrow[pl.ds(aligned(own_base + rows, BLOCK), BLOCK), :].astype(F32)
        section = normalize(stream + attention_out(0, rows), 0, 0, rows)
        res[pl.ds(rows, BLOCK), :] = section
        sb[pl.ds(rows, BLOCK), :] = section.astype(BF16)

    blocks(cross_end)

    advance(position[(SELF, 3)])
    for k in range(3):
        blocks(lambda i, rows: project(sb, rows, wa.at[SELF, k], qkv2.at[k], rows))
    attend(1, qkv2, 2, (0, 3))
    advance(position[(UP, 1)])
    attend(1, qkv2, 2, (3, 6))
    advance(position[(UP, 2)])

    def self_end(i, rows):
        summed = res[pl.ds(rows, BLOCK), :] + attention_out(1, rows)
        section = normalize(summed, 1 + c, 1, rows)
        res[pl.ds(rows, BLOCK), :] = section
        s2all[0, pl.ds(rows, BLOCK), :] = section.astype(BF16)

    blocks(self_end)

    late = []

    def plane_gather(buffer):
        to_x, to_y, from_x, from_y = new_id(), new_id(), new_id(), new_id()

        def sized(action):
            for core in range(2):

                @pl.when(c == core)
                def _():
                    action(BLOCK * (core + 1))

        def part(k, low, size):
            return buffer.at[k, pl.ds(low, size), :]

        def firsts(size):
            return [
                remote(part(0, 0, size), part(1, 0, size), at(d_x, t), to_x),
                remote(part(0, 0, size), part(2, 0, size), at(d_y, t), to_y),
            ]

        def seconds(size):
            half = size // 2
            return [
                remote(part(1, 0, half), part(3, 0, half), at(d_y, t), from_x),
                remote(part(2, half, half), part(3, half, half), at(d_x, t), from_y),
            ]

        def begin():
            sized(lambda size: [copy.start() for copy in firsts(size)])

        def relay():
            def action(size):
                onward = seconds(size)
                arrive(part(1, 0, size), to_x)
                onward[0].start()
                arrive(part(2, 0, size), to_y)
                onward[1].start()

            sized(action)

        def finish():
            def action(size):
                half = size // 2
                arrive(part(3, 0, half), from_x)
                arrive(part(3, half, half), from_y)

            sized(action)

        def close():
            sized(lambda size: [copy.wait_send() for copy in firsts(size) + seconds(size)])

        late.append(close)
        return begin, relay, finish

    s2_begin, s2_relay, s2_finish = plane_gather(s2all)
    z3_begin, z3_relay, z3_finish = plane_gather(zall)
    def feed_up(shard):
        def block(i, rows):
            left = s2all[0, pl.ds(rows, BLOCK), :]
            for n in range(3):
                cols = slice(256 * n, 256 * n + 256)
                upward = dot_nt(left, wf[0, shard, cols, :])
                cumulative = 0.5 * (1.0 + lax.erf(upward * (0.5**0.5)))
                density = jnp.exp(-0.5 * upward * upward) * 0.3989422804014327
                act[shard, pl.ds(rows, BLOCK), cols] = (upward * cumulative).astype(BF16)
                gp[shard, pl.ds(rows, BLOCK), cols] = (cumulative + upward * density).astype(BF16)

        blocks(block)

    feed_up(t)
    for m in range(1, 4):
        advance(position[(UP, m)])
        feed_up(arrivals[m])

    def feed_down(shard):
        def block(i, rows):
            left = act[shard, pl.ds(rows, BLOCK), :]
            for n in range(3):
                cols = slice(256 * n, 256 * n + 256)
                res[pl.ds(rows, BLOCK), cols] += dot_nn(left, wf[1, shard, :, cols])

        blocks(block)

    own_copies[2].wait()
    feed_down(t)
    for m in range(1, 4):
        advance(position[(DOWN, m)])
        if m == 3:
            s2_begin()
            og_relay()
        feed_down(arrivals[m])

    def layer_end(i, rows):
        result = normalize(res[pl.ds(rows, BLOCK), :], 3 + c, 2, rows)
        yb[pl.ds(rows, BLOCK), :] = result.astype(BF16)

    blocks(layer_end)

    def return_row(target):
        idents = [[new_id() for _ in range(3)] for _ in range(2)]
        send_base = new_id(12)
        local_ids = [local_counter[0] + k for k in range(3)]
        local_counter[0] += 3

        def each(action):
            for k in range(12):
                source_core = 0 if k < 4 else 1
                slots, part = k // 3, k % 3
                src = yb.at[pl.ds(64 * k - 256 * source_core, 64), :]
                for r in range(2):
                    dst = target.at[r, pl.ds(64 * part, 64), :]
                    mine = jnp.logical_and(c == source_core, turn == r)
                    here = jnp.logical_and(holder == c, t == slots)

                    @pl.when(jnp.logical_and(mine, here))
                    def _():
                        copy = pltpu.make_async_copy(src, dst, local_sems.at[local_ids[part]])
                        if action == "start":
                            copy.start()
                        elif action == "wait":
                            copy.wait()

                    @pl.when(jnp.logical_and(mine, jnp.logical_not(here)))
                    def _():
                        copy = remote(
                            src, dst, at(d_holder, slots), send_base + k, idents[r][part]
                        )
                        if action == "start":
                            copy.start()
                        elif action == "wait":
                            copy.wait_send()

        def begin():
            each("start")

        def close():
            each("wait")
            for r in range(2):
                for part in range(3):
                    dst = target.at[r, pl.ds(64 * part, 64), :]
                    k = 3 * t + part
                    source_core = jnp.where(k < 4, 0, 1)
                    from_here = jnp.logical_and(
                        jnp.logical_and(source_core == c, turn == r), holder == c
                    )

                    @pl.when(jnp.logical_not(from_here))
                    def _():
                        arrive(dst, idents[r][part])

        return begin, close

    y_begin, y_close = return_row(y_out)
    y_begin()
    og_finish()

    def grad_view(g, unit, shard, half, low, count):
        rows = pl.ds(aligned(192 * shard + unit * low, 16), unit * count)
        if g == SELF:
            return wa.at[SELF, pl.ds(2 * half, 2), rows, :]
        return wa.at[CROSS, 2 * c + half, rows, :]

    def out_view(g, unit, half, low):
        rows = pl.ds(aligned(unit * low, 16), unit)
        if g == SELF:
            return self_out.at[c, pl.ds(2 * half, 2), rows, :]
        return cross_out.at[2 * c + half, rows, :]

    def out_whole(g, owner):
        if g == SELF:
            return self_out.at[owner]
        return cross_out.at[pl.ds(2 * owner, 2)]

    buffers = {
        "self": (
            lambda half, shard: gp.at[pl.ds(2 * half, 2), pl.ds(96 * shard, 96), :],
            lambda half, shard: r2s.at[half, shard],
            lambda half, m: r3s.at[m - 1, half],
        ),
        "cross": (
            lambda half, shard: ogrow.at[pl.ds(384 * half + 96 * shard, 96), :],
            lambda half, shard: r2c.at[half, shard],
            lambda half, m: r3c.at[m - 1, half],
        ),
    }

    own_quarter = [2 * px + py, px + 2 * py]
    own_pair = [2 * px, 2 * py]
    far_pair = [2 * (1 - px), 2 * (1 - py)]
    far_quarter = [2 * px + (1 - py), (1 - px) + 2 * py]
    near_quarter = {
        "x": [2 * (1 - px) + py, (1 - px) + 2 * py],
        "y": [2 * px + (1 - py), px + 2 * (1 - py)],
    }
    opposite = [2 * (1 - px) + (1 - py), (1 - px) + 2 * (1 - py)]
    first_way = [d_x, d_y]
    t_pair, t_far, t_cross = t + 1 - 2 * (t % 2), (t + 2) % 4, 3 - t
    second_way = [d_y, d_x]

    def fold(target, pieces):
        shape = target.shape
        if len(shape) == 3:
            for a in range(shape[0]):
                fold(target.at[a], [piece.at[a] for piece in pieces])
            return
        for low in range(0, shape[0], 96):
            rows = slice(low, min(low + 96, shape[0]))
            total = target[rows, :].astype(F32)
            for piece in pieces:
                total = total + piece[rows, :].astype(F32)
            target[rows, :] = total.astype(BF16)

    class Sum:
        def __init__(self, name, g, unit):
            self.g, self.unit = g, unit
            self.first, self.second, self.third = buffers[name]
            self.shards = [0, 1, 2, 3]
            self.s1 = [new_id(4) for _ in range(2)]
            self.s2 = [new_id(4) for _ in range(2)]
            self.s3 = [new_id(4) for _ in range(2)]
            self.to_x = [new_id() for _ in range(2)]
            self.to_y = [new_id() for _ in range(2)]
            self.across = [new_id() for _ in range(2)]
            self.core = new_id()
            self.keep = local_counter[0]
            local_counter[0] += 2
            self.copies = []

        def grad(self, shard, half, low, count):
            return grad_view(self.g, self.unit, shard, half, low, count)

        def out(self, half, low):
            return out_view(self.g, self.unit, half, low)

        def start(self, half, k):
            send(
                self.grad(self.shards[k], half, far_pair[half], 2),
                self.first(half, k),
                at(first_way[half], t),
                self.s1[half] + k,
            )

        def start_all(self):
            for k in range(len(self.shards)):
                for half in range(2):
                    self.start(half, k)

        def stage2(self, half):
            for k, shard in enumerate(self.shards):
                buffer = self.first(half, k)
                arrive(buffer, self.s1[half] + k)
                fold(self.grad(shard, half, far_quarter[half], 1), [self.part(buffer, half, 1)])
                send(
                    self.grad(shard, half, far_quarter[half], 1),
                    self.second(half, k),
                    at(second_way[half], t),
                    self.s2[half] + k,
                )
            for k, shard in enumerate(self.shards):
                buffer = self.first(half, k)
                fold(self.grad(shard, half, own_quarter[half], 1), [self.part(buffer, half, 0)])

        def part(self, buffer, half, other):
            inner = py if half == 0 else px
            low = aligned(self.unit * ((1 - inner) if other else inner), 16)
            rows = pl.ds(low, self.unit)
            if self.g == SELF:
                return buffer.at[:, rows, :]
            return buffer.at[rows, :]

        def stage3(self, half):
            for k, shard in enumerate(self.shards):
                buffer = self.second(half, k)
                arrive(buffer, self.s2[half] + k)
                fold(self.grad(shard, half, own_quarter[half], 1), [buffer])
            for k, shard in enumerate((t_pair, t_cross)):
                send(
                    self.grad(shard, half, own_quarter[half], 1),
                    self.third(half, 1 + k),
                    at(d, t_pair),
                    self.s3[half] + k,
                )

        def stage4(self, half):
            for k, shard in ((1, t_far), (0, t)):
                buffer = self.third(half, 1 + k)
                arrive(buffer, self.s3[half] + k)
                fold(self.grad(shard, half, own_quarter[half], 1), [buffer])
                if k:
                    send(
                        self.grad(t_far, half, own_quarter[half], 1),
                        self.third(half, 3),
                        at(d, t_far),
                        self.s3[half] + 2,
                    )

        def stage4_end(self, half):
            buffer = self.third(half, 3)
            arrive(buffer, self.s3[half] + 2)
            fold(self.grad(t, half, own_quarter[half], 1), [buffer])
            self.publish(half)

        def publish(self, half):
            total = self.grad(t, half, own_quarter[half], 1)
            spot = self.out(half, own_quarter[half])
            copy = pltpu.make_async_copy(total, spot, local_sems.at[self.keep + half])
            copy.start()
            self.copies.append(copy)
            send(total, spot, at(d_x, t), self.to_x[half])
            send(total, spot, at(d_y, t), self.to_y[half])

        def stage5(self):
            for half, way, ids in ((0, "x", self.to_x), (1, "y", self.to_y)):
                for other in range(2):
                    arrive(self.out(other, near_quarter[way][other]), ids[other])
                piece = self.out(half, near_quarter[way][half])
                send(piece, piece, at(d_y if way == "x" else d_x, t), self.across[half])

        def stage6(self):
            for half in range(2):
                arrive(self.out(half, opposite[half]), self.across[half])
            for copy in self.copies:
                copy.wait()
            mine = out_whole(self.g, c)
            send(mine, mine, at(d_core, t), self.core)

        def stage7(self):
            arrive(out_whole(self.g, 1 - c), self.core)

        def both(self, stage):
            return [functools.partial(stage, 0), functools.partial(stage, 1)]

    sum_self = Sum("self", SELF, 48)
    sum_cross = Sum("cross", CROSS, 48)

    class Quarter:
        def __init__(self, k, target):
            self.k, self.target = k, target
            self.base = new_id(4)
            self.to_x, self.to_y = new_id(), new_id()
            self.from_x, self.from_y = new_id(), new_id()
            self.core = new_id()
            self.keep = local_counter[0]
            local_counter[0] += 1

        def rows(self, quarter, low=0, size=192):
            return pl.ds(aligned(192 * quarter + low, 16), size)

        def piece(self, shard):
            return wf.at[self.k, shard, self.rows(q), :]

        def start(self, m):
            shard = (t + m) % 4
            send(self.piece(shard), rq.at[self.k, m - 1], at(d, shard), self.base + m)

        def collect(self):
            for m in range(1, 4):
                arrive(rq.at[self.k, m - 1], self.base + m)
            total = self.piece(t)
            fold(total, [rq.at[self.k, m] for m in range(3)])
            spot = self.target.at[c, self.rows(q), :]
            self.copy = pltpu.make_async_copy(total, spot, local_sems.at[self.keep])
            self.copy.start()
            send(total, spot, at(d_x, t), self.to_x)
            send(total, spot, at(d_y, t), self.to_y)

        def relay(self):
            arrive(self.target.at[c, self.rows(qx), :], self.to_x)
            part = self.target.at[c, self.rows(qx, 0, 96), :]
            send(part, part, at(d_y, t), self.from_x)
            arrive(self.target.at[c, self.rows(qy), :], self.to_y)
            part = self.target.at[c, self.rows(qy, 96, 96), :]
            send(part, part, at(d_x, t), self.from_y)

        def swap(self):
            arrive(self.target.at[c, self.rows(qd, 0, 96), :], self.from_x)
            arrive(self.target.at[c, self.rows(qd, 96, 96), :], self.from_y)
            self.copy.wait()
            send(self.target.at[c], self.target.at[c], at(d_core, t), self.core)

        def end(self):
            arrive(self.target.at[1 - c], self.core)

    quarters = [Quarter(0, up_out), Quarter(1, down_out)]

    def quarter_grads(shard):
        own_rows = pl.ds(aligned(192 * q, 16), 192)

        def row(r):
            def block(i, rows):
                section = s2all[r, pl.ds(rows, BLOCK), :]
                grad = zall[r, pl.ds(rows, BLOCK), :]
                upward = dot_nt(wf[0, shard, own_rows, :], section)
                cumulative = 0.5 * (1.0 + lax.erf(upward * (0.5**0.5)))
                density = jnp.exp(-0.5 * upward * upward) * 0.3989422804014327
                slope = cumulative + upward * density
                spot = pl.ds(aligned(512 * r + rows, BLOCK), BLOCK)
                units[1, :, spot] = (upward * cumulative).astype(BF16)
                units[0, :, spot] = (
                    dot_nt(wf[1, shard, own_rows, :], grad) * slope
                ).astype(BF16)

            blocks(block)

        times(4, row)
        for k, tokens in ((0, s2all), (1, zall)):
            for n in range(3):
                cols = slice(256 * n, 256 * n + 256)
                right = tokens[:, :, cols].reshape(2048, 256)
                wf[k, shard, own_rows, cols] = dot_nn(units[k], right).astype(BF16)

    def norm_back(upstream, index, slot, rows, target):
        normed = xh[slot, pl.ds(rows, BLOCK), :].astype(F32)
        nrm[pl.ds(index, 1), :] += jnp.sum(upstream * normed, axis=0, keepdims=True)
        nrm[pl.ds(index + 8, 1), :] += jnp.sum(upstream, axis=0, keepdims=True)
        scaled = upstream * gains[pl.ds(index, 1), :]
        grad = rstd[slot, pl.ds(rows, BLOCK), :] * (
            scaled
            - jnp.mean(scaled, axis=-1, keepdims=True)
            - normed * jnp.mean(scaled * normed, axis=-1, keepdims=True)
        )
        res[pl.ds(rows, BLOCK), :] = grad
        target[pl.ds(rows, BLOCK), :] = grad.astype(BF16)

    def out_back(i, rows):
        upstream = ogrow[pl.ds(aligned(own_base + rows, BLOCK), BLOCK), :].astype(F32)
        norm_back(upstream, 3 + c, 2, rows, zall.at[0])

    blocks(out_back)
    z3_begin()
    og_close()
    for device in (d_x, d_y):
        pl.semaphore_signal(credit.at[0], inc=1, device_id=at(device, t), device_id_type=MESH)

    def down_back(shard):
        def block(i, rows):
            left = zall[0, pl.ds(rows, BLOCK), :]
            for n in range(3):
                cols = slice(256 * n, 256 * n + 256)
                active_grad = dot_nt(left, wf[1, shard, cols, :])
                slope = gp[shard, pl.ds(rows, BLOCK), cols].astype(F32)
                gp[shard, pl.ds(rows, BLOCK), cols] = (active_grad * slope).astype(BF16)

        blocks(block)

    times(4, down_back)

    def up_input(i, rows):
        for n in range(3):
            cols = slice(256 * n, 256 * n + 256)
            total = res[pl.ds(rows, BLOCK), cols]
            for shard in range(4):
                total = total + dot_nn(gp[shard, pl.ds(rows, BLOCK), :], wf[0, shard, :, cols])
            acc[pl.ds(rows, BLOCK), cols] = total

    blocks(up_input)
    for device in (d_x, d_y):
        pl.semaphore_signal(credit.at[1], inc=1, device_id=at(device, t), device_id_type=MESH)

    blocks(lambda i, rows: norm_back(acc[pl.ds(rows, BLOCK), :], 1 + c, 1, rows, dzb))
    s2_relay()

    dctx = act.at[0]

    def context_back(which):
        def block(i, rows):
            left = dzb[pl.ds(rows, BLOCK), :]
            for n in range(3):
                cols = slice(256 * n, 256 * n + 256)
                dctx[pl.ds(rows, BLOCK), cols] = dot_nt(left, wa[which, 3, cols, :]).astype(BF16)

        blocks(block)

    def weight_rows(which, member, left_ref, rights):
        def tile(n):
            rows = aligned(n * 256, 256)
            for k in range(3):
                wide = slice(256 * k, 256 * k + 256)
                total = None
                for low, size, ref in rights:
                    term = dot_nn(
                        left_ref[pl.ds(rows, 256), low : low + size], ref[:, wide]
                    )
                    total = term if total is None else total + term
                wa[which, member, pl.ds(rows, 256), wide] = total.astype(BF16)

        times(3, tile)

    def attend_back(which, qkv, code_row, pairs):
        def pair(k, carry):
            lanes = pl.ds(aligned(k * 128, 128), 128)
            kv_acc[...] = jnp.zeros_like(kv_acc)

            def piece(rows, spans):
                key = gathered(qkv.at[1], spans, lanes)
                value = gathered(qkv.at[2], spans, lanes)
                key_t = jnp.transpose(key)
                query = qkv[0, pl.ds(rows, BLOCK), lanes] * jnp.asarray(scaling, BF16)
                grad = dctx[pl.ds(rows, BLOCK), lanes]
                query_code = codes[
                    pl.ds(code_row, 1), pl.ds(aligned(own_base + rows, BLOCK), BLOCK)
                ]
                allowed = gathered(kcode.at[which], spans, slice(None))[:, 0:1] == query_code
                for h in range(2):
                    query_h = query * head_lanes[h]
                    grad_h = grad * head_lanes[h]
                    scores = jnp.where(allowed, dot_nt(key, query_h), -1e30)
                    probs = jnp.exp(
                        scores - lse[which, pl.ds(2 * k + h, 1), pl.ds(rows, BLOCK)]
                    )
                    probs_grad = dot_nt(value, grad_h)
                    delta = jnp.sum(probs * probs_grad, axis=0, keepdims=True)
                    score_grad = (probs * (probs_grad - delta)).astype(BF16)
                    key_part = dot_nn(score_grad, query_h)
                    value_part = dot_nn(probs.astype(BF16), grad_h)
                    low = 0
                    for span in spans:
                        kv_acc[0, span, :] += key_part[low : low + span.size]
                        kv_acc[1, span, :] += value_part[low : low + span.size]
                        low += span.size
                    tt[
                        0, pl.ds(aligned(k * 128 + h * 64, 64), 64), pl.ds(rows, BLOCK)
                    ] = (dot_nn(key_t[64 * h : 64 * h + 64, :], score_grad) * scaling).astype(BF16)

            query_blocks(which, piece)
            for m in range(2):
                tt[1 + m, pl.ds(aligned(k * 128, 128), 128), :] = jnp.transpose(
                    kv_acc[m]
                ).astype(BF16)
            return carry

        lax.fori_loop(pairs[0], pairs[1], pair, 0)

    def pump(*steps):
        for step in steps:
            step()

    context_back(SELF)
    for wait in pending:
        wait()
    pending.clear()
    weight_rows(SELF, 3, ctx_t.at[1], [(0, 512, dzb)])
    attend_back(1, qkv2, 2, (0, 6))
    z3_relay()

    def self_input(i, rows):
        parts = [jnp.transpose(tt[m, :, pl.ds(rows, BLOCK)]) for m in range(3)]
        for n in range(3):
            cols = slice(256 * n, 256 * n + 256)
            total = res[pl.ds(rows, BLOCK), cols]
            for m in range(3):
                total = total + dot_nn(parts[m], wa[SELF, m, :, cols])
            acc[pl.ds(rows, BLOCK), cols] = total

    blocks(self_input)
    for m in range(3):
        weight_rows(SELF, m, tt.at[m], [(0, 512, sb)])
    pl.semaphore_wait(credit.at[1], 2)
    sum_self.start_all()
    pl.semaphore_signal(credit.at[2], inc=1, device_id=at(d_core, t), device_id_type=MESH)

    s2_finish()
    z3_finish()
    for m in (2, 1, 3):
        quarter_grads((t + m) % 4)
        for one in quarters:
            one.start(m)

    blocks(lambda i, rows: norm_back(acc[pl.ds(rows, BLOCK), :], 0, 0, rows, dzb))

    norm_ids = [new_id() for _ in range(5)]
    norm_ways = [
        at(d_core, t),
        at(d_x, t),
        at(d_y, t),
        at(d, t + 1 - 2 * (t % 2)),
        at(d, (t + 2) % 4),
    ]
    norm_steps = []

    def norm_begin(k):
        send(nrm if k == 0 else nrm_recv.at[k - 1, 1], nrm_recv.at[k, 0], norm_ways[k], norm_ids[k])

    def norm_step(k):
        arrive(nrm_recv.at[k, 0], norm_ids[k])
        mine = nrm[...] if k == 0 else nrm_recv[k - 1, 1]
        total = mine + nrm_recv[k, 0]
        if k < 4:
            nrm_recv[k, 1] = total
            norm_begin(k + 1)
        else:
            norm_out[...] = total

    norm_begin(0)
    context_back(CROSS)
    weight_rows(CROSS, 3, ctx_t.at[0], [(0, 512, dzb)])
    norm_step(0)
    attend_back(0, qkv1, 0, (0, 3))
    norm_step(1)
    pump(*sum_self.both(sum_self.stage2))
    attend_back(0, qkv1, 0, (3, 6))
    norm_step(2)

    key_ids = [new_id() for _ in range(2)]

    def key_input(j):
        parts = [jnp.transpose(tt[m, :, 256 * j : 256 * j + 256]) for m in (1, 2)]
        for n in range(3):
            cols = slice(256 * n, 256 * n + 256)
            act[1, 256 * j : 256 * j + 256, cols] = (
                dot_nn(parts[0], wa[CROSS, 1, :, cols]) + dot_nn(parts[1], wa[CROSS, 2, :, cols])
            ).astype(BF16)

    key_input(0)
    key_input(1)
    key_copies = [
        remote(
            act.at[1, pl.ds(256 * j, 256), :],
            dhk_recv.at[j],
            at(d_core, t),
            key_ids[j],
        )
        for j in range(2)
    ]
    key_copies[0].start()

    @pl.when(c == 0)
    def _():
        key_copies[1].start()

    def cross_input(i, rows):
        part = jnp.transpose(tt[0, :, pl.ds(rows, BLOCK)])
        for n in range(3):
            cols = slice(256 * n, 256 * n + 256)
            res[pl.ds(rows, BLOCK), cols] += dot_nn(part, wa[CROSS, 0, :, cols])

    blocks(cross_input)
    weight_rows(CROSS, 0, tt.at[0], [(0, 512, xrow.at[pl.ds(own_base, 512), :])])
    for m in range(1, 3):
        weight_rows(
            CROSS,
            m,
            tt.at[m],
            [
                (0, 256, xrow.at[pl.ds(other_base, 256), :]),
                (256, 256, xrow.at[pl.ds(512, 256), :]),
            ],
        )

    pump(*sum_self.both(sum_self.stage3))
    quarter_grads(t)

    pl.semaphore_wait(credit.at[2], 1)
    core_sums = [(a, n, new_id()) for a in range(2) for n in range(3)]

    def core_slot(a, n):
        k = 3 * a + n
        return qkv2.at[k // 2, pl.ds(256 * (k % 2), 256), :]

    for a, n, ident in core_sums:
        send(
            wa.at[CROSS, 2 * (1 - c) + a, pl.ds(256 * n, 256), :],
            core_slot(a, n),
            at(d_core, t),
            ident,
        )
    norm_step(3)

    y_close()
    arrive(dhk_recv.at[0], key_ids[0])

    @pl.when(c == 1)
    def _():
        arrive(dhk_recv.at[1], key_ids[1])

    yb[:BLOCK, :] = (res[:BLOCK, :] + dhk_recv[0].astype(F32)).astype(BF16)

    @pl.when(c == 1)
    def _():
        own_part = act[1, BLOCK:, :].astype(F32)
        yb[BLOCK:, :] = (res[BLOCK:, :] + dhk_recv[1].astype(F32) + own_part).astype(BF16)

    dx_begin, dx_close = return_row(dx_out)
    pump(*[one.collect for one in quarters])

    for a, n, ident in core_sums:
        arrive(core_slot(a, n), ident)
        fold(wa.at[CROSS, 2 * c + a, pl.ds(256 * n, 256), :], [core_slot(a, n)])
    pl.semaphore_wait(credit.at[0], 2)
    sum_cross.start_all()
    norm_step(4)
    pump(
        *sum_cross.both(sum_cross.stage2),
        *sum_self.both(sum_self.stage4),
        *[one.relay for one in quarters],
        *sum_cross.both(sum_cross.stage3),
        *sum_self.both(sum_self.stage4_end),
        *sum_cross.both(sum_cross.stage4),
        dx_begin,
        *[one.swap for one in quarters],
        sum_self.stage5,
        *sum_cross.both(sum_cross.stage4_end),
        sum_self.stage6,
        sum_cross.stage5,
        sum_cross.stage6,
        *[one.end for one in quarters],
        sum_self.stage7,
        sum_cross.stage7,
    )
    for wait in pending + late:
        wait()
    key_copies[0].wait_send()

    @pl.when(c == 0)
    def _():
        key_copies[1].wait_send()

    dx_close()
    if counter[0] > SEMAPHORES or local_counter[0] > LOCALS:
        raise ValueError((counter[0], local_counter[0]))


SEMAPHORES = 320
SPAN = 384
LOCALS = 40


def call_layer(*operands):
    def vmem(shape, dtype=BF16):
        return pltpu.VMEM(shape, dtype)

    anywhere = pl.BlockSpec(memory_space=pl.ANY)
    whole = pl.BlockSpec(memory_space=pltpu.VMEM)
    x_in = operands[0]
    return pl.pallas_call(
        layer_kernel,
        name="cross_modality_layer",
        out_shape=(
            jax.ShapeDtypeStruct(x_in.shape, BF16),
            jax.ShapeDtypeStruct(x_in.shape, BF16),
            jax.ShapeDtypeStruct((4, 192, 768), BF16),
            jax.ShapeDtypeStruct((2, 4, 192, 768), BF16),
            jax.ShapeDtypeStruct((2, 768, 768), BF16),
            jax.ShapeDtypeStruct((2, 768, 768), BF16),
            jax.ShapeDtypeStruct((16, 768), F32),
        ),
        in_specs=[anywhere] * 9 + [whole] * 2,
        out_specs=(anywhere,) * 6 + (whole,),
        scratch_shapes=[
            vmem((2, 4, 768, 768)),
            vmem((2, 4, 768, 768)),
            vmem((768, 768)),
            vmem((768, 768)),
            vmem((8, 768), F32),
            vmem((2, 512, 128), F32),
            vmem((3, 512, 768)),
            vmem((3, 512, 768)),
            vmem((2, 768, 512)),
            vmem((2, 16, 512), F32),
            vmem((3, 512, 768)),
            vmem((3, 512, 1), F32),
            vmem((512, 768)),
            vmem((512, 768), F32),
            vmem((512, 768), F32),
            vmem((4, 512, 768)),
            vmem((4, 512, 768)),
            vmem((512, 768)),
            vmem((3, 768, 512)),
            vmem((512, 768)),
            vmem((2, 256, 768)),
            vmem((2, 512, 128), F32),
            vmem((16, 768), F32),
            vmem((5, 2, 16, 768), F32),
            vmem((4, 512, 768)),
            vmem((4, 512, 768)),
            vmem((2, 192, 2048)),
            vmem((2, 3, 192, 768)),
            vmem((2, 4, 2, 48, 768)),
            vmem((3, 2, 2, 48, 768)),
            vmem((2, 4, 48, 768)),
            vmem((3, 2, 48, 768)),
            pltpu.SemaphoreType.DMA((SEMAPHORES,)),
            pltpu.SemaphoreType.DMA((SEMAPHORES,)),
            pltpu.SemaphoreType.DMA((LOCALS,)),
            pltpu.SemaphoreType.REGULAR((3,)),
        ],
        compiler_params=pltpu.CompilerParams(
            collective_id=0, has_side_effects=True, vmem_limit_bytes=64 * 1024 * 1024 - 512 * 1024
        ),
    )(*operands)


def results_kernel(
    cross, own, up, down, dx, norm,
    dx_out, cross_qkv, cross_out, self_qkv, self_out, up_out, down_out, gains, biases,
    v_cross, v_own, v_up, v_down, v_dx, v_norm,
    w_dx, w_cross_qkv, w_cross_out, w_self_qkv, w_self_out, w_up, w_down,
    in_sems, out_sems,
):
    sources = [
        (down.at[0], v_down.at[0]),
        (down.at[1], v_down.at[1]),
        (up.at[0], v_up.at[0]),
        (up.at[1], v_up.at[1]),
        (own.at[0], v_own.at[0]),
        (own.at[1], v_own.at[1]),
        (cross, v_cross),
        (dx, v_dx),
        (norm, v_norm),
    ]
    loads = [
        pltpu.make_async_copy(src, dst, in_sems.at[k]) for k, (src, dst) in enumerate(sources)
    ]
    for load in loads:
        load.start()
    stores = []

    def store(src, dst):
        copy = pltpu.make_async_copy(src, dst, out_sems.at[len(stores)])
        copy.start()
        stores.append(copy)

    for k in range(2):
        loads[k].wait()
        w_down[k] = v_down[k].astype(F32)
        store(w_down.at[k], down_out.at[k])
    for k in range(2):
        loads[2 + k].wait()
        for n in range(3):
            cols = slice(256 * n, 256 * n + 256)
            w_up[k, cols, :] = jnp.transpose(v_up[k, :, cols]).astype(F32)
        store(w_up.at[k], up_out.at[k])
    for k in range(2):
        loads[4 + k].wait()
        for n in range(3):
            w_self_qkv[k, n] = v_own[k, n].astype(F32)
        w_self_out[k] = v_own[k, 3].astype(F32)
        store(w_self_qkv.at[k], self_qkv.at[k])
        store(w_self_out.at[k], self_out.at[k])
    loads[6].wait()
    for n in range(3):
        w_cross_qkv[n] = v_cross[n].astype(F32)
    w_cross_out[...] = v_cross[3].astype(F32)
    store(w_cross_qkv, cross_qkv)
    store(w_cross_out, cross_out)
    loads[7].wait()
    w_dx[...] = v_dx[...].astype(F32)
    store(w_dx, dx_out)
    loads[8].wait()
    gains[...] = v_norm[0:5, :]
    biases[...] = v_norm[8:13, :]
    for copy in stores:
        copy.wait()


def call_results(cross, own, up, down, dx, norm):
    anywhere = pl.BlockSpec(memory_space=pl.ANY)
    whole = pl.BlockSpec(memory_space=pltpu.VMEM)

    def out(shape):
        return jax.ShapeDtypeStruct(shape, F32)

    shapes = [
        dx.shape,
        (3, 192, 768),
        (192, 768),
        (2, 3, 192, 768),
        (2, 192, 768),
        (2, 768, 768),
        (2, 768, 768),
    ]
    return pl.pallas_call(
        results_kernel,
        name="results",
        out_shape=tuple(out(shape) for shape in shapes) + (out((5, 768)), out((5, 768))),
        in_specs=[anywhere] * 6,
        out_specs=(anywhere,) * 7 + (whole,) * 2,
        scratch_shapes=[pltpu.VMEM(ref.shape, ref.dtype) for ref in (cross, own, up, down, dx, norm)]
        + [pltpu.VMEM(shape, F32) for shape in shapes]
        + [pltpu.SemaphoreType.DMA((9,)), pltpu.SemaphoreType.DMA((11,))],
        compiler_params=pltpu.CompilerParams(vmem_limit_bytes=56 * 1024 * 1024),
    )(cross, own, up, down, dx, norm)


def solution(mesh):
    extra = []
    step = 8
    while step < mesh.shape["dp"]:
        extra.append(step)
        step *= 2

    def total(array):
        for step in extra:
            pairs = [(k, k ^ step) for k in range(mesh.shape["dp"])]
            array = array + lax.ppermute(array, "dp", pairs)
        return array

    def body(
        layer_input,
        word_segments,
        image_order,
        cross_qkv,
        cross_out,
        self_qkv,
        self_out,
        ffn_up,
        ffn_down,
        norm_gains,
        norm_biases,
        out_grad,
    ):
        rows = layer_input.shape[0]
        images = jnp.repeat(image_order, BOXES, axis=1)
        pads = jnp.full((rows, PADS), CAPTIONS, jnp.int32)
        none = jnp.full((rows, WORDS + REGIONS + PADS), -1, jnp.int32)
        groups = jnp.concatenate([word_segments, images, pads], axis=1)
        keys = jnp.concatenate([word_segments, none[:, :REGIONS], pads], axis=1)
        kinds = jnp.concatenate([word_segments, images + 16, pads + 32], axis=1)
        codes = jnp.stack([groups, keys, kinds, none, none, none, none, none], axis=1).astype(F32)
        y, dx, d_cross, d_self, d_up, d_down, d_norm = call_layer(
            layer_input,
            out_grad,
            codes,
            jnp.swapaxes(cross_qkv, 1, 2),
            cross_out,
            jnp.swapaxes(self_qkv, 2, 3),
            self_out,
            ffn_up,
            ffn_down,
            norm_gains,
            norm_biases,
        )
        dx, *grads = call_results(d_cross, d_self, d_up, d_down, dx, d_norm)
        grads = [total(array) for array in grads]
        grads[0] = jnp.swapaxes(grads[0], 1, 2)
        grads[2] = jnp.swapaxes(grads[2], 2, 3)
        return (y, dx, *grads)

    in_specs = (
        P("dp", "tensor", None),
        P("dp", None),
        P("dp", None),
        P(None, None, "tensor"),
        P("tensor", None),
        P(None, None, None, "tensor"),
        P(None, "tensor", None),
        P(None, None, "tensor"),
        P(None, "tensor", None),
        P(),
        P(),
        P("dp", "tensor", None),
    )
    out_specs = (
        P("dp", "tensor", None),
        P("dp", "tensor", None),
        P(None, None, "tensor"),
        P("tensor", None),
        P(None, None, None, "tensor"),
        P(None, "tensor", None),
        P(None, None, "tensor"),
        P(None, "tensor", None),
        P(),
        P(),
    )
    return jax.shard_map(body, mesh=mesh, in_specs=in_specs, out_specs=out_specs, check_vma=False)
```

```python
import functools

import jax
import jax.numpy as jnp
from jax import lax
from jax.experimental import pallas as pl
from jax.experimental.pallas import tpu as pltpu
from jax.sharding import PartitionSpec as P

HEAD_DIM = 64
WORDS = 256
CAPTIONS = 14
BOXES = 36
REGIONS = 504
PADS = 8
NORM_EPSILON = 1e-12
BLOCK = 256
BF16 = jnp.bfloat16
F32 = jnp.float32
MESH = pl.DeviceIdType.MESH
CROSS, SELF, UP, DOWN = 0, 1, 2, 3


def dot_nn(left, right):
    return jnp.dot(left, right, preferred_element_type=F32)


def dot_nt(left, right):
    return lax.dot_general(left, right, (((1,), (1,)), ((), ())), preferred_element_type=F32)


def aligned(value, step):
    return pl.multiple_of(value, step)


def layer_kernel(
    x_in,
    og_in,
    codes_in,
    cross_in,
    cross_out_in,
    self_in,
    self_out_in,
    up_in,
    down_in,
    gains,
    biases,
    y_out,
    dx_out,
    cross_out,
    self_out,
    up_out,
    down_out,
    norm_out,
    wa,
    wf,
    xrow,
    ogrow,
    codes,
    kcode,
    qkv1,
    qkv2,
    ctx_t,
    lse,
    xh,
    rstd,
    sb,
    res,
    acc,
    act,
    gp,
    dzb,
    tt,
    yb,
    dhk_recv,
    kv_acc,
    nrm,
    nrm_recv,
    s2all,
    zall,
    qacc,
    rq,
    r2s,
    r3s,
    r2c,
    r3c,
    send_sems,
    recv_sems,
    local_sems,
    credit,
):
    d = lax.axis_index("dp")
    t = lax.axis_index("tensor")
    c = d % 2
    px = (d // 2) % 2
    py = (d // 4) % 2
    q = px + 2 * py
    d_core = d + 1 - 2 * c
    d_x = d + 2 - 4 * px
    d_y = d + 4 - 8 * py
    holder = t // 2
    d_holder = d - c + holder
    turn = t % 2
    nb = 1 + c
    near = {"x": d_x, "y": d_y, "core": d_core}

    def at(dp_index, tensor_index):
        return {"dp": dp_index, "tensor": tensor_index}

    counter = [0]
    local_counter = [0]
    pending = []

    def new_id(count=1):
        counter[0] += count
        return counter[0] - count

    def remote(src, dst, device, ident, arrival=None):
        return pltpu.make_async_remote_copy(
            src_ref=src,
            dst_ref=dst,
            send_sem=send_sems.at[ident],
            recv_sem=recv_sems.at[ident if arrival is None else arrival],
            device_id=device,
            device_id_type=MESH,
        )

    def send(src, dst, device, ident):
        copy = remote(src, dst, device, ident)
        copy.start()
        pending.append(copy.wait_send)

    def arrive(dst, ident):
        remote(dst, dst, at(d_core, t), ident).wait_recv()

    def local(src, dst):
        copy = pltpu.make_async_copy(src, dst, local_sems.at[local_counter[0]])
        local_counter[0] += 1
        return copy

    def blocks(body):
        def step(i, carry):
            body(i, aligned(i * BLOCK, BLOCK))
            return carry

        lax.fori_loop(0, nb, step, 0)

    def times(count, body):
        def step(i, carry):
            body(i)
            return carry

        lax.fori_loop(0, count, step, 0)

    barrier = pltpu.get_barrier_semaphore()
    partners = [at(d_core, t), at(d_x, t), at(d_y, t)]
    for m in range(1, 4):
        partners.append(at(d, (t + m) % 4))
        partners.append(at(d_core, (t + m) % 4))
    for partner in partners:
        pl.semaphore_signal(barrier, inc=1, device_id=partner, device_id_type=MESH)

    half_rows = aligned(t * 192, 16)
    own_copies = [
        local(cross_out_in, wa.at[CROSS, 3, pl.ds(half_rows, 192), :]),
        local(self_out_in.at[c], wa.at[SELF, 3, pl.ds(half_rows, 192), :]),
        local(down_in.at[c], wf.at[1, t]),
    ]
    raw_copies = [
        local(cross_in, wa.at[CROSS, pl.ds(0, 3), pl.ds(half_rows, 192), :]),
        local(self_in.at[c], wa.at[SELF, pl.ds(0, 3), pl.ds(half_rows, 192), :]),
    ]
    up_copies = [
        local(up_in.at[c, pl.ds(0, 512), :], qkv1.at[0]),
        local(up_in.at[c, pl.ds(512, 256), :], qkv1.at[1, pl.ds(0, 256), :]),
    ]
    for copy in raw_copies + own_copies + up_copies:
        copy.start()

    zero_half = jnp.zeros((BLOCK, 768), BF16)

    @pl.when(c == 0)
    def _():
        for ref in (qkv2.at[1], qkv2.at[2], sb, dzb):
            ref[BLOCK:, :] = zero_half
        for k in range(2):
            ctx_t[k, :, BLOCK:] = jnp.zeros((768, BLOCK), BF16)
        tt[0, :, BLOCK:] = jnp.zeros((768, BLOCK), BF16)

    nrm[...] = jnp.zeros_like(nrm)
    for g in (CROSS, SELF):
        raw_copies[g].wait()
        own_copies[g].wait()
    pl.semaphore_wait(barrier, len(partners))

    def spread_row(source, row):
        base = new_id(4)
        core_base = new_id(4)
        own = local(source.at[turn], row.at[pl.ds(half_rows, 192), :])

        def each_target(action):
            for r in range(2):
                target = 2 * c + r

                @pl.when(target != t)
                def _():
                    action(
                        remote(
                            source.at[r],
                            row.at[pl.ds(half_rows, 192), :],
                            at(d, target),
                            base + r,
                            base + t,
                        )
                    )

        def each_relay(action):
            @pl.when(holder == c)
            def _():
                for s in range(4):
                    part = row.at[pl.ds(192 * s, 192), :]
                    action(s, part, remote(part, part, at(d_core, t), core_base + s))

        def begin():
            each_target(lambda copy: copy.start())

            @pl.when(holder == c)
            def _():
                own.start()

        def relay():
            def action(s, part, copy):
                @pl.when(t == s)
                def _():
                    own.wait()

                @pl.when(t != s)
                def _():
                    arrive(part, base + s)

                copy.start()

            each_relay(action)

        def finish():
            @pl.when(holder != c)
            def _():
                for s in range(4):
                    arrive(row.at[pl.ds(192 * s, 192), :], core_base + s)

        def close():
            each_target(lambda copy: copy.wait_send())
            each_relay(lambda s, part, copy: copy.wait_send())

        return begin, relay, finish, close

    x_begin, x_relay, x_finish, x_close = spread_row(x_in, xrow)
    og_begin, og_relay, og_finish, og_close = spread_row(og_in, ogrow)
    pending.append(x_close)

    code_ident = new_id()
    code_own = local(codes_in.at[turn], codes)

    @pl.when(holder == c)
    def _():
        code_own.start()
        remote(codes_in.at[turn], codes, at(d_core, t), code_ident).start()

    def share(g, shard, quarter, low, high):
        if g >= UP:
            rows = aligned(quarter * 192 + low * 96, 16)
            return wf.at[g - UP, shard, pl.ds(rows, (high - low) * 96), :]
        rows = aligned(shard * 192 + quarter * 48, 16)
        if g == SELF:
            return wa.at[SELF, pl.ds(2 * low, 2 * (high - low)), pl.ds(rows, 48), :]
        return wa.at[CROSS, pl.ds(2 * c + low, high - low), pl.ds(rows, 48), :]

    def own_share(g):
        if g >= UP:
            rows = pl.ds(aligned(q * 192, 16), 192)
            return wf.at[0, t, rows, :] if g == UP else down_in.at[c, rows, :]
        return share(g, t, q, 0, 2)

    qx, qy = (1 - px) + 2 * py, px + 2 * (1 - py)
    qd = (1 - px) + 2 * (1 - py)
    items = [(g, m) for g in (CROSS, SELF, UP, DOWN) for m in range(1, 4)]
    z_base = {g: new_id(4) for g in (CROSS, SELF, UP, DOWN)}
    own_ids = {g: new_id(2) for g in (CROSS, SELF, UP, DOWN)}
    pass_ids = {item: new_id() for item in items}
    x_ids = {item: new_id() for item in items}
    y_ids = {item: new_id() for item in items}
    fx_ids = {item: new_id() for item in items}
    fy_ids = {item: new_id() for item in items}
    core_ids = {m: new_id() for m in range(1, 4)}
    arrivals = {
        1: t + 1 - 2 * (t % 2),
        2: 2 - t // 2,
        3: 3 - 3 * (t // 2),
    }

    def z_way(g, way):
        exists = t > 0 if way == 0 else t < 3
        target = t - 1 + 2 * way

        def copy():
            return remote(
                own_share(g),
                share(g, t, q, 0, 2),
                at(d, target),
                own_ids[g] + way,
                z_base[g] + t,
            )

        @pl.when(exists)
        def _():
            copy().start()

        def close():
            @pl.when(exists)
            def _():
                copy().wait_send()

        pending.append(close)

    def z_own(g):
        for way in range(2):
            z_way(g, way)

    def first(item):
        g, m = item
        shard = arrivals[m]
        piece = share(g, shard, q, 0, 2)
        arrive(piece, z_base[g] + shard)
        inner = jnp.logical_and(t > 0, t < 3)
        target = jnp.where(shard < t, t + 1, t - 1)

        def copy():
            return remote(piece, piece, at(d, target), pass_ids[item], z_base[g] + shard)

        @pl.when(inner)
        def _():
            copy().start()

        def close():
            @pl.when(inner)
            def _():
                copy().wait_send()

        pending.append(close)
        send(piece, piece, at(d_x, t), x_ids[item])
        send(piece, piece, at(d_y, t), y_ids[item])
        if m == 1 and g < DOWN:
            z_own(g + 1)
        if g == CROSS and m == 1:
            x_begin()
        if item == (DOWN, 1):
            og_begin()

    def second(item):
        g, m = item
        shard = arrivals[m]
        arrive(share(g, shard, qx, 0, 2), x_ids[item])
        low = share(g, shard, qx, 0, 1)
        send(low, low, at(d_y, t), fy_ids[item])
        arrive(share(g, shard, qy, 0, 2), y_ids[item])
        high = share(g, shard, qy, 1, 2)
        send(high, high, at(d_x, t), fx_ids[item])

    def third(item):
        g, m = item
        shard = arrivals[m]
        arrive(share(g, shard, qd, 0, 1), fy_ids[item])
        arrive(share(g, shard, qd, 1, 2), fx_ids[item])
        if g == CROSS:
            rows = pl.ds(aligned(shard * 192, 16), 192)
            whole = wa.at[CROSS, pl.ds(2 * c, 2), rows, :]
            send(whole, whole, at(d_core, t), core_ids[m])

    def last(m):
        shard = arrivals[m]
        rows = pl.ds(aligned(shard * 192, 16), 192)
        arrive(wa.at[CROSS, pl.ds(2 * (1 - c), 2), rows, :], core_ids[m])

    z_own(CROSS)
    for copy in up_copies:
        copy.wait()
    wf[0, t, :, 0:512] = jnp.transpose(qkv1[0])
    wf[0, t, :, 512:768] = jnp.transpose(qkv1[1, 0:256, :])

    steps = []
    position = {}
    for k in range(len(items) + 2):
        if k < len(items):
            steps.append(functools.partial(first, items[k]))
        if 0 <= k - 1 < len(items):
            steps.append(functools.partial(second, items[k - 1]))
        if 0 <= k - 2 < len(items):
            steps.append(functools.partial(third, items[k - 2]))
            position[items[k - 2]] = len(steps)
    done = [0]

    def advance(upto):
        while done[0] < min(upto, len(steps)):
            steps[done[0]]()
            done[0] += 1

    advance(position[(CROSS, 2)])
    x_relay()
    x_finish()

    @pl.when(holder == c)
    def _():
        code_own.wait()
        remote(codes_in.at[turn], codes, at(d_core, t), code_ident).wait_send()

    @pl.when(holder != c)
    def _():
        arrive(codes, code_ident)

    def as_column(row):
        return jnp.transpose(jnp.broadcast_to(row, (128, BLOCK)))

    own_base = aligned(c * BLOCK, BLOCK)
    other_base = aligned((1 - c) * BLOCK, BLOCK)
    kcode[0, :BLOCK, :] = as_column(codes[0:1, pl.ds(other_base, BLOCK)])
    kcode[0, BLOCK:, :] = as_column(codes[pl.ds(c, 1), 512:768])
    kcode[1, :BLOCK, :] = as_column(codes[2:3, pl.ds(own_base, BLOCK)])
    kcode[1, BLOCK:, :] = as_column(codes[pl.ds(3 - c, 1), 512:768])

    lane = lax.broadcasted_iota(jnp.int32, (1, 128), 1)
    head_lanes = [
        (lane < HEAD_DIM).astype(F32).astype(BF16),
        (lane >= HEAD_DIM).astype(F32).astype(BF16),
    ]
    scaling = HEAD_DIM ** (-0.5)

    def project(source, base, weight, target, rows):
        left = source[pl.ds(base, BLOCK), :]
        for n in range(3):
            target[pl.ds(rows, BLOCK), 256 * n : 256 * n + 256] = dot_nt(
                left, weight[256 * n : 256 * n + 256, :]
            ).astype(BF16)

    def attend(which, qkv, code_row, pairs):
        def pair(k):
            lanes = pl.ds(aligned(k * 128, 128), 128)
            key = qkv[1, :, lanes]
            value_t = jnp.transpose(qkv[2, :, lanes])

            def block(i, rows):
                query = qkv[0, pl.ds(rows, BLOCK), lanes] * jnp.asarray(scaling, BF16)
                query_code = codes[
                    pl.ds(code_row, 1), pl.ds(aligned(own_base + rows, BLOCK), BLOCK)
                ]
                allowed = kcode[which, :, 0:1] == query_code
                for h in range(2):
                    scores = dot_nt(key, query * head_lanes[h])
                    scores = jnp.where(allowed, scores, -1e30)
                    top = jnp.max(scores, axis=0, keepdims=True)
                    exponent = jnp.exp(scores - top)
                    total = jnp.sum(exponent, axis=0, keepdims=True)
                    probs = (exponent * (1.0 / total)).astype(BF16)
                    lse[which, pl.ds(2 * k + h, 1), pl.ds(rows, BLOCK)] = top + jnp.log(total)
                    ctx_t[
                        which,
                        pl.ds(aligned(k * 128 + h * 64, 64), 64),
                        pl.ds(rows, BLOCK),
                    ] = dot_nn(value_t[64 * h : 64 * h + 64, :], probs).astype(BF16)

            blocks(block)

        def run(k, carry):
            pair(k)
            return carry

        lax.fori_loop(pairs[0], pairs[1], run, 0)

    def normalize(summed, index, slot, rows):
        center = summed - jnp.mean(summed, axis=-1, keepdims=True)
        inverse = lax.rsqrt(jnp.mean(center * center, axis=-1, keepdims=True) + NORM_EPSILON)
        normed = center * inverse
        xh[slot, pl.ds(rows, BLOCK), :] = normed.astype(BF16)
        rstd[slot, pl.ds(rows, BLOCK), :] = inverse
        return normed * gains[pl.ds(index, 1), :] + biases[pl.ds(index, 1), :]

    def attention_out(which, rows):
        context = jnp.transpose(ctx_t[which, :, pl.ds(rows, BLOCK)])
        return dot_nn(context, wa[which, 3])

    advance(position[(CROSS, 3)])
    for m in range(1, 4):
        last(m)
    blocks(lambda i, rows: project(xrow, own_base + rows, wa.at[CROSS, 0], qkv1.at[0], rows))
    for k in range(1, 3):
        project(xrow, other_base, wa.at[CROSS, k], qkv1.at[k], 0)
        project(xrow, 512, wa.at[CROSS, k], qkv1.at[k], BLOCK)
    attend(0, qkv1, 0, (0, 3))
    advance(position[(SELF, 1)])
    attend(0, qkv1, 0, (3, 6))
    advance(position[(SELF, 2)])

    def cross_end(i, rows):
        stream = xrow[pl.ds(aligned(own_base + rows, BLOCK), BLOCK), :].astype(F32)
        section = normalize(stream + attention_out(0, rows), 0, 0, rows)
        res[pl.ds(rows, BLOCK), :] = section
        sb[pl.ds(rows, BLOCK), :] = section.astype(BF16)

    blocks(cross_end)

    advance(position[(SELF, 3)])
    for k in range(3):
        blocks(lambda i, rows: project(sb, rows, wa.at[SELF, k], qkv2.at[k], rows))
    attend(1, qkv2, 2, (0, 3))
    advance(position[(UP, 1)])
    attend(1, qkv2, 2, (3, 6))
    advance(position[(UP, 2)])

    def self_end(i, rows):
        summed = res[pl.ds(rows, BLOCK), :] + attention_out(1, rows)
        section = normalize(summed, 1 + c, 1, rows)
        res[pl.ds(rows, BLOCK), :] = section
        s2all[0, pl.ds(rows, BLOCK), :] = section.astype(BF16)

    blocks(self_end)

    late = []

    def plane_gather(buffer):
        to_x, to_y, from_x, from_y = new_id(), new_id(), new_id(), new_id()

        def sized(action):
            for core in range(2):

                @pl.when(c == core)
                def _():
                    action(BLOCK * (core + 1))

        def part(k, low, size):
            return buffer.at[k, pl.ds(low, size), :]

        def firsts(size):
            return [
                remote(part(0, 0, size), part(1, 0, size), at(d_x, t), to_x),
                remote(part(0, 0, size), part(2, 0, size), at(d_y, t), to_y),
            ]

        def seconds(size):
            half = size // 2
            return [
                remote(part(1, 0, half), part(3, 0, half), at(d_y, t), from_x),
                remote(part(2, half, half), part(3, half, half), at(d_x, t), from_y),
            ]

        def begin():
            sized(lambda size: [copy.start() for copy in firsts(size)])

        def relay():
            def action(size):
                onward = seconds(size)
                arrive(part(1, 0, size), to_x)
                onward[0].start()
                arrive(part(2, 0, size), to_y)
                onward[1].start()

            sized(action)

        def finish():
            def action(size):
                half = size // 2
                arrive(part(3, 0, half), from_x)
                arrive(part(3, half, half), from_y)

            sized(action)

        def close():
            sized(lambda size: [copy.wait_send() for copy in firsts(size) + seconds(size)])

        late.append(close)
        return begin, relay, finish

    s2_begin, s2_relay, s2_finish = plane_gather(s2all)
    z3_begin, z3_relay, z3_finish = plane_gather(zall)
    def feed_up(shard):
        def block(i, rows):
            left = s2all[0, pl.ds(rows, BLOCK), :]
            for n in range(3):
                cols = slice(256 * n, 256 * n + 256)
                upward = dot_nt(left, wf[0, shard, cols, :])
                cumulative = 0.5 * (1.0 + lax.erf(upward * (0.5**0.5)))
                density = jnp.exp(-0.5 * upward * upward) * 0.3989422804014327
                act[shard, pl.ds(rows, BLOCK), cols] = (upward * cumulative).astype(BF16)
                gp[shard, pl.ds(rows, BLOCK), cols] = (cumulative + upward * density).astype(BF16)

        blocks(block)

    feed_up(t)
    for m in range(1, 4):
        advance(position[(UP, m)])
        feed_up(arrivals[m])

    def feed_down(shard):
        def block(i, rows):
            left = act[shard, pl.ds(rows, BLOCK), :]
            for n in range(3):
                cols = slice(256 * n, 256 * n + 256)
                res[pl.ds(rows, BLOCK), cols] += dot_nn(left, wf[1, shard, :, cols])

        blocks(block)

    own_copies[2].wait()
    feed_down(t)
    for m in range(1, 4):
        advance(position[(DOWN, m)])
        if m == 3:
            s2_begin()
            og_relay()
        feed_down(arrivals[m])

    def layer_end(i, rows):
        result = normalize(res[pl.ds(rows, BLOCK), :], 3 + c, 2, rows)
        yb[pl.ds(rows, BLOCK), :] = result.astype(BF16)

    blocks(layer_end)

    def return_row(target):
        idents = [[new_id() for _ in range(3)] for _ in range(2)]
        send_base = new_id(12)
        local_ids = [local_counter[0] + k for k in range(3)]
        local_counter[0] += 3

        def each(action):
            for k in range(12):
                source_core = 0 if k < 4 else 1
                slots, part = k // 3, k % 3
                src = yb.at[pl.ds(64 * k - 256 * source_core, 64), :]
                for r in range(2):
                    dst = target.at[r, pl.ds(64 * part, 64), :]
                    mine = jnp.logical_and(c == source_core, turn == r)
                    here = jnp.logical_and(holder == c, t == slots)

                    @pl.when(jnp.logical_and(mine, here))
                    def _():
                        copy = pltpu.make_async_copy(src, dst, local_sems.at[local_ids[part]])
                        if action == "start":
                            copy.start()
                        elif action == "wait":
                            copy.wait()

                    @pl.when(jnp.logical_and(mine, jnp.logical_not(here)))
                    def _():
                        copy = remote(
                            src, dst, at(d_holder, slots), send_base + k, idents[r][part]
                        )
                        if action == "start":
                            copy.start()
                        elif action == "wait":
                            copy.wait_send()

        def begin():
            each("start")

        def close():
            each("wait")
            for r in range(2):
                for part in range(3):
                    dst = target.at[r, pl.ds(64 * part, 64), :]
                    k = 3 * t + part
                    source_core = jnp.where(k < 4, 0, 1)
                    from_here = jnp.logical_and(
                        jnp.logical_and(source_core == c, turn == r), holder == c
                    )

                    @pl.when(jnp.logical_not(from_here))
                    def _():
                        arrive(dst, idents[r][part])

        return begin, close

    y_begin, y_close = return_row(y_out)
    y_begin()
    og_finish()

    def grad_view(g, unit, shard, half, low, count):
        rows = pl.ds(aligned(192 * shard + unit * low, 16), unit * count)
        if g == SELF:
            return wa.at[SELF, pl.ds(2 * half, 2), rows, :]
        return wa.at[CROSS, 2 * c + half, rows, :]

    def out_view(g, unit, half, low):
        rows = pl.ds(aligned(unit * low, 16), unit)
        if g == SELF:
            return self_out.at[c, pl.ds(2 * half, 2), rows, :]
        return cross_out.at[2 * c + half, rows, :]

    def out_whole(g, owner):
        if g == SELF:
            return self_out.at[owner]
        return cross_out.at[pl.ds(2 * owner, 2)]

    buffers = {
        "self": (
            lambda half, shard: gp.at[pl.ds(2 * half, 2), pl.ds(96 * shard, 96), :],
            lambda half, shard: r2s.at[half, shard],
            lambda half, m: r3s.at[m - 1, half],
        ),
        "cross": (
            lambda half, shard: ogrow.at[pl.ds(384 * half + 96 * shard, 96), :],
            lambda half, shard: r2c.at[half, shard],
            lambda half, m: r3c.at[m - 1, half],
        ),
    }

    own_quarter = [2 * px + py, px + 2 * py]
    own_pair = [2 * px, 2 * py]
    far_pair = [2 * (1 - px), 2 * (1 - py)]
    far_quarter = [2 * px + (1 - py), (1 - px) + 2 * py]
    near_quarter = {
        "x": [2 * (1 - px) + py, (1 - px) + 2 * py],
        "y": [2 * px + (1 - py), px + 2 * (1 - py)],
    }
    opposite = [2 * (1 - px) + (1 - py), (1 - px) + 2 * (1 - py)]
    first_way = [d_x, d_y]
    t_pair, t_far, t_cross = t + 1 - 2 * (t % 2), (t + 2) % 4, 3 - t
    second_way = [d_y, d_x]

    def fold(target, pieces):
        shape = target.shape
        if len(shape) == 3:
            for a in range(shape[0]):
                fold(target.at[a], [piece.at[a] for piece in pieces])
            return
        for low in range(0, shape[0], 96):
            rows = slice(low, min(low + 96, shape[0]))
            total = target[rows, :].astype(F32)
            for piece in pieces:
                total = total + piece[rows, :].astype(F32)
            target[rows, :] = total.astype(BF16)

    class Sum:
        def __init__(self, name, g, unit):
            self.g, self.unit = g, unit
            self.first, self.second, self.third = buffers[name]
            self.shards = [0, 1, 2, 3]
            self.s1 = [new_id(4) for _ in range(2)]
            self.s2 = [new_id(4) for _ in range(2)]
            self.s3 = [new_id(4) for _ in range(2)]
            self.to_x = [new_id() for _ in range(2)]
            self.to_y = [new_id() for _ in range(2)]
            self.across = [new_id() for _ in range(2)]
            self.core = new_id()
            self.keep = local_counter[0]
            local_counter[0] += 2
            self.copies = []

        def grad(self, shard, half, low, count):
            return grad_view(self.g, self.unit, shard, half, low, count)

        def out(self, half, low):
            return out_view(self.g, self.unit, half, low)

        def start(self, half, k):
            send(
                self.grad(self.shards[k], half, far_pair[half], 2),
                self.first(half, k),
                at(first_way[half], t),
                self.s1[half] + k,
            )

        def start_all(self):
            for k in range(len(self.shards)):
                for half in range(2):
                    self.start(half, k)

        def stage2(self, half):
            for k, shard in enumerate(self.shards):
                buffer = self.first(half, k)
                arrive(buffer, self.s1[half] + k)
                fold(self.grad(shard, half, far_quarter[half], 1), [self.part(buffer, half, 1)])
                send(
                    self.grad(shard, half, far_quarter[half], 1),
                    self.second(half, k),
                    at(second_way[half], t),
                    self.s2[half] + k,
                )
            for k, shard in enumerate(self.shards):
                buffer = self.first(half, k)
                fold(self.grad(shard, half, own_quarter[half], 1), [self.part(buffer, half, 0)])

        def part(self, buffer, half, other):
            inner = py if half == 0 else px
            low = aligned(self.unit * ((1 - inner) if other else inner), 16)
            rows = pl.ds(low, self.unit)
            if self.g == SELF:
                return buffer.at[:, rows, :]
            return buffer.at[rows, :]

        def stage3(self, half):
            for k, shard in enumerate(self.shards):
                buffer = self.second(half, k)
                arrive(buffer, self.s2[half] + k)
                fold(self.grad(shard, half, own_quarter[half], 1), [buffer])
            for k, shard in enumerate((t_pair, t_cross)):
                send(
                    self.grad(shard, half, own_quarter[half], 1),
                    self.third(half, 1 + k),
                    at(d, t_pair),
                    self.s3[half] + k,
                )

        def stage4(self, half):
            for k, shard in ((1, t_far), (0, t)):
                buffer = self.third(half, 1 + k)
                arrive(buffer, self.s3[half] + k)
                fold(self.grad(shard, half, own_quarter[half], 1), [buffer])
                if k:
                    send(
                        self.grad(t_far, half, own_quarter[half], 1),
                        self.third(half, 3),
                        at(d, t_far),
                        self.s3[half] + 2,
                    )

        def stage4_end(self, half):
            buffer = self.third(half, 3)
            arrive(buffer, self.s3[half] + 2)
            fold(self.grad(t, half, own_quarter[half], 1), [buffer])
            self.publish(half)

        def publish(self, half):
            total = self.grad(t, half, own_quarter[half], 1)
            spot = self.out(half, own_quarter[half])
            copy = pltpu.make_async_copy(total, spot, local_sems.at[self.keep + half])
            copy.start()
            self.copies.append(copy)
            send(total, spot, at(d_x, t), self.to_x[half])
            send(total, spot, at(d_y, t), self.to_y[half])

        def stage5(self):
            for half, way, ids in ((0, "x", self.to_x), (1, "y", self.to_y)):
                for other in range(2):
                    arrive(self.out(other, near_quarter[way][other]), ids[other])
                piece = self.out(half, near_quarter[way][half])
                send(piece, piece, at(d_y if way == "x" else d_x, t), self.across[half])

        def stage6(self):
            for half in range(2):
                arrive(self.out(half, opposite[half]), self.across[half])
            for copy in self.copies:
                copy.wait()
            mine = out_whole(self.g, c)
            send(mine, mine, at(d_core, t), self.core)

        def stage7(self):
            arrive(out_whole(self.g, 1 - c), self.core)

        def both(self, stage):
            return [functools.partial(stage, 0), functools.partial(stage, 1)]

    sum_self = Sum("self", SELF, 48)
    sum_cross = Sum("cross", CROSS, 48)

    class Quarter:
        def __init__(self, k, target):
            self.k, self.target = k, target
            self.base = new_id(4)
            self.to_x, self.to_y = new_id(), new_id()
            self.from_x, self.from_y = new_id(), new_id()
            self.core = new_id()
            self.keep = local_counter[0]
            local_counter[0] += 1

        def rows(self, quarter, low=0, size=192):
            return pl.ds(aligned(192 * quarter + low, 16), size)

        def piece(self, shard):
            return wf.at[self.k, shard, self.rows(q), :]

        def start(self, m):
            shard = (t + m) % 4
            send(self.piece(shard), rq.at[self.k, m - 1], at(d, shard), self.base + m)

        def collect(self):
            for m in range(1, 4):
                arrive(rq.at[self.k, m - 1], self.base + m)
            total = self.piece(t)
            fold(total, [rq.at[self.k, m] for m in range(3)])
            spot = self.target.at[c, self.rows(q), :]
            self.copy = pltpu.make_async_copy(total, spot, local_sems.at[self.keep])
            self.copy.start()
            send(total, spot, at(d_x, t), self.to_x)
            send(total, spot, at(d_y, t), self.to_y)

        def relay(self):
            arrive(self.target.at[c, self.rows(qx), :], self.to_x)
            part = self.target.at[c, self.rows(qx, 0, 96), :]
            send(part, part, at(d_y, t), self.from_x)
            arrive(self.target.at[c, self.rows(qy), :], self.to_y)
            part = self.target.at[c, self.rows(qy, 96, 96), :]
            send(part, part, at(d_x, t), self.from_y)

        def swap(self):
            arrive(self.target.at[c, self.rows(qd, 0, 96), :], self.from_x)
            arrive(self.target.at[c, self.rows(qd, 96, 96), :], self.from_y)
            self.copy.wait()
            send(self.target.at[c], self.target.at[c], at(d_core, t), self.core)

        def end(self):
            arrive(self.target.at[1 - c], self.core)

    quarters = [Quarter(0, up_out), Quarter(1, down_out)]

    def quarter_grads(shard):
        own_rows = pl.ds(aligned(192 * q, 16), 192)
        qacc[...] = jnp.zeros_like(qacc)

        def row(r):
            def block(i, rows):
                section = s2all[r, pl.ds(rows, BLOCK), :]
                grad = zall[r, pl.ds(rows, BLOCK), :]
                upward = dot_nt(wf[0, shard, own_rows, :], section)
                cumulative = 0.5 * (1.0 + lax.erf(upward * (0.5**0.5)))
                density = jnp.exp(-0.5 * upward * upward) * 0.3989422804014327
                active = (upward * cumulative).astype(BF16)
                slope = cumulative + upward * density
                up_grad = (dot_nt(wf[1, shard, own_rows, :], grad) * slope).astype(BF16)
                for n in range(3):
                    cols = slice(256 * n, 256 * n + 256)
                    qacc[0, :, cols] += dot_nn(up_grad, section[:, cols])
                    qacc[1, :, cols] += dot_nn(active, grad[:, cols])

            blocks(block)

        times(4, row)
        for k in range(2):
            wf[k, shard, own_rows, :] = qacc[k].astype(BF16)

    def norm_back(upstream, index, slot, rows, target):
        normed = xh[slot, pl.ds(rows, BLOCK), :].astype(F32)
        nrm[pl.ds(index, 1), :] += jnp.sum(upstream * normed, axis=0, keepdims=True)
        nrm[pl.ds(index + 8, 1), :] += jnp.sum(upstream, axis=0, keepdims=True)
        scaled = upstream * gains[pl.ds(index, 1), :]
        grad = rstd[slot, pl.ds(rows, BLOCK), :] * (
            scaled
            - jnp.mean(scaled, axis=-1, keepdims=True)
            - normed * jnp.mean(scaled * normed, axis=-1, keepdims=True)
        )
        res[pl.ds(rows, BLOCK), :] = grad
        target[pl.ds(rows, BLOCK), :] = grad.astype(BF16)

    def out_back(i, rows):
        upstream = ogrow[pl.ds(aligned(own_base + rows, BLOCK), BLOCK), :].astype(F32)
        norm_back(upstream, 3 + c, 2, rows, zall.at[0])

    blocks(out_back)
    z3_begin()
    og_close()
    for device in (d_x, d_y):
        pl.semaphore_signal(credit.at[0], inc=1, device_id=at(device, t), device_id_type=MESH)

    def down_back(shard):
        def block(i, rows):
            left = zall[0, pl.ds(rows, BLOCK), :]
            for n in range(3):
                cols = slice(256 * n, 256 * n + 256)
                active_grad = dot_nt(left, wf[1, shard, cols, :])
                slope = gp[shard, pl.ds(rows, BLOCK), cols].astype(F32)
                gp[shard, pl.ds(rows, BLOCK), cols] = (active_grad * slope).astype(BF16)

        blocks(block)

    times(4, down_back)

    def up_input(i, rows):
        for n in range(3):
            cols = slice(256 * n, 256 * n + 256)
            total = res[pl.ds(rows, BLOCK), cols]
            for shard in range(4):
                total = total + dot_nn(gp[shard, pl.ds(rows, BLOCK), :], wf[0, shard, :, cols])
            acc[pl.ds(rows, BLOCK), cols] = total

    blocks(up_input)
    for device in (d_x, d_y):
        pl.semaphore_signal(credit.at[1], inc=1, device_id=at(device, t), device_id_type=MESH)

    blocks(lambda i, rows: norm_back(acc[pl.ds(rows, BLOCK), :], 1 + c, 1, rows, dzb))
    s2_relay()

    dctx = act.at[0]

    def context_back(which):
        def block(i, rows):
            left = dzb[pl.ds(rows, BLOCK), :]
            for n in range(3):
                cols = slice(256 * n, 256 * n + 256)
                dctx[pl.ds(rows, BLOCK), cols] = dot_nt(left, wa[which, 3, cols, :]).astype(BF16)

        blocks(block)

    def weight_rows(which, member, left_ref, rights):
        def tile(n):
            rows = aligned(n * 256, 256)
            for k in range(3):
                wide = slice(256 * k, 256 * k + 256)
                total = None
                for low, size, ref in rights:
                    term = dot_nn(
                        left_ref[pl.ds(rows, 256), low : low + size], ref[:, wide]
                    )
                    total = term if total is None else total + term
                wa[which, member, pl.ds(rows, 256), wide] = total.astype(BF16)

        times(3, tile)

    def attend_back(which, qkv, code_row, pairs):
        def pair(k, carry):
            lanes = pl.ds(aligned(k * 128, 128), 128)
            key = qkv[1, :, lanes]
            value = qkv[2, :, lanes]
            key_t = jnp.transpose(key)
            kv_acc[...] = jnp.zeros_like(kv_acc)

            def block(i, rows):
                query = qkv[0, pl.ds(rows, BLOCK), lanes] * jnp.asarray(scaling, BF16)
                grad = dctx[pl.ds(rows, BLOCK), lanes]
                query_code = codes[
                    pl.ds(code_row, 1), pl.ds(aligned(own_base + rows, BLOCK), BLOCK)
                ]
                allowed = kcode[which, :, 0:1] == query_code
                for h in range(2):
                    query_h = query * head_lanes[h]
                    grad_h = grad * head_lanes[h]
                    scores = jnp.where(allowed, dot_nt(key, query_h), -1e30)
                    probs = jnp.exp(
                        scores - lse[which, pl.ds(2 * k + h, 1), pl.ds(rows, BLOCK)]
                    )
                    probs_grad = dot_nt(value, grad_h)
                    delta = jnp.sum(probs * probs_grad, axis=0, keepdims=True)
                    score_grad = (probs * (probs_grad - delta)).astype(BF16)
                    kv_acc[0] += dot_nn(score_grad, query_h)
                    kv_acc[1] += dot_nn(probs.astype(BF16), grad_h)
                    tt[
                        0, pl.ds(aligned(k * 128 + h * 64, 64), 64), pl.ds(rows, BLOCK)
                    ] = (dot_nn(key_t[64 * h : 64 * h + 64, :], score_grad) * scaling).astype(BF16)

            blocks(block)
            for m in range(2):
                tt[1 + m, pl.ds(aligned(k * 128, 128), 128), :] = jnp.transpose(
                    kv_acc[m]
                ).astype(BF16)
            return carry

        lax.fori_loop(pairs[0], pairs[1], pair, 0)

    def pump(*steps):
        for step in steps:
            step()

    context_back(SELF)
    for wait in pending:
        wait()
    pending.clear()
    weight_rows(SELF, 3, ctx_t.at[1], [(0, 512, dzb)])
    attend_back(1, qkv2, 2, (0, 6))
    z3_relay()

    def self_input(i, rows):
        parts = [jnp.transpose(tt[m, :, pl.ds(rows, BLOCK)]) for m in range(3)]
        for n in range(3):
            cols = slice(256 * n, 256 * n + 256)
            total = res[pl.ds(rows, BLOCK), cols]
            for m in range(3):
                total = total + dot_nn(parts[m], wa[SELF, m, :, cols])
            acc[pl.ds(rows, BLOCK), cols] = total

    blocks(self_input)
    for m in range(3):
        weight_rows(SELF, m, tt.at[m], [(0, 512, sb)])
    pl.semaphore_wait(credit.at[1], 2)
    sum_self.start_all()
    pl.semaphore_signal(credit.at[2], inc=1, device_id=at(d_core, t), device_id_type=MESH)

    s2_finish()
    z3_finish()
    for m in (2, 1, 3):
        quarter_grads((t + m) % 4)
        for one in quarters:
            one.start(m)

    blocks(lambda i, rows: norm_back(acc[pl.ds(rows, BLOCK), :], 0, 0, rows, dzb))

    norm_ids = [new_id() for _ in range(5)]
    norm_ways = [
        at(d_core, t),
        at(d_x, t),
        at(d_y, t),
        at(d, t + 1 - 2 * (t % 2)),
        at(d, (t + 2) % 4),
    ]
    norm_steps = []

    def norm_begin(k):
        send(nrm if k == 0 else nrm_recv.at[k - 1, 1], nrm_recv.at[k, 0], norm_ways[k], norm_ids[k])

    def norm_step(k):
        arrive(nrm_recv.at[k, 0], norm_ids[k])
        mine = nrm[...] if k == 0 else nrm_recv[k - 1, 1]
        total = mine + nrm_recv[k, 0]
        if k < 4:
            nrm_recv[k, 1] = total
            norm_begin(k + 1)
        else:
            norm_out[...] = total

    norm_begin(0)
    context_back(CROSS)
    weight_rows(CROSS, 3, ctx_t.at[0], [(0, 512, dzb)])
    norm_step(0)
    attend_back(0, qkv1, 0, (0, 3))
    norm_step(1)
    pump(*sum_self.both(sum_self.stage2))
    attend_back(0, qkv1, 0, (3, 6))
    norm_step(2)

    key_ids = [new_id() for _ in range(2)]

    def key_input(j):
        parts = [jnp.transpose(tt[m, :, 256 * j : 256 * j + 256]) for m in (1, 2)]
        for n in range(3):
            cols = slice(256 * n, 256 * n + 256)
            act[1, 256 * j : 256 * j + 256, cols] = (
                dot_nn(parts[0], wa[CROSS, 1, :, cols]) + dot_nn(parts[1], wa[CROSS, 2, :, cols])
            ).astype(BF16)

    key_input(0)
    key_input(1)
    key_copies = [
        remote(
            act.at[1, pl.ds(256 * j, 256), :],
            dhk_recv.at[j],
            at(d_core, t),
            key_ids[j],
        )
        for j in range(2)
    ]
    key_copies[0].start()

    @pl.when(c == 0)
    def _():
        key_copies[1].start()

    def cross_input(i, rows):
        part = jnp.transpose(tt[0, :, pl.ds(rows, BLOCK)])
        for n in range(3):
            cols = slice(256 * n, 256 * n + 256)
            res[pl.ds(rows, BLOCK), cols] += dot_nn(part, wa[CROSS, 0, :, cols])

    blocks(cross_input)
    weight_rows(CROSS, 0, tt.at[0], [(0, 512, xrow.at[pl.ds(own_base, 512), :])])
    for m in range(1, 3):
        weight_rows(
            CROSS,
            m,
            tt.at[m],
            [
                (0, 256, xrow.at[pl.ds(other_base, 256), :]),
                (256, 256, xrow.at[pl.ds(512, 256), :]),
            ],
        )

    pump(*sum_self.both(sum_self.stage3))
    quarter_grads(t)

    pl.semaphore_wait(credit.at[2], 1)
    core_sums = [(a, n, new_id()) for a in range(2) for n in range(3)]

    def core_slot(a, n):
        k = 3 * a + n
        return qkv2.at[k // 2, pl.ds(256 * (k % 2), 256), :]

    for a, n, ident in core_sums:
        send(
            wa.at[CROSS, 2 * (1 - c) + a, pl.ds(256 * n, 256), :],
            core_slot(a, n),
            at(d_core, t),
            ident,
        )
    norm_step(3)

    y_close()
    arrive(dhk_recv.at[0], key_ids[0])

    @pl.when(c == 1)
    def _():
        arrive(dhk_recv.at[1], key_ids[1])

    yb[:BLOCK, :] = (res[:BLOCK, :] + dhk_recv[0].astype(F32)).astype(BF16)

    @pl.when(c == 1)
    def _():
        own_part = act[1, BLOCK:, :].astype(F32)
        yb[BLOCK:, :] = (res[BLOCK:, :] + dhk_recv[1].astype(F32) + own_part).astype(BF16)

    dx_begin, dx_close = return_row(dx_out)
    pump(*[one.collect for one in quarters])

    for a, n, ident in core_sums:
        arrive(core_slot(a, n), ident)
        fold(wa.at[CROSS, 2 * c + a, pl.ds(256 * n, 256), :], [core_slot(a, n)])
    pl.semaphore_wait(credit.at[0], 2)
    sum_cross.start_all()
    norm_step(4)
    pump(
        *sum_cross.both(sum_cross.stage2),
        *sum_self.both(sum_self.stage4),
        *[one.relay for one in quarters],
        *sum_cross.both(sum_cross.stage3),
        dx_begin,
        *sum_self.both(sum_self.stage4_end),
        *sum_cross.both(sum_cross.stage4),
        *[one.swap for one in quarters],
        sum_self.stage5,
        *sum_cross.both(sum_cross.stage4_end),
        sum_self.stage6,
        sum_cross.stage5,
        sum_cross.stage6,
        *[one.end for one in quarters],
        sum_self.stage7,
        sum_cross.stage7,
    )
    for wait in pending + late:
        wait()
    key_copies[0].wait_send()

    @pl.when(c == 0)
    def _():
        key_copies[1].wait_send()

    dx_close()
    if counter[0] > SEMAPHORES or local_counter[0] > LOCALS:
        raise ValueError((counter[0], local_counter[0]))


SEMAPHORES = 320
LOCALS = 40


def call_layer(*operands):
    def vmem(shape, dtype=BF16):
        return pltpu.VMEM(shape, dtype)

    anywhere = pl.BlockSpec(memory_space=pl.ANY)
    whole = pl.BlockSpec(memory_space=pltpu.VMEM)
    x_in = operands[0]
    return pl.pallas_call(
        layer_kernel,
        name="cross_modality_layer",
        out_shape=(
            jax.ShapeDtypeStruct(x_in.shape, BF16),
            jax.ShapeDtypeStruct(x_in.shape, BF16),
            jax.ShapeDtypeStruct((4, 192, 768), BF16),
            jax.ShapeDtypeStruct((2, 4, 192, 768), BF16),
            jax.ShapeDtypeStruct((2, 768, 768), BF16),
            jax.ShapeDtypeStruct((2, 768, 768), BF16),
            jax.ShapeDtypeStruct((16, 768), F32),
        ),
        in_specs=[anywhere] * 9 + [whole] * 2,
        out_specs=(anywhere,) * 6 + (whole,),
        scratch_shapes=[
            vmem((2, 4, 768, 768)),
            vmem((2, 4, 768, 768)),
            vmem((768, 768)),
            vmem((768, 768)),
            vmem((8, 768), F32),
            vmem((2, 512, 128), F32),
            vmem((3, 512, 768)),
            vmem((3, 512, 768)),
            vmem((2, 768, 512)),
            vmem((2, 16, 512), F32),
            vmem((3, 512, 768)),
            vmem((3, 512, 1), F32),
            vmem((512, 768)),
            vmem((512, 768), F32),
            vmem((512, 768), F32),
            vmem((4, 512, 768)),
            vmem((4, 512, 768)),
            vmem((512, 768)),
            vmem((3, 768, 512)),
            vmem((512, 768)),
            vmem((2, 256, 768)),
            vmem((2, 512, 128), F32),
            vmem((16, 768), F32),
            vmem((5, 2, 16, 768), F32),
            vmem((4, 512, 768)),
            vmem((4, 512, 768)),
            vmem((2, 192, 768), F32),
            vmem((2, 3, 192, 768)),
            vmem((2, 4, 2, 48, 768)),
            vmem((3, 2, 2, 48, 768)),
            vmem((2, 4, 48, 768)),
            vmem((3, 2, 48, 768)),
            pltpu.SemaphoreType.DMA((SEMAPHORES,)),
            pltpu.SemaphoreType.DMA((SEMAPHORES,)),
            pltpu.SemaphoreType.DMA((LOCALS,)),
            pltpu.SemaphoreType.REGULAR((3,)),
        ],
        compiler_params=pltpu.CompilerParams(
            collective_id=0, has_side_effects=True, vmem_limit_bytes=64 * 1024 * 1024 - 512 * 1024
        ),
    )(*operands)


def results_kernel(
    cross, own, up, down, dx, norm,
    dx_out, cross_qkv, cross_out, self_qkv, self_out, up_out, down_out, gains, biases,
    v_cross, v_own, v_up, v_down, v_dx, v_norm,
    w_dx, w_cross_qkv, w_cross_out, w_self_qkv, w_self_out, w_up, w_down,
    in_sems, out_sems,
):
    sources = [
        (down.at[0], v_down.at[0]),
        (down.at[1], v_down.at[1]),
        (up.at[0], v_up.at[0]),
        (up.at[1], v_up.at[1]),
        (own.at[0], v_own.at[0]),
        (own.at[1], v_own.at[1]),
        (cross, v_cross),
        (dx, v_dx),
        (norm, v_norm),
    ]
    loads = [
        pltpu.make_async_copy(src, dst, in_sems.at[k]) for k, (src, dst) in enumerate(sources)
    ]
    for load in loads:
        load.start()
    stores = []

    def store(src, dst):
        copy = pltpu.make_async_copy(src, dst, out_sems.at[len(stores)])
        copy.start()
        stores.append(copy)

    for k in range(2):
        loads[k].wait()
        w_down[k] = v_down[k].astype(F32)
        store(w_down.at[k], down_out.at[k])
    for k in range(2):
        loads[2 + k].wait()
        for n in range(3):
            cols = slice(256 * n, 256 * n + 256)
            w_up[k, cols, :] = jnp.transpose(v_up[k, :, cols]).astype(F32)
        store(w_up.at[k], up_out.at[k])
    for k in range(2):
        loads[4 + k].wait()
        for n in range(3):
            w_self_qkv[k, n] = v_own[k, n].astype(F32)
        w_self_out[k] = v_own[k, 3].astype(F32)
        store(w_self_qkv.at[k], self_qkv.at[k])
        store(w_self_out.at[k], self_out.at[k])
    loads[6].wait()
    for n in range(3):
        w_cross_qkv[n] = v_cross[n].astype(F32)
    w_cross_out[...] = v_cross[3].astype(F32)
    store(w_cross_qkv, cross_qkv)
    store(w_cross_out, cross_out)
    loads[7].wait()
    w_dx[...] = v_dx[...].astype(F32)
    store(w_dx, dx_out)
    loads[8].wait()
    gains[...] = v_norm[0:5, :]
    biases[...] = v_norm[8:13, :]
    for copy in stores:
        copy.wait()


def call_results(cross, own, up, down, dx, norm):
    anywhere = pl.BlockSpec(memory_space=pl.ANY)
    whole = pl.BlockSpec(memory_space=pltpu.VMEM)

    def out(shape):
        return jax.ShapeDtypeStruct(shape, F32)

    shapes = [
        dx.shape,
        (3, 192, 768),
        (192, 768),
        (2, 3, 192, 768),
        (2, 192, 768),
        (2, 768, 768),
        (2, 768, 768),
    ]
    return pl.pallas_call(
        results_kernel,
        name="results",
        out_shape=tuple(out(shape) for shape in shapes) + (out((5, 768)), out((5, 768))),
        in_specs=[anywhere] * 6,
        out_specs=(anywhere,) * 7 + (whole,) * 2,
        scratch_shapes=[pltpu.VMEM(ref.shape, ref.dtype) for ref in (cross, own, up, down, dx, norm)]
        + [pltpu.VMEM(shape, F32) for shape in shapes]
        + [pltpu.SemaphoreType.DMA((9,)), pltpu.SemaphoreType.DMA((11,))],
        compiler_params=pltpu.CompilerParams(vmem_limit_bytes=56 * 1024 * 1024),
    )(cross, own, up, down, dx, norm)


def solution(mesh):
    extra = []
    step = 8
    while step < mesh.shape["dp"]:
        extra.append(step)
        step *= 2

    def total(array):
        for step in extra:
            pairs = [(k, k ^ step) for k in range(mesh.shape["dp"])]
            array = array + lax.ppermute(array, "dp", pairs)
        return array

    def body(
        layer_input,
        word_segments,
        image_order,
        cross_qkv,
        cross_out,
        self_qkv,
        self_out,
        ffn_up,
        ffn_down,
        norm_gains,
        norm_biases,
        out_grad,
    ):
        rows = layer_input.shape[0]
        images = jnp.repeat(image_order, BOXES, axis=1)
        pads = jnp.full((rows, PADS), CAPTIONS, jnp.int32)
        none = jnp.full((rows, WORDS + REGIONS + PADS), -1, jnp.int32)
        groups = jnp.concatenate([word_segments, images, pads], axis=1)
        keys = jnp.concatenate([word_segments, none[:, :REGIONS], pads], axis=1)
        kinds = jnp.concatenate([word_segments, images + 16, pads + 32], axis=1)
        codes = jnp.stack([groups, keys, kinds, none, none, none, none, none], axis=1).astype(F32)
        y, dx, d_cross, d_self, d_up, d_down, d_norm = call_layer(
            layer_input,
            out_grad,
            codes,
            jnp.swapaxes(cross_qkv, 1, 2),
            cross_out,
            jnp.swapaxes(self_qkv, 2, 3),
            self_out,
            ffn_up,
            ffn_down,
            norm_gains,
            norm_biases,
        )
        dx, *grads = call_results(d_cross, d_self, d_up, d_down, dx, d_norm)
        grads = [total(array) for array in grads]
        grads[0] = jnp.swapaxes(grads[0], 1, 2)
        grads[2] = jnp.swapaxes(grads[2], 2, 3)
        return (y, dx, *grads)

    in_specs = (
        P("dp", "tensor", None),
        P("dp", None),
        P("dp", None),
        P(None, None, "tensor"),
        P("tensor", None),
        P(None, None, None, "tensor"),
        P(None, "tensor", None),
        P(None, None, "tensor"),
        P(None, "tensor", None),
        P(),
        P(),
        P("dp", "tensor", None),
    )
    out_specs = (
        P("dp", "tensor", None),
        P("dp", "tensor", None),
        P(None, None, "tensor"),
        P("tensor", None),
        P(None, None, None, "tensor"),
        P(None, "tensor", None),
        P(None, None, "tensor"),
        P(None, "tensor", None),
        P(),
        P(),
    )
    return jax.shard_map(body, mesh=mesh, in_specs=in_specs, out_specs=out_specs, check_vma=False)
```
